512 devices in a mesh: row: 32 (over y, x_hi, core), col: 16 (over z, x_lo).
Axes of the slice: x: 4 (x_hi: 2, x_lo: 2; x = x_hi * 2 + x_lo), y: 8, z: 8, core: 2. Of those that a mesh axis runs over, the one named last changes fastest.
Arguments:
- features: bfloat16 [65536, 512], P(('col', 'row')), may hold values from -6 to 6
- block_values: bfloat16 [32, 16, 12, 128, 128], P('row', 'col'), may hold values from -0.21875 to 0.21875
- block_rows: int32 [32, 16, 12], P('row', 'col'), may hold values from 0 to 15
- block_cols: int32 [32, 16, 12], P('row', 'col'), may hold values from 0 to 31
- block_count: int32 [32, 16], P('row', 'col'), may hold values from 3 to 12, as said below
- weight: bfloat16 [512, 512], replicated, may hold values from -0.25 to 0.25
- bias: float32 [512], replicated, may hold values from -3 to 3
- cotangent: bfloat16 [65536, 512], P(('row', 'col')), may hold values from -6 to 6
Outputs:
- hidden: bfloat16 [65536, 512], P(('row', 'col'))
- weight_grad: float32 [512, 512], replicated
- bias_grad: float32 [512], replicated
- feature_grad: bfloat16 [65536, 512], P(('col', 'row'))
The draws below stay inside these ranges and needn't reach their ends.
Inputs may be any that keep to these rules, and one draw needn't show every extreme that they name: `block_count`: no grid tile has more than 12 live slots, and some tile has exactly 12.
All inputs are finite; a program needn't handle non-finite values.
Results may differ from the reference program's by a relative error of at most 0.017.
Values may be sent and summed in bfloat16 or wider, within the bound.
A program may use at most 64 MiB of HBM per device.

```python
import jax
import jax.numpy as jnp
from jax import lax

F = 512
BS = 128
CAP = 12
NODES = 65536
RB = 16
CB = 32
N_ROW = 32
N_COL = 16


def draw_block_count(key, part):
    first_key, second_key = jax.random.split(jax.random.fold_in(key, 17))
    counts = jax.random.randint(first_key, (N_ROW, N_COL), max(1, CAP // 4), CAP + 1)
    chosen = jax.random.randint(second_key, (), 0, N_ROW * N_COL)
    places = jnp.arange(N_ROW * N_COL).reshape(N_ROW, N_COL)
    return jnp.where(places == chosen, CAP, counts).astype(jnp.int32)


def touch_ends(result, key, least, largest):
    dims = result.shape
    place = [jax.random.randint(jax.random.fold_in(key, axis), (), 0, dims[axis]) for axis in range(len(dims))]
    result = result.at[tuple(place)].set(least)
    longest = dims.index(max(dims))
    place[longest] = (place[longest] + 1) % dims[longest]
    return result.at[tuple(place)].set(largest)


def block_scale(own_key, extent, shards, smallest, top_value):
    gain, own = 1.0, jax.random.fold_in(own_key, 6)
    for dim, blocks in shards:
        steps = jnp.exp(jax.random.uniform(jax.random.fold_in(own, dim), (blocks,), jnp.float32, smallest / len(shards), top_value / len(shards)))
        gain = gain * jnp.repeat(steps, extent[dim] // blocks).reshape([-1 if axis == dim else 1 for axis in range(len(extent))])
    return gain


def scatter_about(stream_key, extent, deviation, limit, shards=(), kind=jnp.bfloat16):
    array = jax.random.normal(stream_key, extent, jnp.float32) * deviation
    if len(shards) > 0:
        array = block_scale(stream_key, extent, shards, -0.22, 0.18) * array
    return jnp.clip(array, min=-limit, max=limit).astype(kind)


def setup_inputs(seed: int = 0) -> dict:
    keys = jax.random.split(jax.random.key(seed), 9)
    features = scatter_about(keys[0], (NODES, F), 1.0, 6.0, ((0, 512),))
    block_values = scatter_about(keys[1], (N_ROW, N_COL, CAP, BS, BS), (CAP * BS * N_COL // (2 * RB)) ** -0.5, 0.21875, ((0, 32), (1, 16)))
    block_rows = touch_ends(jax.random.randint(keys[2], (N_ROW, N_COL, CAP), 0, RB), jax.random.fold_in(keys[2], 1), 0, RB - 1).astype(jnp.int32)
    block_cols = touch_ends(jax.random.randint(keys[3], (N_ROW, N_COL, CAP), 0, CB), jax.random.fold_in(keys[3], 1), 0, CB - 1).astype(jnp.int32)
    block_count = draw_block_count(jax.random.fold_in(keys[8], 71), 0)
    weight = scatter_about(keys[5], (F, F), F ** -0.5, 0.25)
    bias = scatter_about(keys[6], (F,), 0.5, 3.0, (), jnp.float32)
    cotangent = scatter_about(keys[7], (NODES, F), 1.0, 6.0, ((0, 512),))
    return dict(features=features, block_values=block_values, block_rows=block_rows, block_cols=block_cols, block_count=block_count, weight=weight, bias=bias, cotangent=cotangent)


def tile_pass(carry_total, values_all, rows_all, cols_all, count_all, source, src_len, dst_len, backward):
    def one_tile(total, flat_index):
        grid_row = flat_index // N_COL
        grid_col = flat_index % N_COL
        if backward:
            src_start = grid_row * src_len
            dst_start = grid_col * dst_len
        else:
            src_start = grid_col * src_len
            dst_start = grid_row * dst_len
        gathered = lax.dynamic_slice_in_dim(source, src_start, src_len, 0).astype(jnp.float32)
        tile_values = values_all[grid_row, grid_col]
        tile_rows = rows_all[grid_row, grid_col]
        tile_cols = cols_all[grid_row, grid_col]
        live_count = count_all[grid_row, grid_col]

        def add_block(slot, partial_value):
            block = tile_values[slot].astype(jnp.float32)
            if backward:
                segment = lax.dynamic_slice_in_dim(gathered, tile_rows[slot] * BS, BS, 0)
                target = tile_cols[slot] * BS
                product = jnp.dot(block.T, segment)
            else:
                segment = lax.dynamic_slice_in_dim(gathered, tile_cols[slot] * BS, BS, 0)
                target = tile_rows[slot] * BS
                product = jnp.dot(block, segment)
            current = lax.dynamic_slice_in_dim(partial_value, target, BS, 0)
            return lax.dynamic_update_slice_in_dim(partial_value, current + product, target, 0)

        partial_value = lax.fori_loop(0, live_count, add_block, jnp.zeros((dst_len, F), jnp.float32))
        rounded = lax.optimization_barrier(partial_value.astype(jnp.bfloat16)).astype(jnp.float32)
        current = lax.dynamic_slice_in_dim(total, dst_start, dst_len, 0)
        total = lax.dynamic_update_slice_in_dim(total, current + rounded, dst_start, 0)
        return total, None

    total, _ = lax.scan(one_tile, carry_total, jnp.arange(N_ROW * N_COL, dtype=jnp.int32))
    return total


def reference(features, block_values, block_rows, block_cols, block_count, weight, bias, cotangent):
    row_tile = RB * BS
    col_tile = CB * BS
    zeros = jnp.zeros((NODES, F), jnp.float32)
    aggregate = tile_pass(zeros, block_values, block_rows, block_cols, block_count, features, col_tile, row_tile, False).astype(jnp.bfloat16)
    preact = jnp.dot(aggregate, weight, preferred_element_type=jnp.float32) + bias
    hidden = jax.nn.silu(preact).astype(jnp.bfloat16)
    sigma = jax.nn.sigmoid(preact)
    grad_pre = cotangent.astype(jnp.float32) * sigma * (1.0 + preact * (1.0 - sigma))
    grad_low = grad_pre.astype(jnp.bfloat16)
    weight_grad = jnp.dot(aggregate.T, grad_low, preferred_element_type=jnp.float32)
    bias_grad = jnp.sum(grad_pre, axis=0)
    grad_agg = jnp.dot(grad_low, weight.T, preferred_element_type=jnp.float32).astype(jnp.bfloat16)
    feature_grad = tile_pass(zeros, block_values, block_rows, block_cols, block_count, grad_agg, row_tile, col_tile, True).astype(jnp.bfloat16)
    return hidden, weight_grad, bias_grad, feature_grad
```

```python
import jax
import jax.numpy as jnp
from jax import lax
from jax.sharding import PartitionSpec as P


def slot_product(tile_values, tile_rows, tile_cols, live_count, source, out_len, backward):
    capacity = tile_values.shape[0]
    block_size = tile_values.shape[1]
    width = source.shape[1]
    group = max([d for d in range(1, min(capacity, 16) + 1) if capacity % d == 0])
    groups = capacity // group
    panels = source.reshape(source.shape[0] // block_size, block_size, width)
    out_blocks = out_len // block_size
    if backward:
        source_ids = tile_rows
        target_ids = tile_cols
        form = "sba,sbf->saf"
    else:
        source_ids = tile_cols
        target_ids = tile_rows
        form = "sab,sbf->saf"
    alive = jnp.arange(capacity, dtype=jnp.int32) < live_count
    places = jnp.arange(out_blocks, dtype=jnp.int32)

    def one_group(total, items):
        values_part, source_part, target_part, alive_part = items
        segments = jnp.take(panels, source_part, axis=0)
        products = jnp.einsum(form, values_part, segments, preferred_element_type=jnp.float32)
        selector = ((target_part[None, :] == places[:, None]) & alive_part[None, :]).astype(
            jnp.float32
        )
        added = jnp.einsum("rs,saf->raf", selector, products, precision=lax.Precision.HIGHEST)
        return (total + added, None)

    items = (
        tile_values.reshape(groups, group, block_size, block_size),
        source_ids.reshape(groups, group),
        target_ids.reshape(groups, group),
        alive.reshape(groups, group),
    )
    start = jnp.zeros((out_blocks, block_size, width), jnp.float32)
    total, _ = lax.scan(one_group, start, items)
    return total.reshape(out_len, width)


def gather_rows(x, axis):
    count = lax.axis_size(axis)
    stacked = jnp.broadcast_to(x[None], (count,) + x.shape)
    received = lax.all_to_all(stacked, axis, split_axis=0, concat_axis=0, tiled=True)
    return received.reshape((count * x.shape[0],) + x.shape[1:])


def scatter_sum(x, axis):
    count = lax.axis_size(axis)
    pieces = x.reshape((count, x.shape[0] // count) + x.shape[1:])
    received = lax.all_to_all(pieces, axis, split_axis=0, concat_axis=0, tiled=True)
    return jnp.sum(received.astype(jnp.float32), axis=0)


def global_grads(local_weight, local_bias):
    width = local_weight.shape[1]
    pad = jnp.zeros((local_weight.shape[0], 127), jnp.float32)
    packed = jnp.concatenate([local_weight, local_bias[:, None], pad], axis=1)
    by_col = scatter_sum(packed, "col")
    total = scatter_sum(by_col, "row")
    whole = gather_rows(gather_rows(total, "row"), "col")
    return whole[:, :width], whole[:, width]


def transposed_product(left, weight):
    return lax.dot_general(
        left, weight, (((1,), (1,)), ((), ())), preferred_element_type=jnp.float32
    ).astype(jnp.bfloat16)


def source_total(received):
    return jnp.sum(received.astype(jnp.float32), axis=0).astype(jnp.bfloat16)


def per_device(
    features, block_values, block_rows, block_cols, block_count, weight, bias, cotangent
):
    tile_values = block_values[0, 0]
    tile_rows = block_rows[0, 0]
    tile_cols = block_cols[0, 0]
    live_count = block_count[0, 0]
    own_nodes = features.shape[0]
    width = features.shape[1]
    row_len = lax.axis_size("col") * own_nodes
    gathered = gather_rows(features, "row")
    col_len = gathered.shape[0]
    partial_value = slot_product(
        tile_values, tile_rows, tile_cols, live_count, gathered, row_len, False
    )
    aggregate = scatter_sum(partial_value.astype(jnp.bfloat16), "col").astype(jnp.bfloat16)
    preact = jnp.dot(aggregate, weight, preferred_element_type=jnp.float32) + bias
    hidden = jax.nn.silu(preact).astype(jnp.bfloat16)
    sigma = jax.nn.sigmoid(preact)
    grad_pre = cotangent.astype(jnp.float32) * sigma * (1.0 + preact * (1.0 - sigma))
    grad_low = grad_pre.astype(jnp.bfloat16)
    local_weight = lax.dot_general(
        aggregate, grad_low, (((0,), (0,)), ((), ())), preferred_element_type=jnp.float32
    )
    local_bias = jnp.sum(grad_pre, axis=0)
    grad_agg = transposed_product(grad_low, weight)
    grad_panel = gather_rows(grad_agg, "col")
    back = slot_product(tile_values, tile_rows, tile_cols, live_count, grad_panel, col_len, True)
    back_low = back.astype(jnp.bfloat16).reshape(col_len // own_nodes, own_nodes, width)
    received = lax.all_to_all(back_low, "row", split_axis=0, concat_axis=0, tiled=True)
    feature_grad = source_total(received)
    weight_grad, bias_grad = global_grads(local_weight, local_bias)
    return (hidden, weight_grad, bias_grad, feature_grad)


def solution(mesh):
    in_specs = (
        P(("col", "row"), None),
        P("row", "col", None, None, None),
        P("row", "col", None),
        P("row", "col", None),
        P("row", "col"),
        P(),
        P(),
        P(("row", "col"), None),
    )
    out_specs = (P(("row", "col"), None), P(), P(), P(("col", "row"), None))
    return jax.shard_map(
        per_device, mesh=mesh, in_specs=in_specs, out_specs=out_specs, check_vma=False
    )
```

```python
import functools

import jax
import jax.numpy as jnp
from jax import lax
from jax.experimental import pallas as pl
from jax.experimental.pallas import tpu as pltpu
from jax.sharding import PartitionSpec as P

MESH_ID = pl.DeviceIdType.MESH


def _exchange_kernel(axis, other, n, broadcast, src_ref, out_ref, send_sem, recv_sem, own_sem):
    me = lax.axis_index(axis)
    there = lax.axis_index(other)

    def device(k):
        return (k, there) if axis == "row" else (there, k)

    def piece(k):
        return src_ref if broadcast else src_ref.at[k]

    barrier = pltpu.get_barrier_semaphore()

    def greet(step, carry):
        peer = lax.rem(me + step, n)
        pl.semaphore_signal(barrier, inc=1, device_id=device(peer), device_id_type=MESH_ID)
        return carry

    lax.fori_loop(1, n, greet, 0)
    pl.semaphore_wait(barrier, n - 1)

    own = pltpu.make_async_copy(piece(me), out_ref.at[me], own_sem)
    own.start()

    def send(step, carry):
        peer = lax.rem(me + step, n)
        pltpu.make_async_remote_copy(
            src_ref=piece(peer), dst_ref=out_ref.at[me], send_sem=send_sem.at[step],
            recv_sem=recv_sem.at[step], device_id=device(peer), device_id_type=MESH_ID,
        ).start()
        return carry

    lax.fori_loop(1, n, send, 0)

    def finish(step, carry):
        peer = lax.rem(me + step, n)
        source = lax.rem(me + n - step, n)
        pltpu.make_async_remote_copy(
            src_ref=piece(peer), dst_ref=out_ref.at[me], send_sem=send_sem.at[step],
            recv_sem=recv_sem.at[step], device_id=device(peer), device_id_type=MESH_ID,
        ).wait_send()
        pltpu.make_async_remote_copy(
            src_ref=piece(source), dst_ref=out_ref.at[source], send_sem=send_sem.at[step],
            recv_sem=recv_sem.at[step], device_id=device(source), device_id_type=MESH_ID,
        ).wait_recv()
        return carry

    lax.fori_loop(1, n, finish, 0)
    own.wait()


def exchange(x, axis, broadcast, ident):
    n = lax.axis_size(axis)
    other = "col" if axis == "row" else "row"
    shape = (n,) + (x.shape if broadcast else x.shape[1:])
    return pl.pallas_call(
        functools.partial(_exchange_kernel, axis, other, n, broadcast),
        out_shape=jax.ShapeDtypeStruct(shape, x.dtype),
        in_specs=[pl.BlockSpec(memory_space=pl.ANY)],
        out_specs=pl.BlockSpec(memory_space=pl.ANY),
        scratch_shapes=[
            pltpu.SemaphoreType.DMA((n,)),
            pltpu.SemaphoreType.DMA((n,)),
            pltpu.SemaphoreType.DMA(()),
        ],
        compiler_params=pltpu.CompilerParams(collective_id=ident, has_side_effects=True),
        cost_estimate=pl.CostEstimate(
            flops=0, transcendentals=0, bytes_accessed=2 * n * x.size * x.dtype.itemsize
        ),
    )(x)


def slot_product(tile_values, tile_rows, tile_cols, live_count, source, out_len, backward):
    capacity = tile_values.shape[0]
    block_size = tile_values.shape[1]
    width = source.shape[1]
    group = max([d for d in range(1, min(capacity, 16) + 1) if capacity % d == 0])
    groups = capacity // group
    panels = source.reshape(source.shape[0] // block_size, block_size, width)
    out_blocks = out_len // block_size
    if backward:
        source_ids = tile_rows
        target_ids = tile_cols
        form = "sba,sbf->saf"
    else:
        source_ids = tile_cols
        target_ids = tile_rows
        form = "sab,sbf->saf"
    alive = jnp.arange(capacity, dtype=jnp.int32) < live_count
    places = jnp.arange(out_blocks, dtype=jnp.int32)

    def one_group(total, items):
        values_part, source_part, target_part, alive_part = items
        segments = jnp.take(panels, source_part, axis=0)
        products = jnp.einsum(form, values_part, segments, preferred_element_type=jnp.float32)
        selector = ((target_part[None, :] == places[:, None]) & alive_part[None, :]).astype(
            jnp.float32
        )
        added = jnp.einsum("rs,saf->raf", selector, products, precision=lax.Precision.HIGHEST)
        return (total + added, None)

    items = (
        tile_values.reshape(groups, group, block_size, block_size),
        source_ids.reshape(groups, group),
        target_ids.reshape(groups, group),
        alive.reshape(groups, group),
    )
    start = jnp.zeros((out_blocks, block_size, width), jnp.float32)
    total, _ = lax.scan(one_group, start, items)
    return total.reshape(out_len, width)


def gather_rows(x, axis):
    count = lax.axis_size(axis)
    stacked = jnp.broadcast_to(x[None], (count,) + x.shape)
    received = lax.all_to_all(stacked, axis, split_axis=0, concat_axis=0, tiled=True)
    return received.reshape((count * x.shape[0],) + x.shape[1:])


def scatter_sum(x, axis):
    count = lax.axis_size(axis)
    pieces = x.reshape((count, x.shape[0] // count) + x.shape[1:])
    received = lax.all_to_all(pieces, axis, split_axis=0, concat_axis=0, tiled=True)
    return jnp.sum(received.astype(jnp.float32), axis=0)


def pack_grads(local_weight, local_bias):
    pad = jnp.zeros((local_weight.shape[0], 127), jnp.float32)
    return jnp.concatenate([local_weight, local_bias[:, None], pad], axis=1)


def unpack_grads(by_col_then_row, width):
    cols, rows = by_col_then_row.shape[0], by_col_then_row.shape[1]
    whole = by_col_then_row.transpose(1, 0, 2).reshape(cols * rows, -1)
    return whole[:, :width], whole[:, width]


def transposed_product(left, weight):
    return lax.dot_general(
        left, weight, (((1,), (1,)), ((), ())), preferred_element_type=jnp.float32
    ).astype(jnp.bfloat16)


def source_total(received):
    return jnp.sum(received.astype(jnp.float32), axis=0).astype(jnp.bfloat16)


def per_device(
    features, block_values, block_rows, block_cols, block_count, weight, bias, cotangent
):
    tile_values = block_values[0, 0]
    tile_rows = block_rows[0, 0]
    tile_cols = block_cols[0, 0]
    live_count = block_count[0, 0]
    own_nodes = features.shape[0]
    width = features.shape[1]
    row_len = lax.axis_size("col") * own_nodes
    gathered = gather_rows(features, "row")
    col_len = gathered.shape[0]
    partial_value = slot_product(
        tile_values, tile_rows, tile_cols, live_count, gathered, row_len, False
    )
    aggregate = scatter_sum(partial_value.astype(jnp.bfloat16), "col").astype(jnp.bfloat16)
    preact = jnp.dot(aggregate, weight, preferred_element_type=jnp.float32) + bias
    hidden = jax.nn.silu(preact).astype(jnp.bfloat16)
    sigma = jax.nn.sigmoid(preact)
    grad_pre = cotangent.astype(jnp.float32) * sigma * (1.0 + preact * (1.0 - sigma))
    grad_low = grad_pre.astype(jnp.bfloat16)
    local_weight = lax.dot_general(
        aggregate, grad_low, (((0,), (0,)), ((), ())), preferred_element_type=jnp.float32
    )
    local_bias = jnp.sum(grad_pre, axis=0)
    grad_agg = transposed_product(grad_low, weight)
    packed = pack_grads(local_weight, local_bias)
    by_row = scatter_sum(packed, "row")
    grad_panel = exchange(grad_agg, "col", True, 0).reshape(-1, width)
    grad_panel, by_row = lax.optimization_barrier((grad_panel, by_row))
    reduced = scatter_sum(by_row, "col")
    back = slot_product(tile_values, tile_rows, tile_cols, live_count, grad_panel, col_len, True)
    back_low = back.astype(jnp.bfloat16).reshape(col_len // own_nodes, own_nodes, width)
    back_low, reduced = lax.optimization_barrier((back_low, reduced))
    row_part = gather_rows(reduced, "row")
    back_low, row_part = lax.optimization_barrier((back_low, row_part))
    received = exchange(back_low, "row", False, 1)
    every = gather_rows(row_part[None], "col")
    feature_grad = source_total(received)
    weight_grad, bias_grad = unpack_grads(every, width)
    return (hidden, weight_grad, bias_grad, feature_grad)


def solution(mesh):
    in_specs = (
        P(("col", "row"), None),
        P("row", "col", None, None, None),
        P("row", "col", None),
        P("row", "col", None),
        P("row", "col"),
        P(),
        P(),
        P(("row", "col"), None),
    )
    out_specs = (P(("row", "col"), None), P(), P(), P(("col", "row"), None))
    return jax.shard_map(
        per_device, mesh=mesh, in_specs=in_specs, out_specs=out_specs, check_vma=False
    )
```

```python
import functools

import jax
import jax.numpy as jnp
from jax import lax
from jax.experimental import pallas as pl
from jax.experimental.pallas import tpu as pltpu
from jax.sharding import PartitionSpec as P

MESH_ID = pl.DeviceIdType.MESH


def _exchange_kernel(axis, other, n, broadcast, src_ref, out_ref, send_sem, recv_sem, own_sem):
    me = lax.axis_index(axis)
    there = lax.axis_index(other)

    def device(k):
        return (k, there) if axis == "row" else (there, k)

    def piece(k):
        return src_ref if broadcast else src_ref.at[k]

    barrier = pltpu.get_barrier_semaphore()

    def greet(step, carry):
        peer = lax.rem(me + step, n)
        pl.semaphore_signal(barrier, inc=1, device_id=device(peer), device_id_type=MESH_ID)
        return carry

    lax.fori_loop(1, n, greet, 0)
    pl.semaphore_wait(barrier, n - 1)

    own = pltpu.make_async_copy(piece(me), out_ref.at[me], own_sem)
    own.start()

    def send(step, carry):
        peer = lax.rem(me + step, n)
        pltpu.make_async_remote_copy(
            src_ref=piece(peer), dst_ref=out_ref.at[me], send_sem=send_sem.at[step],
            recv_sem=recv_sem.at[step], device_id=device(peer), device_id_type=MESH_ID,
        ).start()
        return carry

    lax.fori_loop(1, n, send, 0)

    def finish(step, carry):
        peer = lax.rem(me + step, n)
        source = lax.rem(me + n - step, n)
        pltpu.make_async_remote_copy(
            src_ref=piece(peer), dst_ref=out_ref.at[me], send_sem=send_sem.at[step],
            recv_sem=recv_sem.at[step], device_id=device(peer), device_id_type=MESH_ID,
        ).wait_send()
        pltpu.make_async_remote_copy(
            src_ref=piece(source), dst_ref=out_ref.at[source], send_sem=send_sem.at[step],
            recv_sem=recv_sem.at[step], device_id=device(source), device_id_type=MESH_ID,
        ).wait_recv()
        return carry

    lax.fori_loop(1, n, finish, 0)
    own.wait()


def exchange(x, axis, broadcast, ident):
    n = lax.axis_size(axis)
    other = "col" if axis == "row" else "row"
    shape = (n,) + (x.shape if broadcast else x.shape[1:])
    return pl.pallas_call(
        functools.partial(_exchange_kernel, axis, other, n, broadcast),
        out_shape=jax.ShapeDtypeStruct(shape, x.dtype),
        in_specs=[pl.BlockSpec(memory_space=pl.ANY)],
        out_specs=pl.BlockSpec(memory_space=pl.ANY),
        scratch_shapes=[
            pltpu.SemaphoreType.DMA((n,)),
            pltpu.SemaphoreType.DMA((n,)),
            pltpu.SemaphoreType.DMA(()),
        ],
        compiler_params=pltpu.CompilerParams(collective_id=ident, has_side_effects=True),
        cost_estimate=pl.CostEstimate(
            flops=0, transcendentals=0, bytes_accessed=2 * n * x.size * x.dtype.itemsize
        ),
    )(x)


def _slot_kernel(backward, slots, src_ids, tgt_ids, count_ref, vals_ref, src_ref, out_ref, acc_ref):
    s = pl.program_id(0)

    @pl.when(s == 0)
    def _():
        acc_ref[...] = jnp.zeros_like(acc_ref)

    @pl.when(s < count_ref[0])
    def _():
        block = vals_ref[0]
        segment = src_ref[0]
        if backward:
            dims = (((0,), (0,)), ((), ()))
        else:
            dims = (((1,), (0,)), ((), ()))
        product = lax.dot_general(block, segment, dims, preferred_element_type=jnp.float32)
        target = tgt_ids[s]
        acc_ref[target] = acc_ref[target] + product

    @pl.when(s == slots - 1)
    def _():
        out_ref[...] = acc_ref[...].astype(out_ref.dtype)


def slot_product(tile_values, tile_rows, tile_cols, live_count, source, out_len, backward):
    slots, block_size = tile_values.shape[0], tile_values.shape[1]
    width = source.shape[1]
    n_src = source.shape[0] // block_size
    n_out = out_len // block_size
    panels = source.reshape(n_src, block_size, width)
    if backward:
        src_ids, tgt_ids = tile_rows, tile_cols
    else:
        src_ids, tgt_ids = tile_cols, tile_rows
    src_ids = jnp.clip(src_ids, 0, n_src - 1).astype(jnp.int32)
    tgt_ids = jnp.clip(tgt_ids, 0, n_out - 1).astype(jnp.int32)
    count = jnp.reshape(live_count, (1,)).astype(jnp.int32)
    grid_spec = pltpu.PrefetchScalarGridSpec(
        num_scalar_prefetch=3,
        grid=(slots,),
        in_specs=[
            pl.BlockSpec((1, block_size, block_size), lambda s, src, tgt, cnt: (s, 0, 0)),
            pl.BlockSpec((1, block_size, width), lambda s, src, tgt, cnt: (src[s], 0, 0)),
        ],
        out_specs=pl.BlockSpec((n_out, block_size, width), lambda s, src, tgt, cnt: (0, 0, 0)),
        scratch_shapes=[pltpu.VMEM((n_out, block_size, width), jnp.float32)],
    )
    out = pl.pallas_call(
        functools.partial(_slot_kernel, backward, slots),
        out_shape=jax.ShapeDtypeStruct((n_out, block_size, width), jnp.bfloat16),
        grid_spec=grid_spec,
        compiler_params=pltpu.CompilerParams(
            dimension_semantics=("arbitrary",), vmem_limit_bytes=48 * 1024 * 1024
        ),
        cost_estimate=pl.CostEstimate(
            flops=2 * slots * block_size * block_size * width,
            transcendentals=0,
            bytes_accessed=2 * (slots * block_size * (block_size + width) + n_out * block_size * width),
        ),
    )(src_ids, tgt_ids, count, tile_values, panels)
    return out.reshape(out_len, width)


def gather_rows(x, axis):
    count = lax.axis_size(axis)
    stacked = jnp.broadcast_to(x[None], (count,) + x.shape)
    received = lax.all_to_all(stacked, axis, split_axis=0, concat_axis=0, tiled=True)
    return received.reshape((count * x.shape[0],) + x.shape[1:])


def scatter_sum(x, axis):
    count = lax.axis_size(axis)
    pieces = x.reshape((count, x.shape[0] // count) + x.shape[1:])
    received = lax.all_to_all(pieces, axis, split_axis=0, concat_axis=0, tiled=True)
    return jnp.sum(received.astype(jnp.float32), axis=0)


def pack_grads(local_weight, local_bias):
    pad = jnp.zeros((local_weight.shape[0], 127), jnp.float32)
    return jnp.concatenate([local_weight, local_bias[:, None], pad], axis=1)


def unpack_grads(by_col_then_row, width):
    cols, rows = by_col_then_row.shape[0], by_col_then_row.shape[1]
    whole = by_col_then_row.transpose(1, 0, 2).reshape(cols * rows, -1)
    return whole[:, :width], whole[:, width]


def transposed_product(left, weight):
    return lax.dot_general(
        left, weight, (((1,), (1,)), ((), ())), preferred_element_type=jnp.float32
    ).astype(jnp.bfloat16)


def source_total(received):
    return jnp.sum(received.astype(jnp.float32), axis=0).astype(jnp.bfloat16)


def per_device(
    features, block_values, block_rows, block_cols, block_count, weight, bias, cotangent
):
    tile_values = block_values[0, 0]
    tile_rows = block_rows[0, 0]
    tile_cols = block_cols[0, 0]
    live_count = block_count[0, 0]
    own_nodes = features.shape[0]
    width = features.shape[1]
    row_len = lax.axis_size("col") * own_nodes
    gathered = gather_rows(features, "row")
    col_len = gathered.shape[0]
    partial_value = slot_product(
        tile_values, tile_rows, tile_cols, live_count, gathered, row_len, False
    )
    aggregate = scatter_sum(partial_value.astype(jnp.bfloat16), "col").astype(jnp.bfloat16)
    preact = jnp.dot(aggregate, weight, preferred_element_type=jnp.float32) + bias
    hidden = jax.nn.silu(preact).astype(jnp.bfloat16)
    sigma = jax.nn.sigmoid(preact)
    grad_pre = cotangent.astype(jnp.float32) * sigma * (1.0 + preact * (1.0 - sigma))
    grad_low = grad_pre.astype(jnp.bfloat16)
    local_weight = lax.dot_general(
        aggregate, grad_low, (((0,), (0,)), ((), ())), preferred_element_type=jnp.float32
    )
    local_bias = jnp.sum(grad_pre, axis=0)
    grad_agg = transposed_product(grad_low, weight)
    packed = pack_grads(local_weight, local_bias)
    by_row = scatter_sum(packed, "row")
    grad_panel = exchange(grad_agg, "col", True, 0).reshape(-1, width)
    grad_panel, by_row = lax.optimization_barrier((grad_panel, by_row))
    reduced = scatter_sum(by_row, "col")
    back = slot_product(tile_values, tile_rows, tile_cols, live_count, grad_panel, col_len, True)
    back_low = back.astype(jnp.bfloat16).reshape(col_len // own_nodes, own_nodes, width)
    back_low, reduced = lax.optimization_barrier((back_low, reduced))
    row_part = gather_rows(reduced, "row")
    back_low, row_part = lax.optimization_barrier((back_low, row_part))
    received = exchange(back_low, "row", False, 1)
    every = gather_rows(row_part[None], "col")
    feature_grad = source_total(received)
    weight_grad, bias_grad = unpack_grads(every, width)
    return (hidden, weight_grad, bias_grad, feature_grad)


def solution(mesh):
    in_specs = (
        P(("col", "row"), None),
        P("row", "col", None, None, None),
        P("row", "col", None),
        P("row", "col", None),
        P("row", "col"),
        P(),
        P(),
        P(("row", "col"), None),
    )
    out_specs = (P(("row", "col"), None), P(), P(), P(("col", "row"), None))
    return jax.shard_map(
        per_device, mesh=mesh, in_specs=in_specs, out_specs=out_specs, check_vma=False
    )
```

```python
import functools

import jax
import jax.numpy as jnp
from jax import lax
from jax.experimental import pallas as pl
from jax.experimental.pallas import tpu as pltpu
from jax.sharding import PartitionSpec as P

MESH_ID = pl.DeviceIdType.MESH


def _exchange_kernel(axis, other, n, broadcast, src_ref, out_ref, send_sem, recv_sem, own_sem):
    me = lax.axis_index(axis)
    there = lax.axis_index(other)

    def device(k):
        return (k, there) if axis == "row" else (there, k)

    def piece(k):
        return src_ref if broadcast else src_ref.at[k]

    barrier = pltpu.get_barrier_semaphore()

    def greet(step, carry):
        peer = lax.rem(me + step, n)
        pl.semaphore_signal(barrier, inc=1, device_id=device(peer), device_id_type=MESH_ID)
        return carry

    lax.fori_loop(1, n, greet, 0)
    pl.semaphore_wait(barrier, n - 1)

    own = pltpu.make_async_copy(piece(me), out_ref.at[me], own_sem)
    own.start()

    def send(step, carry):
        peer = lax.rem(me + step, n)
        pltpu.make_async_remote_copy(
            src_ref=piece(peer), dst_ref=out_ref.at[me], send_sem=send_sem.at[step],
            recv_sem=recv_sem.at[step], device_id=device(peer), device_id_type=MESH_ID,
        ).start()
        return carry

    lax.fori_loop(1, n, send, 0)

    def finish(step, carry):
        peer = lax.rem(me + step, n)
        source = lax.rem(me + n - step, n)
        pltpu.make_async_remote_copy(
            src_ref=piece(peer), dst_ref=out_ref.at[me], send_sem=send_sem.at[step],
            recv_sem=recv_sem.at[step], device_id=device(peer), device_id_type=MESH_ID,
        ).wait_send()
        pltpu.make_async_remote_copy(
            src_ref=piece(source), dst_ref=out_ref.at[source], send_sem=send_sem.at[step],
            recv_sem=recv_sem.at[step], device_id=device(source), device_id_type=MESH_ID,
        ).wait_recv()
        return carry

    lax.fori_loop(1, n, finish, 0)
    own.wait()


def _steps_kernel(axis, other, n, lo, hi, src_ref, out_ref, send_sem, recv_sem, own_sem):
    me = lax.axis_index(axis)
    there = lax.axis_index(other)
    first = max(lo, 1)

    def device(k):
        return (k, there) if axis == "row" else (there, k)

    def copy(step, peer, piece):
        return pltpu.make_async_remote_copy(
            src_ref=src_ref.at[piece], dst_ref=out_ref.at[step - lo], send_sem=send_sem.at[step - lo],
            recv_sem=recv_sem.at[step - lo], device_id=device(peer), device_id_type=MESH_ID,
        )

    barrier = pltpu.get_barrier_semaphore()

    def greet(step, carry):
        for peer in (lax.rem(me + step, n), lax.rem(me + n - step, n)):
            pl.semaphore_signal(barrier, inc=1, device_id=device(peer), device_id_type=MESH_ID)
        return carry

    lax.fori_loop(first, hi, greet, 0)
    pl.semaphore_wait(barrier, 2 * (hi - first))
    if lo == 0:
        own = pltpu.make_async_copy(src_ref.at[me], out_ref.at[0], own_sem)
        own.start()

    def send(step, carry):
        peer = lax.rem(me + step, n)
        copy(step, peer, peer).start()
        return carry

    lax.fori_loop(first, hi, send, 0)

    def finish(step, carry):
        peer = lax.rem(me + step, n)
        copy(step, peer, peer).wait_send()
        source = lax.rem(me + n - step, n)
        copy(step, source, me).wait_recv()
        return carry

    lax.fori_loop(first, hi, finish, 0)
    if lo == 0:
        own.wait()


def exchange_steps(pieces, axis, lo, hi, ident):
    n = lax.axis_size(axis)
    other = "col" if axis == "row" else "row"
    shape = (hi - lo,) + pieces.shape[1:]
    return pl.pallas_call(
        functools.partial(_steps_kernel, axis, other, n, lo, hi),
        out_shape=jax.ShapeDtypeStruct(shape, pieces.dtype),
        in_specs=[pl.BlockSpec(memory_space=pl.ANY)],
        out_specs=pl.BlockSpec(memory_space=pl.ANY),
        scratch_shapes=[
            pltpu.SemaphoreType.DMA((hi - lo,)),
            pltpu.SemaphoreType.DMA((hi - lo,)),
            pltpu.SemaphoreType.DMA(()),
        ],
        compiler_params=pltpu.CompilerParams(collective_id=ident, has_side_effects=True),
        cost_estimate=pl.CostEstimate(
            flops=0, transcendentals=0, bytes_accessed=2 * (hi - lo) * pieces[0].size * pieces.dtype.itemsize
        ),
    )(pieces)


def exchange(x, axis, broadcast, ident):
    n = lax.axis_size(axis)
    other = "col" if axis == "row" else "row"
    shape = (n,) + (x.shape if broadcast else x.shape[1:])
    return pl.pallas_call(
        functools.partial(_exchange_kernel, axis, other, n, broadcast),
        out_shape=jax.ShapeDtypeStruct(shape, x.dtype),
        in_specs=[pl.BlockSpec(memory_space=pl.ANY)],
        out_specs=pl.BlockSpec(memory_space=pl.ANY),
        scratch_shapes=[
            pltpu.SemaphoreType.DMA((n,)),
            pltpu.SemaphoreType.DMA((n,)),
            pltpu.SemaphoreType.DMA(()),
        ],
        compiler_params=pltpu.CompilerParams(collective_id=ident, has_side_effects=True),
        cost_estimate=pl.CostEstimate(
            flops=0, transcendentals=0, bytes_accessed=2 * n * x.size * x.dtype.itemsize
        ),
    )(x)


def _slot_kernel(backward, slots, src_ids, tgt_ids, count_ref, vals_ref, src_ref, out_ref, acc_ref):
    s = pl.program_id(0)

    @pl.when(s == 0)
    def _():
        acc_ref[...] = jnp.zeros_like(acc_ref)

    @pl.when(s < count_ref[0])
    def _():
        block = vals_ref[0]
        segment = src_ref[0]
        if backward:
            dims = (((0,), (0,)), ((), ()))
        else:
            dims = (((1,), (0,)), ((), ()))
        product = lax.dot_general(block, segment, dims, preferred_element_type=jnp.float32)
        target = tgt_ids[s]
        acc_ref[target] = acc_ref[target] + product

    @pl.when(s == slots - 1)
    def _():
        out_ref[...] = acc_ref[...].astype(out_ref.dtype)


def slot_product(tile_values, tile_rows, tile_cols, live_count, source, out_len, backward):
    slots, block_size = tile_values.shape[0], tile_values.shape[1]
    width = source.shape[1]
    n_src = source.shape[0] // block_size
    n_out = out_len // block_size
    panels = source.reshape(n_src, block_size, width)
    if backward:
        src_ids, tgt_ids = tile_rows, tile_cols
    else:
        src_ids, tgt_ids = tile_cols, tile_rows
    src_ids = jnp.clip(src_ids, 0, n_src - 1).astype(jnp.int32)
    tgt_ids = jnp.clip(tgt_ids, 0, n_out - 1).astype(jnp.int32)
    count = jnp.reshape(live_count, (1,)).astype(jnp.int32)
    grid_spec = pltpu.PrefetchScalarGridSpec(
        num_scalar_prefetch=3,
        grid=(slots,),
        in_specs=[
            pl.BlockSpec((1, block_size, block_size), lambda s, src, tgt, cnt: (s, 0, 0)),
            pl.BlockSpec((1, block_size, width), lambda s, src, tgt, cnt: (src[s], 0, 0)),
        ],
        out_specs=pl.BlockSpec((n_out, block_size, width), lambda s, src, tgt, cnt: (0, 0, 0)),
        scratch_shapes=[pltpu.VMEM((n_out, block_size, width), jnp.float32)],
    )
    out = pl.pallas_call(
        functools.partial(_slot_kernel, backward, slots),
        out_shape=jax.ShapeDtypeStruct((n_out, block_size, width), jnp.bfloat16),
        grid_spec=grid_spec,
        compiler_params=pltpu.CompilerParams(
            dimension_semantics=("arbitrary",), vmem_limit_bytes=48 * 1024 * 1024
        ),
        cost_estimate=pl.CostEstimate(
            flops=2 * slots * block_size * block_size * width,
            transcendentals=0,
            bytes_accessed=2 * (slots * block_size * (block_size + width) + n_out * block_size * width),
        ),
    )(src_ids, tgt_ids, count, tile_values, panels)
    return out.reshape(out_len, width)


def gather_rows(x, axis):
    count = lax.axis_size(axis)
    stacked = jnp.broadcast_to(x[None], (count,) + x.shape)
    received = lax.all_to_all(stacked, axis, split_axis=0, concat_axis=0, tiled=True)
    return received.reshape((count * x.shape[0],) + x.shape[1:])


def scatter_sum(x, axis):
    count = lax.axis_size(axis)
    pieces = x.reshape((count, x.shape[0] // count) + x.shape[1:])
    received = lax.all_to_all(pieces, axis, split_axis=0, concat_axis=0, tiled=True)
    return jnp.sum(received.astype(jnp.float32), axis=0)


def pack_grads(local_weight, local_bias):
    pad = jnp.zeros((local_weight.shape[0], 127), jnp.float32)
    return jnp.concatenate([local_weight, local_bias[:, None], pad], axis=1)


def unpack_grads(by_col_then_row, width):
    cols, rows = by_col_then_row.shape[0], by_col_then_row.shape[1]
    whole = by_col_then_row.transpose(1, 0, 2).reshape(cols * rows, -1)
    return whole[:, :width], whole[:, width]


def transposed_product(left, weight):
    return lax.dot_general(
        left, weight, (((1,), (1,)), ((), ())), preferred_element_type=jnp.float32
    ).astype(jnp.bfloat16)


def source_total(received):
    return jnp.sum(received.astype(jnp.float32), axis=0).astype(jnp.bfloat16)


def per_device(
    features, block_values, block_rows, block_cols, block_count, weight, bias, cotangent
):
    tile_values = block_values[0, 0]
    tile_rows = block_rows[0, 0]
    tile_cols = block_cols[0, 0]
    live_count = block_count[0, 0]
    own_nodes = features.shape[0]
    width = features.shape[1]
    row_len = lax.axis_size("col") * own_nodes
    gathered = gather_rows(features, "row")
    col_len = gathered.shape[0]
    partial_value = slot_product(
        tile_values, tile_rows, tile_cols, live_count, gathered, row_len, False
    )
    pieces = partial_value.reshape(lax.axis_size("col"), own_nodes, width)
    received = exchange_steps(pieces, "col", 0, lax.axis_size("col"), 2)
    aggregate = jnp.sum(received.astype(jnp.float32), axis=0).astype(jnp.bfloat16)
    preact = jnp.dot(aggregate, weight, preferred_element_type=jnp.float32) + bias
    hidden = jax.nn.silu(preact).astype(jnp.bfloat16)
    sigma = jax.nn.sigmoid(preact)
    grad_pre = cotangent.astype(jnp.float32) * sigma * (1.0 + preact * (1.0 - sigma))
    grad_low = grad_pre.astype(jnp.bfloat16)
    local_weight = lax.dot_general(
        aggregate, grad_low, (((0,), (0,)), ((), ())), preferred_element_type=jnp.float32
    )
    local_bias = jnp.sum(grad_pre, axis=0)
    grad_agg = transposed_product(grad_low, weight)
    packed = pack_grads(local_weight, local_bias)
    by_row = scatter_sum(packed, "row")
    grad_panel = exchange(grad_agg, "col", True, 0).reshape(-1, width)
    grad_panel, by_row = lax.optimization_barrier((grad_panel, by_row))
    reduced = scatter_sum(by_row, "col")
    back = slot_product(tile_values, tile_rows, tile_cols, live_count, grad_panel, col_len, True)
    back_low = back.astype(jnp.bfloat16).reshape(col_len // own_nodes, own_nodes, width)
    back_low, reduced = lax.optimization_barrier((back_low, reduced))
    row_part = gather_rows(reduced, "row")
    half = lax.axis_size("row") // 2
    first_half = exchange_steps(back_low, "row", 0, half, 1)
    first_half, row_part, back_low = lax.optimization_barrier((first_half, row_part, back_low))
    every = gather_rows(row_part[None], "col")
    second_half = exchange_steps(back_low, "row", half, lax.axis_size("row"), 3)
    every_piece = jnp.concatenate([first_half, second_half], axis=0)
    feature_grad = jnp.sum(every_piece.astype(jnp.float32), axis=0).astype(jnp.bfloat16)
    weight_grad, bias_grad = unpack_grads(every, width)
    return (hidden, weight_grad, bias_grad, feature_grad)


def solution(mesh):
    in_specs = (
        P(("col", "row"), None),
        P("row", "col", None, None, None),
        P("row", "col", None),
        P("row", "col", None),
        P("row", "col"),
        P(),
        P(),
        P(("row", "col"), None),
    )
    out_specs = (P(("row", "col"), None), P(), P(), P(("col", "row"), None))
    return jax.shard_map(
        per_device, mesh=mesh, in_specs=in_specs, out_specs=out_specs, check_vma=False
    )
```

```python
import functools

import jax
import jax.numpy as jnp
from jax import lax
from jax.experimental import pallas as pl
from jax.experimental.pallas import tpu as pltpu
from jax.sharding import PartitionSpec as P

MESH_ID = pl.DeviceIdType.MESH


def _exchange_kernel(axis, other, n, broadcast, src_ref, out_ref, send_sem, recv_sem, own_sem):
    me = lax.axis_index(axis)
    there = lax.axis_index(other)

    def device(k):
        return (k, there) if axis == "row" else (there, k)

    def piece(k):
        return src_ref if broadcast else src_ref.at[k]

    barrier = pltpu.get_barrier_semaphore()

    def greet(step, carry):
        peer = lax.rem(me + step, n)
        pl.semaphore_signal(barrier, inc=1, device_id=device(peer), device_id_type=MESH_ID)
        return carry

    lax.fori_loop(1, n, greet, 0)
    pl.semaphore_wait(barrier, n - 1)

    own = pltpu.make_async_copy(piece(me), out_ref.at[me], own_sem)
    own.start()

    def send(step, carry):
        peer = lax.rem(me + step, n)
        pltpu.make_async_remote_copy(
            src_ref=piece(peer), dst_ref=out_ref.at[me], send_sem=send_sem.at[step],
            recv_sem=recv_sem.at[step], device_id=device(peer), device_id_type=MESH_ID,
        ).start()
        return carry

    lax.fori_loop(1, n, send, 0)

    def finish(step, carry):
        peer = lax.rem(me + step, n)
        source = lax.rem(me + n - step, n)
        pltpu.make_async_remote_copy(
            src_ref=piece(peer), dst_ref=out_ref.at[me], send_sem=send_sem.at[step],
            recv_sem=recv_sem.at[step], device_id=device(peer), device_id_type=MESH_ID,
        ).wait_send()
        pltpu.make_async_remote_copy(
            src_ref=piece(source), dst_ref=out_ref.at[source], send_sem=send_sem.at[step],
            recv_sem=recv_sem.at[step], device_id=device(source), device_id_type=MESH_ID,
        ).wait_recv()
        return carry

    lax.fori_loop(1, n, finish, 0)
    own.wait()


def _steps_kernel(axis, other, n, first, stride, count, src_ref, out_ref, send_sem, recv_sem, own_sem):
    me = lax.axis_index(axis)
    there = lax.axis_index(other)
    begin = 1 if first == 0 else 0

    def device(k):
        return (k, there) if axis == "row" else (there, k)

    def copy(slot, peer, piece):
        return pltpu.make_async_remote_copy(
            src_ref=src_ref.at[piece], dst_ref=out_ref.at[slot], send_sem=send_sem.at[slot],
            recv_sem=recv_sem.at[slot], device_id=device(peer), device_id_type=MESH_ID,
        )

    barrier = pltpu.get_barrier_semaphore()

    def greet(slot, carry):
        step = first + stride * slot
        for peer in (lax.rem(me + step, n), lax.rem(me + n - step, n)):
            pl.semaphore_signal(barrier, inc=1, device_id=device(peer), device_id_type=MESH_ID)
        return carry

    lax.fori_loop(begin, count, greet, 0)
    pl.semaphore_wait(barrier, 2 * (count - begin))
    if first == 0:
        own = pltpu.make_async_copy(src_ref.at[me], out_ref.at[0], own_sem)
        own.start()

    def send(slot, carry):
        peer = lax.rem(me + first + stride * slot, n)
        copy(slot, peer, peer).start()
        return carry

    lax.fori_loop(begin, count, send, 0)

    def finish(slot, carry):
        step = first + stride * slot
        peer = lax.rem(me + step, n)
        copy(slot, peer, peer).wait_send()
        source = lax.rem(me + n - step, n)
        copy(slot, source, me).wait_recv()
        return carry

    lax.fori_loop(begin, count, finish, 0)
    if first == 0:
        own.wait()


def exchange_steps(pieces, axis, first, stride, ident):
    n = lax.axis_size(axis)
    count = (n - first + stride - 1) // stride
    other = "col" if axis == "row" else "row"
    shape = (count,) + pieces.shape[1:]
    return pl.pallas_call(
        functools.partial(_steps_kernel, axis, other, n, first, stride, count),
        out_shape=jax.ShapeDtypeStruct(shape, pieces.dtype),
        in_specs=[pl.BlockSpec(memory_space=pl.ANY)],
        out_specs=pl.BlockSpec(memory_space=pl.ANY),
        scratch_shapes=[
            pltpu.SemaphoreType.DMA((count,)),
            pltpu.SemaphoreType.DMA((count,)),
            pltpu.SemaphoreType.DMA(()),
        ],
        compiler_params=pltpu.CompilerParams(collective_id=ident, has_side_effects=True),
        cost_estimate=pl.CostEstimate(
            flops=0, transcendentals=0, bytes_accessed=2 * count * pieces[0].size * pieces.dtype.itemsize
        ),
    )(pieces)


def exchange(x, axis, broadcast, ident):
    n = lax.axis_size(axis)
    other = "col" if axis == "row" else "row"
    shape = (n,) + (x.shape if broadcast else x.shape[1:])
    return pl.pallas_call(
        functools.partial(_exchange_kernel, axis, other, n, broadcast),
        out_shape=jax.ShapeDtypeStruct(shape, x.dtype),
        in_specs=[pl.BlockSpec(memory_space=pl.ANY)],
        out_specs=pl.BlockSpec(memory_space=pl.ANY),
        scratch_shapes=[
            pltpu.SemaphoreType.DMA((n,)),
            pltpu.SemaphoreType.DMA((n,)),
            pltpu.SemaphoreType.DMA(()),
        ],
        compiler_params=pltpu.CompilerParams(collective_id=ident, has_side_effects=True),
        cost_estimate=pl.CostEstimate(
            flops=0, transcendentals=0, bytes_accessed=2 * n * x.size * x.dtype.itemsize
        ),
    )(x)


def _slot_kernel(backward, slots, src_ids, tgt_ids, count_ref, vals_ref, src_ref, out_ref, acc_ref):
    s = pl.program_id(0)

    @pl.when(s == 0)
    def _():
        acc_ref[...] = jnp.zeros_like(acc_ref)

    @pl.when(s < count_ref[0])
    def _():
        block = vals_ref[0]
        segment = src_ref[0]
        if backward:
            dims = (((0,), (0,)), ((), ()))
        else:
            dims = (((1,), (0,)), ((), ()))
        product = lax.dot_general(block, segment, dims, preferred_element_type=jnp.float32)
        target = tgt_ids[s]
        acc_ref[target] = acc_ref[target] + product

    @pl.when(s == slots - 1)
    def _():
        out_ref[...] = acc_ref[...].astype(out_ref.dtype)


def slot_product(tile_values, tile_rows, tile_cols, live_count, source, out_len, backward):
    slots, block_size = tile_values.shape[0], tile_values.shape[1]
    width = source.shape[1]
    n_src = source.shape[0] // block_size
    n_out = out_len // block_size
    panels = source.reshape(n_src, block_size, width)
    if backward:
        src_ids, tgt_ids = tile_rows, tile_cols
    else:
        src_ids, tgt_ids = tile_cols, tile_rows
    src_ids = jnp.clip(src_ids, 0, n_src - 1).astype(jnp.int32)
    tgt_ids = jnp.clip(tgt_ids, 0, n_out - 1).astype(jnp.int32)
    count = jnp.reshape(live_count, (1,)).astype(jnp.int32)
    grid_spec = pltpu.PrefetchScalarGridSpec(
        num_scalar_prefetch=3,
        grid=(slots,),
        in_specs=[
            pl.BlockSpec((1, block_size, block_size), lambda s, src, tgt, cnt: (s, 0, 0)),
            pl.BlockSpec((1, block_size, width), lambda s, src, tgt, cnt: (src[s], 0, 0)),
        ],
        out_specs=pl.BlockSpec((n_out, block_size, width), lambda s, src, tgt, cnt: (0, 0, 0)),
        scratch_shapes=[pltpu.VMEM((n_out, block_size, width), jnp.float32)],
    )
    out = pl.pallas_call(
        functools.partial(_slot_kernel, backward, slots),
        out_shape=jax.ShapeDtypeStruct((n_out, block_size, width), jnp.bfloat16),
        grid_spec=grid_spec,
        compiler_params=pltpu.CompilerParams(
            dimension_semantics=("arbitrary",), vmem_limit_bytes=48 * 1024 * 1024
        ),
        cost_estimate=pl.CostEstimate(
            flops=2 * slots * block_size * block_size * width,
            transcendentals=0,
            bytes_accessed=2 * (slots * block_size * (block_size + width) + n_out * block_size * width),
        ),
    )(src_ids, tgt_ids, count, tile_values, panels)
    return out.reshape(out_len, width)


def gather_rows(x, axis):
    count = lax.axis_size(axis)
    stacked = jnp.broadcast_to(x[None], (count,) + x.shape)
    received = lax.all_to_all(stacked, axis, split_axis=0, concat_axis=0, tiled=True)
    return received.reshape((count * x.shape[0],) + x.shape[1:])


def scatter_sum(x, axis):
    count = lax.axis_size(axis)
    pieces = x.reshape((count, x.shape[0] // count) + x.shape[1:])
    received = lax.all_to_all(pieces, axis, split_axis=0, concat_axis=0, tiled=True)
    return jnp.sum(received.astype(jnp.float32), axis=0)


def pack_grads(local_weight, local_bias):
    pad = jnp.zeros((local_weight.shape[0], 127), jnp.float32)
    return jnp.concatenate([local_weight, local_bias[:, None], pad], axis=1)


def unpack_grads(by_col_then_row, width):
    cols, rows = by_col_then_row.shape[0], by_col_then_row.shape[1]
    whole = by_col_then_row.transpose(1, 0, 2).reshape(cols * rows, -1)
    return whole[:, :width], whole[:, width]


def transposed_product(left, weight):
    return lax.dot_general(
        left, weight, (((1,), (1,)), ((), ())), preferred_element_type=jnp.float32
    ).astype(jnp.bfloat16)


def source_total(received):
    return jnp.sum(received.astype(jnp.float32), axis=0).astype(jnp.bfloat16)


def per_device(
    features, block_values, block_rows, block_cols, block_count, weight, bias, cotangent
):
    tile_values = block_values[0, 0]
    tile_rows = block_rows[0, 0]
    tile_cols = block_cols[0, 0]
    live_count = block_count[0, 0]
    own_nodes = features.shape[0]
    width = features.shape[1]
    row_len = lax.axis_size("col") * own_nodes
    gathered = gather_rows(features, "row")
    col_len = gathered.shape[0]
    partial_value = slot_product(
        tile_values, tile_rows, tile_cols, live_count, gathered, row_len, False
    )
    pieces = partial_value.reshape(lax.axis_size("col"), own_nodes, width)
    received = exchange_steps(pieces, "col", 0, 1, 2)
    aggregate = jnp.sum(received.astype(jnp.float32), axis=0).astype(jnp.bfloat16)
    preact = jnp.dot(aggregate, weight, preferred_element_type=jnp.float32) + bias
    hidden = jax.nn.silu(preact).astype(jnp.bfloat16)
    sigma = jax.nn.sigmoid(preact)
    grad_pre = cotangent.astype(jnp.float32) * sigma * (1.0 + preact * (1.0 - sigma))
    grad_low = grad_pre.astype(jnp.bfloat16)
    local_weight = lax.dot_general(
        aggregate, grad_low, (((0,), (0,)), ((), ())), preferred_element_type=jnp.float32
    )
    local_bias = jnp.sum(grad_pre, axis=0)
    grad_agg = transposed_product(grad_low, weight)
    packed = pack_grads(local_weight, local_bias)
    by_row = scatter_sum(packed, "row")
    grad_panel = exchange(grad_agg, "col", True, 0).reshape(-1, width)
    grad_panel, by_row = lax.optimization_barrier((grad_panel, by_row))
    reduced = scatter_sum(by_row, "col")
    back = slot_product(tile_values, tile_rows, tile_cols, live_count, grad_panel, col_len, True)
    back_low = back.astype(jnp.bfloat16).reshape(col_len // own_nodes, own_nodes, width)
    back_low, reduced = lax.optimization_barrier((back_low, reduced))
    row_part = gather_rows(reduced, "row")
    first_half = exchange_steps(back_low, "row", 1, 2, 1)
    first_half, row_part, back_low = lax.optimization_barrier((first_half, row_part, back_low))
    every = gather_rows(row_part[None], "col")
    second_half = exchange_steps(back_low, "row", 0, 2, 3)
    every_piece = jnp.concatenate([first_half, second_half], axis=0)
    feature_grad = jnp.sum(every_piece.astype(jnp.float32), axis=0).astype(jnp.bfloat16)
    weight_grad, bias_grad = unpack_grads(every, width)
    return (hidden, weight_grad, bias_grad, feature_grad)


def solution(mesh):
    in_specs = (
        P(("col", "row"), None),
        P("row", "col", None, None, None),
        P("row", "col", None),
        P("row", "col", None),
        P("row", "col"),
        P(),
        P(),
        P(("row", "col"), None),
    )
    out_specs = (P(("row", "col"), None), P(), P(), P(("col", "row"), None))
    return jax.shard_map(
        per_device, mesh=mesh, in_specs=in_specs, out_specs=out_specs, check_vma=False
    )
```

```python
import functools

import jax
import jax.numpy as jnp
from jax import lax
from jax.experimental import pallas as pl
from jax.experimental.pallas import tpu as pltpu
from jax.sharding import PartitionSpec as P

MESH_ID = pl.DeviceIdType.MESH


def _exchange_kernel(axis, other, n, broadcast, src_ref, out_ref, send_sem, recv_sem, own_sem):
    me = lax.axis_index(axis)
    there = lax.axis_index(other)

    def device(k):
        return (k, there) if axis == "row" else (there, k)

    def piece(k):
        return src_ref if broadcast else src_ref.at[k]

    barrier = pltpu.get_barrier_semaphore()

    def greet(step, carry):
        peer = lax.rem(me + step, n)
        pl.semaphore_signal(barrier, inc=1, device_id=device(peer), device_id_type=MESH_ID)
        return carry

    lax.fori_loop(1, n, greet, 0)
    pl.semaphore_wait(barrier, n - 1)

    own = pltpu.make_async_copy(piece(me), out_ref.at[me], own_sem)
    own.start()

    def send(step, carry):
        peer = lax.rem(me + step, n)
        pltpu.make_async_remote_copy(
            src_ref=piece(peer), dst_ref=out_ref.at[me], send_sem=send_sem.at[step],
            recv_sem=recv_sem.at[step], device_id=device(peer), device_id_type=MESH_ID,
        ).start()
        return carry

    lax.fori_loop(1, n, send, 0)

    def finish(step, carry):
        peer = lax.rem(me + step, n)
        source = lax.rem(me + n - step, n)
        pltpu.make_async_remote_copy(
            src_ref=piece(peer), dst_ref=out_ref.at[me], send_sem=send_sem.at[step],
            recv_sem=recv_sem.at[step], device_id=device(peer), device_id_type=MESH_ID,
        ).wait_send()
        pltpu.make_async_remote_copy(
            src_ref=piece(source), dst_ref=out_ref.at[source], send_sem=send_sem.at[step],
            recv_sem=recv_sem.at[step], device_id=device(source), device_id_type=MESH_ID,
        ).wait_recv()
        return carry

    lax.fori_loop(1, n, finish, 0)
    own.wait()


def _steps_kernel(axis, other, n, first, stride, count, src_ref, out_ref, send_sem, recv_sem, own_sem):
    me = lax.axis_index(axis)
    there = lax.axis_index(other)
    begin = 1 if first == 0 else 0

    def device(k):
        return (k, there) if axis == "row" else (there, k)

    def copy(slot, peer, piece):
        return pltpu.make_async_remote_copy(
            src_ref=src_ref.at[piece], dst_ref=out_ref.at[slot], send_sem=send_sem.at[slot],
            recv_sem=recv_sem.at[slot], device_id=device(peer), device_id_type=MESH_ID,
        )

    barrier = pltpu.get_barrier_semaphore()

    def greet(slot, carry):
        step = first + stride * slot
        for peer in (lax.rem(me + step, n), lax.rem(me + n - step, n)):
            pl.semaphore_signal(barrier, inc=1, device_id=device(peer), device_id_type=MESH_ID)
        return carry

    lax.fori_loop(begin, count, greet, 0)
    pl.semaphore_wait(barrier, 2 * (count - begin))
    if first == 0:
        own = pltpu.make_async_copy(src_ref.at[me], out_ref.at[0], own_sem)
        own.start()

    def send(slot, carry):
        peer = lax.rem(me + first + stride * slot, n)
        copy(slot, peer, peer).start()
        return carry

    lax.fori_loop(begin, count, send, 0)

    def finish(slot, carry):
        step = first + stride * slot
        peer = lax.rem(me + step, n)
        copy(slot, peer, peer).wait_send()
        source = lax.rem(me + n - step, n)
        copy(slot, source, me).wait_recv()
        return carry

    lax.fori_loop(begin, count, finish, 0)
    if first == 0:
        own.wait()


def exchange_steps(pieces, axis, first, stride, ident):
    n = lax.axis_size(axis)
    count = (n - first + stride - 1) // stride
    other = "col" if axis == "row" else "row"
    shape = (count,) + pieces.shape[1:]
    return pl.pallas_call(
        functools.partial(_steps_kernel, axis, other, n, first, stride, count),
        out_shape=jax.ShapeDtypeStruct(shape, pieces.dtype),
        in_specs=[pl.BlockSpec(memory_space=pl.ANY)],
        out_specs=pl.BlockSpec(memory_space=pl.ANY),
        scratch_shapes=[
            pltpu.SemaphoreType.DMA((count,)),
            pltpu.SemaphoreType.DMA((count,)),
            pltpu.SemaphoreType.DMA(()),
        ],
        compiler_params=pltpu.CompilerParams(collective_id=ident, has_side_effects=True),
        cost_estimate=pl.CostEstimate(
            flops=0, transcendentals=0, bytes_accessed=2 * count * pieces[0].size * pieces.dtype.itemsize
        ),
    )(pieces)


def _steps_gather_kernel(
    axis, other, n, m, first, stride, count, src_ref, extra_ref, out_ref, extra_out,
    send_sem, recv_sem, own_sem, extra_send, extra_recv, extra_own,
):
    me = lax.axis_index(axis)
    there = lax.axis_index(other)
    begin = 1 if first == 0 else 0

    def device(k):
        return (k, there) if axis == "row" else (there, k)

    def across(k):
        return (me, k) if axis == "row" else (k, me)

    def copy(slot, peer, piece):
        return pltpu.make_async_remote_copy(
            src_ref=src_ref.at[piece], dst_ref=out_ref.at[slot], send_sem=send_sem.at[slot],
            recv_sem=recv_sem.at[slot], device_id=device(peer), device_id_type=MESH_ID,
        )

    def extra_copy(offset, peer, slot):
        return pltpu.make_async_remote_copy(
            src_ref=extra_ref, dst_ref=extra_out.at[slot], send_sem=extra_send.at[offset],
            recv_sem=extra_recv.at[offset], device_id=across(peer), device_id_type=MESH_ID,
        )

    barrier = pltpu.get_barrier_semaphore()

    def greet(slot, carry):
        step = first + stride * slot
        for peer in (lax.rem(me + step, n), lax.rem(me + n - step, n)):
            pl.semaphore_signal(barrier, inc=1, device_id=device(peer), device_id_type=MESH_ID)
        return carry

    def greet_across(offset, carry):
        peer = lax.rem(there + offset, m)
        pl.semaphore_signal(barrier, inc=1, device_id=across(peer), device_id_type=MESH_ID)
        return carry

    lax.fori_loop(begin, count, greet, 0)
    lax.fori_loop(1, m, greet_across, 0)
    pl.semaphore_wait(barrier, 2 * (count - begin) + m - 1)
    own_extra = pltpu.make_async_copy(extra_ref, extra_out.at[there], extra_own)
    own_extra.start()
    if first == 0:
        own = pltpu.make_async_copy(src_ref.at[me], out_ref.at[0], own_sem)
        own.start()

    def send_across(offset, carry):
        extra_copy(offset, lax.rem(there + offset, m), there).start()
        return carry

    lax.fori_loop(1, m, send_across, 0)

    def send(slot, carry):
        peer = lax.rem(me + first + stride * slot, n)
        copy(slot, peer, peer).start()
        return carry

    lax.fori_loop(begin, count, send, 0)

    def finish(slot, carry):
        step = first + stride * slot
        peer = lax.rem(me + step, n)
        copy(slot, peer, peer).wait_send()
        source = lax.rem(me + n - step, n)
        copy(slot, source, me).wait_recv()
        return carry

    lax.fori_loop(begin, count, finish, 0)

    def finish_across(offset, carry):
        extra_copy(offset, lax.rem(there + offset, m), there).wait_send()
        source = lax.rem(there + m - offset, m)
        extra_copy(offset, source, source).wait_recv()
        return carry

    lax.fori_loop(1, m, finish_across, 0)
    own_extra.wait()
    if first == 0:
        own.wait()


def exchange_steps_and_gather(pieces, extra, axis, first, stride, ident):
    n = lax.axis_size(axis)
    other = "col" if axis == "row" else "row"
    m = lax.axis_size(other)
    count = (n - first + stride - 1) // stride
    shapes = (
        jax.ShapeDtypeStruct((count,) + pieces.shape[1:], pieces.dtype),
        jax.ShapeDtypeStruct((m,) + extra.shape, extra.dtype),
    )
    moved = 2 * count * pieces[0].size * pieces.dtype.itemsize + 2 * m * extra.size * extra.dtype.itemsize
    return pl.pallas_call(
        functools.partial(_steps_gather_kernel, axis, other, n, m, first, stride, count),
        out_shape=shapes,
        in_specs=[pl.BlockSpec(memory_space=pl.ANY), pl.BlockSpec(memory_space=pl.ANY)],
        out_specs=(pl.BlockSpec(memory_space=pl.ANY), pl.BlockSpec(memory_space=pl.ANY)),
        scratch_shapes=[
            pltpu.SemaphoreType.DMA((count,)),
            pltpu.SemaphoreType.DMA((count,)),
            pltpu.SemaphoreType.DMA(()),
            pltpu.SemaphoreType.DMA((m,)),
            pltpu.SemaphoreType.DMA((m,)),
            pltpu.SemaphoreType.DMA(()),
        ],
        compiler_params=pltpu.CompilerParams(collective_id=ident, has_side_effects=True),
        cost_estimate=pl.CostEstimate(flops=0, transcendentals=0, bytes_accessed=moved),
    )(pieces, extra)


def exchange(x, axis, broadcast, ident):
    n = lax.axis_size(axis)
    other = "col" if axis == "row" else "row"
    shape = (n,) + (x.shape if broadcast else x.shape[1:])
    return pl.pallas_call(
        functools.partial(_exchange_kernel, axis, other, n, broadcast),
        out_shape=jax.ShapeDtypeStruct(shape, x.dtype),
        in_specs=[pl.BlockSpec(memory_space=pl.ANY)],
        out_specs=pl.BlockSpec(memory_space=pl.ANY),
        scratch_shapes=[
            pltpu.SemaphoreType.DMA((n,)),
            pltpu.SemaphoreType.DMA((n,)),
            pltpu.SemaphoreType.DMA(()),
        ],
        compiler_params=pltpu.CompilerParams(collective_id=ident, has_side_effects=True),
        cost_estimate=pl.CostEstimate(
            flops=0, transcendentals=0, bytes_accessed=2 * n * x.size * x.dtype.itemsize
        ),
    )(x)


def _slot_kernel(backward, slots, src_ids, tgt_ids, count_ref, vals_ref, src_ref, out_ref, acc_ref):
    s = pl.program_id(0)

    @pl.when(s == 0)
    def _():
        acc_ref[...] = jnp.zeros_like(acc_ref)

    @pl.when(s < count_ref[0])
    def _():
        block = vals_ref[0]
        segment = src_ref[0]
        if backward:
            dims = (((0,), (0,)), ((), ()))
        else:
            dims = (((1,), (0,)), ((), ()))
        product = lax.dot_general(block, segment, dims, preferred_element_type=jnp.float32)
        target = tgt_ids[s]
        acc_ref[target] = acc_ref[target] + product

    @pl.when(s == slots - 1)
    def _():
        out_ref[...] = acc_ref[...].astype(out_ref.dtype)


def slot_product(tile_values, tile_rows, tile_cols, live_count, source, out_len, backward):
    slots, block_size = tile_values.shape[0], tile_values.shape[1]
    width = source.shape[1]
    n_src = source.shape[0] // block_size
    n_out = out_len // block_size
    panels = source.reshape(n_src, block_size, width)
    if backward:
        src_ids, tgt_ids = tile_rows, tile_cols
    else:
        src_ids, tgt_ids = tile_cols, tile_rows
    src_ids = jnp.clip(src_ids, 0, n_src - 1).astype(jnp.int32)
    tgt_ids = jnp.clip(tgt_ids, 0, n_out - 1).astype(jnp.int32)
    count = jnp.reshape(live_count, (1,)).astype(jnp.int32)
    grid_spec = pltpu.PrefetchScalarGridSpec(
        num_scalar_prefetch=3,
        grid=(slots,),
        in_specs=[
            pl.BlockSpec((1, block_size, block_size), lambda s, src, tgt, cnt: (s, 0, 0)),
            pl.BlockSpec((1, block_size, width), lambda s, src, tgt, cnt: (src[s], 0, 0)),
        ],
        out_specs=pl.BlockSpec((n_out, block_size, width), lambda s, src, tgt, cnt: (0, 0, 0)),
        scratch_shapes=[pltpu.VMEM((n_out, block_size, width), jnp.float32)],
    )
    out = pl.pallas_call(
        functools.partial(_slot_kernel, backward, slots),
        out_shape=jax.ShapeDtypeStruct((n_out, block_size, width), jnp.bfloat16),
        grid_spec=grid_spec,
        compiler_params=pltpu.CompilerParams(
            dimension_semantics=("arbitrary",), vmem_limit_bytes=48 * 1024 * 1024
        ),
        cost_estimate=pl.CostEstimate(
            flops=2 * slots * block_size * block_size * width,
            transcendentals=0,
            bytes_accessed=2 * (slots * block_size * (block_size + width) + n_out * block_size * width),
        ),
    )(src_ids, tgt_ids, count, tile_values, panels)
    return out.reshape(out_len, width)


def gather_rows(x, axis):
    count = lax.axis_size(axis)
    stacked = jnp.broadcast_to(x[None], (count,) + x.shape)
    received = lax.all_to_all(stacked, axis, split_axis=0, concat_axis=0, tiled=True)
    return received.reshape((count * x.shape[0],) + x.shape[1:])


def scatter_sum(x, axis):
    count = lax.axis_size(axis)
    pieces = x.reshape((count, x.shape[0] // count) + x.shape[1:])
    received = lax.all_to_all(pieces, axis, split_axis=0, concat_axis=0, tiled=True)
    return jnp.sum(received.astype(jnp.float32), axis=0)


def pack_grads(local_weight, local_bias):
    pad = jnp.zeros((local_weight.shape[0], 127), jnp.float32)
    return jnp.concatenate([local_weight, local_bias[:, None], pad], axis=1)


def unpack_grads(by_col_then_row, width):
    cols, rows = by_col_then_row.shape[0], by_col_then_row.shape[1]
    whole = by_col_then_row.transpose(1, 0, 2).reshape(cols * rows, -1)
    return whole[:, :width], whole[:, width]


def transposed_product(left, weight):
    return lax.dot_general(
        left, weight, (((1,), (1,)), ((), ())), preferred_element_type=jnp.float32
    ).astype(jnp.bfloat16)


def source_total(received):
    return jnp.sum(received.astype(jnp.float32), axis=0).astype(jnp.bfloat16)


def per_device(
    features, block_values, block_rows, block_cols, block_count, weight, bias, cotangent
):
    tile_values = block_values[0, 0]
    tile_rows = block_rows[0, 0]
    tile_cols = block_cols[0, 0]
    live_count = block_count[0, 0]
    own_nodes = features.shape[0]
    width = features.shape[1]
    row_len = lax.axis_size("col") * own_nodes
    gathered = gather_rows(features, "row")
    col_len = gathered.shape[0]
    partial_value = slot_product(
        tile_values, tile_rows, tile_cols, live_count, gathered, row_len, False
    )
    pieces = partial_value.reshape(lax.axis_size("col"), own_nodes, width)
    received = exchange_steps(pieces, "col", 0, 1, 2)
    aggregate = jnp.sum(received.astype(jnp.float32), axis=0).astype(jnp.bfloat16)
    preact = jnp.dot(aggregate, weight, preferred_element_type=jnp.float32) + bias
    hidden = jax.nn.silu(preact).astype(jnp.bfloat16)
    sigma = jax.nn.sigmoid(preact)
    grad_pre = cotangent.astype(jnp.float32) * sigma * (1.0 + preact * (1.0 - sigma))
    grad_low = grad_pre.astype(jnp.bfloat16)
    local_weight = lax.dot_general(
        aggregate, grad_low, (((0,), (0,)), ((), ())), preferred_element_type=jnp.float32
    )
    local_bias = jnp.sum(grad_pre, axis=0)
    grad_agg = transposed_product(grad_low, weight)
    packed = pack_grads(local_weight, local_bias)
    by_row = scatter_sum(packed, "row")
    grad_panel = exchange(grad_agg, "col", True, 0).reshape(-1, width)
    grad_panel, by_row = lax.optimization_barrier((grad_panel, by_row))
    reduced = scatter_sum(by_row, "col")
    back = slot_product(tile_values, tile_rows, tile_cols, live_count, grad_panel, col_len, True)
    back_low = back.astype(jnp.bfloat16).reshape(col_len // own_nodes, own_nodes, width)
    back_low, reduced = lax.optimization_barrier((back_low, reduced))
    row_part = gather_rows(reduced, "row")
    first_half = exchange_steps(back_low, "row", 1, 2, 1)
    first_half, row_part, back_low = lax.optimization_barrier((first_half, row_part, back_low))
    second_half, every = exchange_steps_and_gather(back_low, row_part, "row", 0, 2, 3)
    every_piece = jnp.concatenate([first_half, second_half], axis=0)
    feature_grad = jnp.sum(every_piece.astype(jnp.float32), axis=0).astype(jnp.bfloat16)
    weight_grad, bias_grad = unpack_grads(every, width)
    return (hidden, weight_grad, bias_grad, feature_grad)


def solution(mesh):
    in_specs = (
        P(("col", "row"), None),
        P("row", "col", None, None, None),
        P("row", "col", None),
        P("row", "col", None),
        P("row", "col"),
        P(),
        P(),
        P(("row", "col"), None),
    )
    out_specs = (P(("row", "col"), None), P(), P(), P(("col", "row"), None))
    return jax.shard_map(
        per_device, mesh=mesh, in_specs=in_specs, out_specs=out_specs, check_vma=False
    )
```

```python
import functools

import jax
import jax.numpy as jnp
from jax import lax
from jax.experimental import pallas as pl
from jax.experimental.pallas import tpu as pltpu
from jax.sharding import PartitionSpec as P

MESH_ID = pl.DeviceIdType.MESH


def _exchange_kernel(axis, other, n, broadcast, src_ref, out_ref, send_sem, recv_sem, own_sem):
    me = lax.axis_index(axis)
    there = lax.axis_index(other)

    def device(k):
        return (k, there) if axis == "row" else (there, k)

    def piece(k):
        return src_ref if broadcast else src_ref.at[k]

    barrier = pltpu.get_barrier_semaphore()

    def greet(step, carry):
        peer = lax.rem(me + step, n)
        pl.semaphore_signal(barrier, inc=1, device_id=device(peer), device_id_type=MESH_ID)
        return carry

    lax.fori_loop(1, n, greet, 0)
    pl.semaphore_wait(barrier, n - 1)

    own = pltpu.make_async_copy(piece(me), out_ref.at[me], own_sem)
    own.start()

    def send(step, carry):
        peer = lax.rem(me + step, n)
        pltpu.make_async_remote_copy(
            src_ref=piece(peer), dst_ref=out_ref.at[me], send_sem=send_sem.at[step],
            recv_sem=recv_sem.at[step], device_id=device(peer), device_id_type=MESH_ID,
        ).start()
        return carry

    lax.fori_loop(1, n, send, 0)

    def finish(step, carry):
        peer = lax.rem(me + step, n)
        source = lax.rem(me + n - step, n)
        pltpu.make_async_remote_copy(
            src_ref=piece(peer), dst_ref=out_ref.at[me], send_sem=send_sem.at[step],
            recv_sem=recv_sem.at[step], device_id=device(peer), device_id_type=MESH_ID,
        ).wait_send()
        pltpu.make_async_remote_copy(
            src_ref=piece(source), dst_ref=out_ref.at[source], send_sem=send_sem.at[step],
            recv_sem=recv_sem.at[step], device_id=device(source), device_id_type=MESH_ID,
        ).wait_recv()
        return carry

    lax.fori_loop(1, n, finish, 0)
    own.wait()


def _steps_kernel(axis, other, n, first, stride, count, src_ref, out_ref, send_sem, recv_sem, own_sem):
    me = lax.axis_index(axis)
    there = lax.axis_index(other)
    begin = 1 if first == 0 else 0

    def device(k):
        return (k, there) if axis == "row" else (there, k)

    def copy(slot, peer, piece):
        return pltpu.make_async_remote_copy(
            src_ref=src_ref.at[piece], dst_ref=out_ref.at[slot], send_sem=send_sem.at[slot],
            recv_sem=recv_sem.at[slot], device_id=device(peer), device_id_type=MESH_ID,
        )

    barrier = pltpu.get_barrier_semaphore()

    def greet(slot, carry):
        step = first + stride * slot
        for peer in (lax.rem(me + step, n), lax.rem(me + n - step, n)):
            pl.semaphore_signal(barrier, inc=1, device_id=device(peer), device_id_type=MESH_ID)
        return carry

    lax.fori_loop(begin, count, greet, 0)
    pl.semaphore_wait(barrier, 2 * (count - begin))
    if first == 0:
        own = pltpu.make_async_copy(src_ref.at[me], out_ref.at[0], own_sem)
        own.start()

    def send(slot, carry):
        peer = lax.rem(me + first + stride * slot, n)
        copy(slot, peer, peer).start()
        return carry

    lax.fori_loop(begin, count, send, 0)

    def finish(slot, carry):
        step = first + stride * slot
        peer = lax.rem(me + step, n)
        copy(slot, peer, peer).wait_send()
        source = lax.rem(me + n - step, n)
        copy(slot, source, me).wait_recv()
        return carry

    lax.fori_loop(begin, count, finish, 0)
    if first == 0:
        own.wait()


def exchange_steps(pieces, axis, first, stride, ident):
    n = lax.axis_size(axis)
    count = (n - first + stride - 1) // stride
    other = "col" if axis == "row" else "row"
    shape = (count,) + pieces.shape[1:]
    return pl.pallas_call(
        functools.partial(_steps_kernel, axis, other, n, first, stride, count),
        out_shape=jax.ShapeDtypeStruct(shape, pieces.dtype),
        in_specs=[pl.BlockSpec(memory_space=pl.ANY)],
        out_specs=pl.BlockSpec(memory_space=pl.ANY),
        scratch_shapes=[
            pltpu.SemaphoreType.DMA((count,)),
            pltpu.SemaphoreType.DMA((count,)),
            pltpu.SemaphoreType.DMA(()),
        ],
        compiler_params=pltpu.CompilerParams(collective_id=ident, has_side_effects=True),
        cost_estimate=pl.CostEstimate(
            flops=0, transcendentals=0, bytes_accessed=2 * count * pieces[0].size * pieces.dtype.itemsize
        ),
    )(pieces)


def exchange(x, axis, broadcast, ident):
    n = lax.axis_size(axis)
    other = "col" if axis == "row" else "row"
    shape = (n,) + (x.shape if broadcast else x.shape[1:])
    return pl.pallas_call(
        functools.partial(_exchange_kernel, axis, other, n, broadcast),
        out_shape=jax.ShapeDtypeStruct(shape, x.dtype),
        in_specs=[pl.BlockSpec(memory_space=pl.ANY)],
        out_specs=pl.BlockSpec(memory_space=pl.ANY),
        scratch_shapes=[
            pltpu.SemaphoreType.DMA((n,)),
            pltpu.SemaphoreType.DMA((n,)),
            pltpu.SemaphoreType.DMA(()),
        ],
        compiler_params=pltpu.CompilerParams(collective_id=ident, has_side_effects=True),
        cost_estimate=pl.CostEstimate(
            flops=0, transcendentals=0, bytes_accessed=2 * n * x.size * x.dtype.itemsize
        ),
    )(x)


def _slot_kernel(backward, slots, src_ids, tgt_ids, count_ref, vals_ref, src_ref, out_ref, acc_ref):
    s = pl.program_id(0)

    @pl.when(s == 0)
    def _():
        acc_ref[...] = jnp.zeros_like(acc_ref)

    @pl.when(s < count_ref[0])
    def _():
        block = vals_ref[0]
        segment = src_ref[0]
        if backward:
            dims = (((0,), (0,)), ((), ()))
        else:
            dims = (((1,), (0,)), ((), ()))
        product = lax.dot_general(block, segment, dims, preferred_element_type=jnp.float32)
        target = tgt_ids[s]
        acc_ref[target] = acc_ref[target] + product

    @pl.when(s == slots - 1)
    def _():
        out_ref[...] = acc_ref[...].astype(out_ref.dtype)


def slot_product(tile_values, tile_rows, tile_cols, live_count, source, out_len, backward):
    slots, block_size = tile_values.shape[0], tile_values.shape[1]
    width = source.shape[1]
    n_src = source.shape[0] // block_size
    n_out = out_len // block_size
    panels = source.reshape(n_src, block_size, width)
    if backward:
        src_ids, tgt_ids = tile_rows, tile_cols
    else:
        src_ids, tgt_ids = tile_cols, tile_rows
    src_ids = jnp.clip(src_ids, 0, n_src - 1).astype(jnp.int32)
    tgt_ids = jnp.clip(tgt_ids, 0, n_out - 1).astype(jnp.int32)
    count = jnp.reshape(live_count, (1,)).astype(jnp.int32)
    grid_spec = pltpu.PrefetchScalarGridSpec(
        num_scalar_prefetch=3,
        grid=(slots,),
        in_specs=[
            pl.BlockSpec((1, block_size, block_size), lambda s, src, tgt, cnt: (s, 0, 0)),
            pl.BlockSpec((1, block_size, width), lambda s, src, tgt, cnt: (src[s], 0, 0)),
        ],
        out_specs=pl.BlockSpec((n_out, block_size, width), lambda s, src, tgt, cnt: (0, 0, 0)),
        scratch_shapes=[pltpu.VMEM((n_out, block_size, width), jnp.float32)],
    )
    out = pl.pallas_call(
        functools.partial(_slot_kernel, backward, slots),
        out_shape=jax.ShapeDtypeStruct((n_out, block_size, width), jnp.bfloat16),
        grid_spec=grid_spec,
        compiler_params=pltpu.CompilerParams(
            dimension_semantics=("arbitrary",), vmem_limit_bytes=48 * 1024 * 1024
        ),
        cost_estimate=pl.CostEstimate(
            flops=2 * slots * block_size * block_size * width,
            transcendentals=0,
            bytes_accessed=2 * (slots * block_size * (block_size + width) + n_out * block_size * width),
        ),
    )(src_ids, tgt_ids, count, tile_values, panels)
    return out.reshape(out_len, width)


def gather_rows(x, axis):
    count = lax.axis_size(axis)
    stacked = jnp.broadcast_to(x[None], (count,) + x.shape)
    received = lax.all_to_all(stacked, axis, split_axis=0, concat_axis=0, tiled=True)
    return received.reshape((count * x.shape[0],) + x.shape[1:])


def scatter_sum(x, axis):
    count = lax.axis_size(axis)
    pieces = x.reshape((count, x.shape[0] // count) + x.shape[1:])
    received = lax.all_to_all(pieces, axis, split_axis=0, concat_axis=0, tiled=True)
    return jnp.sum(received.astype(jnp.float32), axis=0)


def pack_grads(local_weight, local_bias):
    pad = jnp.zeros((local_weight.shape[0], 127), jnp.float32)
    return jnp.concatenate([local_weight, local_bias[:, None], pad], axis=1)


def unpack_grads(by_col_then_row, width):
    cols, rows = by_col_then_row.shape[0], by_col_then_row.shape[1]
    whole = by_col_then_row.transpose(1, 0, 2).reshape(cols * rows, -1)
    return whole[:, :width], whole[:, width]


def transposed_product(left, weight):
    return lax.dot_general(
        left, weight, (((1,), (1,)), ((), ())), preferred_element_type=jnp.float32
    ).astype(jnp.bfloat16)


def source_total(received):
    return jnp.sum(received.astype(jnp.float32), axis=0).astype(jnp.bfloat16)


def per_device(
    features, block_values, block_rows, block_cols, block_count, weight, bias, cotangent
):
    tile_values = block_values[0, 0]
    tile_rows = block_rows[0, 0]
    tile_cols = block_cols[0, 0]
    live_count = block_count[0, 0]
    own_nodes = features.shape[0]
    width = features.shape[1]
    row_len = lax.axis_size("col") * own_nodes
    gathered = exchange(features, "row", True, 4).reshape(-1, width)
    col_len = gathered.shape[0]
    partial_value = slot_product(
        tile_values, tile_rows, tile_cols, live_count, gathered, row_len, False
    )
    pieces = partial_value.reshape(lax.axis_size("col"), own_nodes, width)
    received = exchange_steps(pieces, "col", 0, 1, 2)
    aggregate = jnp.sum(received.astype(jnp.float32), axis=0).astype(jnp.bfloat16)
    preact = jnp.dot(aggregate, weight, preferred_element_type=jnp.float32) + bias
    hidden = jax.nn.silu(preact).astype(jnp.bfloat16)
    sigma = jax.nn.sigmoid(preact)
    grad_pre = cotangent.astype(jnp.float32) * sigma * (1.0 + preact * (1.0 - sigma))
    grad_low = grad_pre.astype(jnp.bfloat16)
    local_weight = lax.dot_general(
        aggregate, grad_low, (((0,), (0,)), ((), ())), preferred_element_type=jnp.float32
    )
    local_bias = jnp.sum(grad_pre, axis=0)
    grad_agg = transposed_product(grad_low, weight)
    packed = pack_grads(local_weight, local_bias)
    by_row = scatter_sum(packed, "row")
    grad_panel = exchange(grad_agg, "col", True, 0).reshape(-1, width)
    grad_panel, by_row = lax.optimization_barrier((grad_panel, by_row))
    reduced = scatter_sum(by_row, "col")
    back = slot_product(tile_values, tile_rows, tile_cols, live_count, grad_panel, col_len, True)
    back_low = back.astype(jnp.bfloat16).reshape(col_len // own_nodes, own_nodes, width)
    back_low, reduced = lax.optimization_barrier((back_low, reduced))
    row_part = gather_rows(reduced, "row")
    first_half = exchange_steps(back_low, "row", 1, 2, 1)
    first_half, row_part, back_low = lax.optimization_barrier((first_half, row_part, back_low))
    every = gather_rows(row_part[None], "col")
    second_half = exchange_steps(back_low, "row", 0, 2, 3)
    every_piece = jnp.concatenate([first_half, second_half], axis=0)
    feature_grad = jnp.sum(every_piece.astype(jnp.float32), axis=0).astype(jnp.bfloat16)
    weight_grad, bias_grad = unpack_grads(every, width)
    return (hidden, weight_grad, bias_grad, feature_grad)


def solution(mesh):
    in_specs = (
        P(("col", "row"), None),
        P("row", "col", None, None, None),
        P("row", "col", None),
        P("row", "col", None),
        P("row", "col"),
        P(),
        P(),
        P(("row", "col"), None),
    )
    out_specs = (P(("row", "col"), None), P(), P(), P(("col", "row"), None))
    return jax.shard_map(
        per_device, mesh=mesh, in_specs=in_specs, out_specs=out_specs, check_vma=False
    )
```

```python
import functools

import jax
import jax.numpy as jnp
from jax import lax
from jax.experimental import pallas as pl
from jax.experimental.pallas import tpu as pltpu
from jax.sharding import PartitionSpec as P

MESH_ID = pl.DeviceIdType.MESH


def _exchange_kernel(axis, other, n, broadcast, src_ref, out_ref, send_sem, recv_sem, own_sem):
    me = lax.axis_index(axis)
    there = lax.axis_index(other)

    def device(k):
        return (k, there) if axis == "row" else (there, k)

    def piece(k):
        return src_ref if broadcast else src_ref.at[k]

    barrier = pltpu.get_barrier_semaphore()

    def greet(step, carry):
        peer = lax.rem(me + step, n)
        pl.semaphore_signal(barrier, inc=1, device_id=device(peer), device_id_type=MESH_ID)
        return carry

    lax.fori_loop(1, n, greet, 0)
    pl.semaphore_wait(barrier, n - 1)

    own = pltpu.make_async_copy(piece(me), out_ref.at[me], own_sem)
    own.start()

    def send(step, carry):
        peer = lax.rem(me + step, n)
        pltpu.make_async_remote_copy(
            src_ref=piece(peer), dst_ref=out_ref.at[me], send_sem=send_sem.at[step],
            recv_sem=recv_sem.at[step], device_id=device(peer), device_id_type=MESH_ID,
        ).start()
        return carry

    lax.fori_loop(1, n, send, 0)

    def finish(step, carry):
        peer = lax.rem(me + step, n)
        source = lax.rem(me + n - step, n)
        pltpu.make_async_remote_copy(
            src_ref=piece(peer), dst_ref=out_ref.at[me], send_sem=send_sem.at[step],
            recv_sem=recv_sem.at[step], device_id=device(peer), device_id_type=MESH_ID,
        ).wait_send()
        pltpu.make_async_remote_copy(
            src_ref=piece(source), dst_ref=out_ref.at[source], send_sem=send_sem.at[step],
            recv_sem=recv_sem.at[step], device_id=device(source), device_id_type=MESH_ID,
        ).wait_recv()
        return carry

    lax.fori_loop(1, n, finish, 0)
    own.wait()


def _steps_kernel(axis, other, n, first, stride, count, src_ref, out_ref, send_sem, recv_sem, own_sem):
    me = lax.axis_index(axis)
    there = lax.axis_index(other)
    begin = 1 if first == 0 else 0

    def device(k):
        return (k, there) if axis == "row" else (there, k)

    def copy(slot, peer, piece):
        return pltpu.make_async_remote_copy(
            src_ref=src_ref.at[piece], dst_ref=out_ref.at[slot], send_sem=send_sem.at[slot],
            recv_sem=recv_sem.at[slot], device_id=device(peer), device_id_type=MESH_ID,
        )

    barrier = pltpu.get_barrier_semaphore()

    def greet(slot, carry):
        step = first + stride * slot
        for peer in (lax.rem(me + step, n), lax.rem(me + n - step, n)):
            pl.semaphore_signal(barrier, inc=1, device_id=device(peer), device_id_type=MESH_ID)
        return carry

    lax.fori_loop(begin, count, greet, 0)
    pl.semaphore_wait(barrier, 2 * (count - begin))
    if first == 0:
        own = pltpu.make_async_copy(src_ref.at[me], out_ref.at[0], own_sem)
        own.start()

    def send(slot, carry):
        peer = lax.rem(me + first + stride * slot, n)
        copy(slot, peer, peer).start()
        return carry

    lax.fori_loop(begin, count, send, 0)

    def finish(slot, carry):
        step = first + stride * slot
        peer = lax.rem(me + step, n)
        copy(slot, peer, peer).wait_send()
        source = lax.rem(me + n - step, n)
        copy(slot, source, me).wait_recv()
        return carry

    lax.fori_loop(begin, count, finish, 0)
    if first == 0:
        own.wait()


def exchange_steps(pieces, axis, first, stride, ident):
    n = lax.axis_size(axis)
    count = (n - first + stride - 1) // stride
    other = "col" if axis == "row" else "row"
    shape = (count,) + pieces.shape[1:]
    return pl.pallas_call(
        functools.partial(_steps_kernel, axis, other, n, first, stride, count),
        out_shape=jax.ShapeDtypeStruct(shape, pieces.dtype),
        in_specs=[pl.BlockSpec(memory_space=pl.ANY)],
        out_specs=pl.BlockSpec(memory_space=pl.ANY),
        scratch_shapes=[
            pltpu.SemaphoreType.DMA((count,)),
            pltpu.SemaphoreType.DMA((count,)),
            pltpu.SemaphoreType.DMA(()),
        ],
        compiler_params=pltpu.CompilerParams(collective_id=ident, has_side_effects=True),
        cost_estimate=pl.CostEstimate(
            flops=0, transcendentals=0, bytes_accessed=2 * count * pieces[0].size * pieces.dtype.itemsize
        ),
    )(pieces)


def _gather_steps_kernel(
    axis, other, n, m, src_ref, pieces_ref, out_ref, pieces_out,
    send_sem, recv_sem, own_sem, piece_send, piece_recv, piece_own,
):
    me = lax.axis_index(axis)
    there = lax.axis_index(other)

    def device(k):
        return (k, there) if axis == "row" else (there, k)

    def across(k):
        return (me, k) if axis == "row" else (k, me)

    def gather_copy(step, peer, slot):
        return pltpu.make_async_remote_copy(
            src_ref=src_ref, dst_ref=out_ref.at[slot], send_sem=send_sem.at[step],
            recv_sem=recv_sem.at[step], device_id=device(peer), device_id_type=MESH_ID,
        )

    def piece_copy(step, peer, piece):
        return pltpu.make_async_remote_copy(
            src_ref=pieces_ref.at[piece], dst_ref=pieces_out.at[step], send_sem=piece_send.at[step],
            recv_sem=piece_recv.at[step], device_id=across(peer), device_id_type=MESH_ID,
        )

    barrier = pltpu.get_barrier_semaphore()

    def greet(step, carry):
        pl.semaphore_signal(barrier, inc=1, device_id=device(lax.rem(me + step, n)), device_id_type=MESH_ID)
        return carry

    def greet_across(step, carry):
        pl.semaphore_signal(barrier, inc=1, device_id=across(lax.rem(there + step, m)), device_id_type=MESH_ID)
        return carry

    lax.fori_loop(1, n, greet, 0)
    lax.fori_loop(1, m, greet_across, 0)
    pl.semaphore_wait(barrier, n - 1 + m - 1)
    own = pltpu.make_async_copy(src_ref, out_ref.at[me], own_sem)
    own.start()
    own_piece = pltpu.make_async_copy(pieces_ref.at[there], pieces_out.at[0], piece_own)
    own_piece.start()

    def send(step, carry):
        gather_copy(step, lax.rem(me + step, n), me).start()
        return carry

    def send_across(step, carry):
        peer = lax.rem(there + step, m)
        piece_copy(step, peer, peer).start()
        return carry

    lax.fori_loop(1, m, send_across, 0)
    lax.fori_loop(1, n, send, 0)

    def finish(step, carry):
        gather_copy(step, lax.rem(me + step, n), me).wait_send()
        source = lax.rem(me + n - step, n)
        gather_copy(step, source, source).wait_recv()
        return carry

    def finish_across(step, carry):
        peer = lax.rem(there + step, m)
        piece_copy(step, peer, peer).wait_send()
        source = lax.rem(there + m - step, m)
        piece_copy(step, source, there).wait_recv()
        return carry

    lax.fori_loop(1, n, finish, 0)
    lax.fori_loop(1, m, finish_across, 0)
    own.wait()
    own_piece.wait()


def gather_and_exchange(x, pieces, axis, ident):
    n = lax.axis_size(axis)
    other = "col" if axis == "row" else "row"
    m = lax.axis_size(other)
    shapes = (
        jax.ShapeDtypeStruct((n,) + x.shape, x.dtype),
        jax.ShapeDtypeStruct(pieces.shape, pieces.dtype),
    )
    moved = 2 * n * x.size * x.dtype.itemsize + 2 * pieces.size * pieces.dtype.itemsize
    return pl.pallas_call(
        functools.partial(_gather_steps_kernel, axis, other, n, m),
        out_shape=shapes,
        in_specs=[pl.BlockSpec(memory_space=pl.ANY), pl.BlockSpec(memory_space=pl.ANY)],
        out_specs=(pl.BlockSpec(memory_space=pl.ANY), pl.BlockSpec(memory_space=pl.ANY)),
        scratch_shapes=[
            pltpu.SemaphoreType.DMA((n,)),
            pltpu.SemaphoreType.DMA((n,)),
            pltpu.SemaphoreType.DMA(()),
            pltpu.SemaphoreType.DMA((m,)),
            pltpu.SemaphoreType.DMA((m,)),
            pltpu.SemaphoreType.DMA(()),
        ],
        compiler_params=pltpu.CompilerParams(collective_id=ident, has_side_effects=True),
        cost_estimate=pl.CostEstimate(flops=0, transcendentals=0, bytes_accessed=moved),
    )(x, pieces)


def exchange(x, axis, broadcast, ident):
    n = lax.axis_size(axis)
    other = "col" if axis == "row" else "row"
    shape = (n,) + (x.shape if broadcast else x.shape[1:])
    return pl.pallas_call(
        functools.partial(_exchange_kernel, axis, other, n, broadcast),
        out_shape=jax.ShapeDtypeStruct(shape, x.dtype),
        in_specs=[pl.BlockSpec(memory_space=pl.ANY)],
        out_specs=pl.BlockSpec(memory_space=pl.ANY),
        scratch_shapes=[
            pltpu.SemaphoreType.DMA((n,)),
            pltpu.SemaphoreType.DMA((n,)),
            pltpu.SemaphoreType.DMA(()),
        ],
        compiler_params=pltpu.CompilerParams(collective_id=ident, has_side_effects=True),
        cost_estimate=pl.CostEstimate(
            flops=0, transcendentals=0, bytes_accessed=2 * n * x.size * x.dtype.itemsize
        ),
    )(x)


def _slot_kernel(backward, slots, src_ids, tgt_ids, count_ref, vals_ref, src_ref, out_ref, acc_ref):
    s = pl.program_id(0)

    @pl.when(s == 0)
    def _():
        acc_ref[...] = jnp.zeros_like(acc_ref)

    @pl.when(s < count_ref[0])
    def _():
        block = vals_ref[0]
        segment = src_ref[0]
        if backward:
            dims = (((0,), (0,)), ((), ()))
        else:
            dims = (((1,), (0,)), ((), ()))
        product = lax.dot_general(block, segment, dims, preferred_element_type=jnp.float32)
        target = tgt_ids[s]
        acc_ref[target] = acc_ref[target] + product

    @pl.when(s == slots - 1)
    def _():
        out_ref[...] = acc_ref[...].astype(out_ref.dtype)


def slot_product(tile_values, tile_rows, tile_cols, live_count, source, out_len, backward):
    slots, block_size = tile_values.shape[0], tile_values.shape[1]
    width = source.shape[1]
    n_src = source.shape[0] // block_size
    n_out = out_len // block_size
    panels = source.reshape(n_src, block_size, width)
    if backward:
        src_ids, tgt_ids = tile_rows, tile_cols
    else:
        src_ids, tgt_ids = tile_cols, tile_rows
    src_ids = jnp.clip(src_ids, 0, n_src - 1).astype(jnp.int32)
    tgt_ids = jnp.clip(tgt_ids, 0, n_out - 1).astype(jnp.int32)
    count = jnp.reshape(live_count, (1,)).astype(jnp.int32)
    grid_spec = pltpu.PrefetchScalarGridSpec(
        num_scalar_prefetch=3,
        grid=(slots,),
        in_specs=[
            pl.BlockSpec((1, block_size, block_size), lambda s, src, tgt, cnt: (s, 0, 0)),
            pl.BlockSpec((1, block_size, width), lambda s, src, tgt, cnt: (src[s], 0, 0)),
        ],
        out_specs=pl.BlockSpec((n_out, block_size, width), lambda s, src, tgt, cnt: (0, 0, 0)),
        scratch_shapes=[pltpu.VMEM((n_out, block_size, width), jnp.float32)],
    )
    out = pl.pallas_call(
        functools.partial(_slot_kernel, backward, slots),
        out_shape=jax.ShapeDtypeStruct((n_out, block_size, width), jnp.bfloat16),
        grid_spec=grid_spec,
        compiler_params=pltpu.CompilerParams(
            dimension_semantics=("arbitrary",), vmem_limit_bytes=48 * 1024 * 1024
        ),
        cost_estimate=pl.CostEstimate(
            flops=2 * slots * block_size * block_size * width,
            transcendentals=0,
            bytes_accessed=2 * (slots * block_size * (block_size + width) + n_out * block_size * width),
        ),
    )(src_ids, tgt_ids, count, tile_values, panels)
    return out.reshape(out_len, width)


def gather_rows(x, axis):
    count = lax.axis_size(axis)
    stacked = jnp.broadcast_to(x[None], (count,) + x.shape)
    received = lax.all_to_all(stacked, axis, split_axis=0, concat_axis=0, tiled=True)
    return received.reshape((count * x.shape[0],) + x.shape[1:])


def scatter_sum(x, axis):
    count = lax.axis_size(axis)
    pieces = x.reshape((count, x.shape[0] // count) + x.shape[1:])
    received = lax.all_to_all(pieces, axis, split_axis=0, concat_axis=0, tiled=True)
    return jnp.sum(received.astype(jnp.float32), axis=0)


def pack_grads(local_weight, local_bias):
    pad = jnp.zeros((local_weight.shape[0], 127), jnp.float32)
    return jnp.concatenate([local_weight, local_bias[:, None], pad], axis=1)


def unpack_grads(by_col_then_row, width):
    cols, rows = by_col_then_row.shape[0], by_col_then_row.shape[1]
    whole = by_col_then_row.transpose(1, 0, 2).reshape(cols * rows, -1)
    return whole[:, :width], whole[:, width]


def transposed_product(left, weight):
    return lax.dot_general(
        left, weight, (((1,), (1,)), ((), ())), preferred_element_type=jnp.float32
    ).astype(jnp.bfloat16)


def source_total(received):
    return jnp.sum(received.astype(jnp.float32), axis=0).astype(jnp.bfloat16)


def per_device(
    features, block_values, block_rows, block_cols, block_count, weight, bias, cotangent
):
    tile_values = block_values[0, 0]
    tile_rows = block_rows[0, 0]
    tile_cols = block_cols[0, 0]
    live_count = block_count[0, 0]
    own_nodes = features.shape[0]
    width = features.shape[1]
    row_len = lax.axis_size("col") * own_nodes
    gathered = exchange(features, "row", True, 4).reshape(-1, width)
    col_len = gathered.shape[0]
    partial_value = slot_product(
        tile_values, tile_rows, tile_cols, live_count, gathered, row_len, False
    )
    pieces = partial_value.reshape(lax.axis_size("col"), own_nodes, width)
    received = exchange_steps(pieces, "col", 0, 1, 2)
    aggregate = jnp.sum(received.astype(jnp.float32), axis=0).astype(jnp.bfloat16)
    preact = jnp.dot(aggregate, weight, preferred_element_type=jnp.float32) + bias
    hidden = jax.nn.silu(preact).astype(jnp.bfloat16)
    sigma = jax.nn.sigmoid(preact)
    grad_pre = cotangent.astype(jnp.float32) * sigma * (1.0 + preact * (1.0 - sigma))
    grad_low = grad_pre.astype(jnp.bfloat16)
    local_weight = lax.dot_general(
        aggregate, grad_low, (((0,), (0,)), ((), ())), preferred_element_type=jnp.float32
    )
    local_bias = jnp.sum(grad_pre, axis=0)
    grad_agg = transposed_product(grad_low, weight)
    packed = pack_grads(local_weight, local_bias)
    rows_count = lax.axis_size("row")
    row_pieces = packed.reshape((rows_count, packed.shape[0] // rows_count) + packed.shape[1:])
    grad_stack, by_row_pieces = gather_and_exchange(grad_agg, row_pieces, "col", 0)
    grad_panel = grad_stack.reshape(-1, width)
    by_row = jnp.sum(by_row_pieces, axis=0)
    reduced = scatter_sum(by_row, "col")
    back = slot_product(tile_values, tile_rows, tile_cols, live_count, grad_panel, col_len, True)
    back_low = back.astype(jnp.bfloat16).reshape(col_len // own_nodes, own_nodes, width)
    back_low, reduced = lax.optimization_barrier((back_low, reduced))
    row_part = gather_rows(reduced, "row")
    first_half = exchange_steps(back_low, "row", 1, 2, 1)
    first_half, row_part, back_low = lax.optimization_barrier((first_half, row_part, back_low))
    every = gather_rows(row_part[None], "col")
    second_half = exchange_steps(back_low, "row", 0, 2, 3)
    every_piece = jnp.concatenate([first_half, second_half], axis=0)
    feature_grad = jnp.sum(every_piece.astype(jnp.float32), axis=0).astype(jnp.bfloat16)
    weight_grad, bias_grad = unpack_grads(every, width)
    return (hidden, weight_grad, bias_grad, feature_grad)


def solution(mesh):
    in_specs = (
        P(("col", "row"), None),
        P("row", "col", None, None, None),
        P("row", "col", None),
        P("row", "col", None),
        P("row", "col"),
        P(),
        P(),
        P(("row", "col"), None),
    )
    out_specs = (P(("row", "col"), None), P(), P(), P(("col", "row"), None))
    return jax.shard_map(
        per_device, mesh=mesh, in_specs=in_specs, out_specs=out_specs, check_vma=False
    )
```

```python
import functools

import jax
import jax.numpy as jnp
from jax import lax
from jax.experimental import pallas as pl
from jax.experimental.pallas import tpu as pltpu
from jax.sharding import PartitionSpec as P

MESH_ID = pl.DeviceIdType.MESH


def _exchange_kernel(axis, other, n, broadcast, src_ref, out_ref, send_sem, recv_sem, own_sem):
    me = lax.axis_index(axis)
    there = lax.axis_index(other)

    def device(k):
        return (k, there) if axis == "row" else (there, k)

    def piece(k):
        return src_ref if broadcast else src_ref.at[k]

    barrier = pltpu.get_barrier_semaphore()

    def greet(step, carry):
        peer = lax.rem(me + step, n)
        pl.semaphore_signal(barrier, inc=1, device_id=device(peer), device_id_type=MESH_ID)
        return carry

    lax.fori_loop(1, n, greet, 0)
    pl.semaphore_wait(barrier, n - 1)

    own = pltpu.make_async_copy(piece(me), out_ref.at[me], own_sem)
    own.start()

    def send(step, carry):
        peer = lax.rem(me + step, n)
        pltpu.make_async_remote_copy(
            src_ref=piece(peer), dst_ref=out_ref.at[me], send_sem=send_sem.at[step],
            recv_sem=recv_sem.at[step], device_id=device(peer), device_id_type=MESH_ID,
        ).start()
        return carry

    lax.fori_loop(1, n, send, 0)

    def finish(step, carry):
        peer = lax.rem(me + step, n)
        source = lax.rem(me + n - step, n)
        pltpu.make_async_remote_copy(
            src_ref=piece(peer), dst_ref=out_ref.at[me], send_sem=send_sem.at[step],
            recv_sem=recv_sem.at[step], device_id=device(peer), device_id_type=MESH_ID,
        ).wait_send()
        pltpu.make_async_remote_copy(
            src_ref=piece(source), dst_ref=out_ref.at[source], send_sem=send_sem.at[step],
            recv_sem=recv_sem.at[step], device_id=device(source), device_id_type=MESH_ID,
        ).wait_recv()
        return carry

    lax.fori_loop(1, n, finish, 0)
    own.wait()


def _steps_kernel(axis, other, n, first, stride, count, src_ref, out_ref, send_sem, recv_sem, own_sem):
    me = lax.axis_index(axis)
    there = lax.axis_index(other)
    begin = 1 if first == 0 else 0

    def device(k):
        return (k, there) if axis == "row" else (there, k)

    def copy(slot, peer, piece):
        return pltpu.make_async_remote_copy(
            src_ref=src_ref.at[piece], dst_ref=out_ref.at[slot], send_sem=send_sem.at[slot],
            recv_sem=recv_sem.at[slot], device_id=device(peer), device_id_type=MESH_ID,
        )

    barrier = pltpu.get_barrier_semaphore()

    def greet(slot, carry):
        step = first + stride * slot
        for peer in (lax.rem(me + step, n), lax.rem(me + n - step, n)):
            pl.semaphore_signal(barrier, inc=1, device_id=device(peer), device_id_type=MESH_ID)
        return carry

    lax.fori_loop(begin, count, greet, 0)
    pl.semaphore_wait(barrier, 2 * (count - begin))
    if first == 0:
        own = pltpu.make_async_copy(src_ref.at[me], out_ref.at[0], own_sem)
        own.start()

    def send(slot, carry):
        peer = lax.rem(me + first + stride * slot, n)
        copy(slot, peer, peer).start()
        return carry

    lax.fori_loop(begin, count, send, 0)

    def finish(slot, carry):
        step = first + stride * slot
        peer = lax.rem(me + step, n)
        copy(slot, peer, peer).wait_send()
        source = lax.rem(me + n - step, n)
        copy(slot, source, me).wait_recv()
        return carry

    lax.fori_loop(begin, count, finish, 0)
    if first == 0:
        own.wait()


def exchange_steps(pieces, axis, first, stride, ident):
    n = lax.axis_size(axis)
    count = (n - first + stride - 1) // stride
    other = "col" if axis == "row" else "row"
    shape = (count,) + pieces.shape[1:]
    return pl.pallas_call(
        functools.partial(_steps_kernel, axis, other, n, first, stride, count),
        out_shape=jax.ShapeDtypeStruct(shape, pieces.dtype),
        in_specs=[pl.BlockSpec(memory_space=pl.ANY)],
        out_specs=pl.BlockSpec(memory_space=pl.ANY),
        scratch_shapes=[
            pltpu.SemaphoreType.DMA((count,)),
            pltpu.SemaphoreType.DMA((count,)),
            pltpu.SemaphoreType.DMA(()),
        ],
        compiler_params=pltpu.CompilerParams(collective_id=ident, has_side_effects=True),
        cost_estimate=pl.CostEstimate(
            flops=0, transcendentals=0, bytes_accessed=2 * count * pieces[0].size * pieces.dtype.itemsize
        ),
    )(pieces)


def _gather_steps_kernel(
    axis, other, n, m, src_ref, pieces_ref, out_ref, pieces_out,
    send_sem, recv_sem, own_sem, piece_send, piece_recv, piece_own,
):
    me = lax.axis_index(axis)
    there = lax.axis_index(other)

    def device(k):
        return (k, there) if axis == "row" else (there, k)

    def across(k):
        return (me, k) if axis == "row" else (k, me)

    def gather_copy(step, peer, slot):
        return pltpu.make_async_remote_copy(
            src_ref=src_ref, dst_ref=out_ref.at[slot], send_sem=send_sem.at[step],
            recv_sem=recv_sem.at[step], device_id=device(peer), device_id_type=MESH_ID,
        )

    def piece_copy(step, peer, piece):
        return pltpu.make_async_remote_copy(
            src_ref=pieces_ref.at[piece], dst_ref=pieces_out.at[step], send_sem=piece_send.at[step],
            recv_sem=piece_recv.at[step], device_id=across(peer), device_id_type=MESH_ID,
        )

    barrier = pltpu.get_barrier_semaphore()

    def greet(step, carry):
        pl.semaphore_signal(barrier, inc=1, device_id=device(lax.rem(me + step, n)), device_id_type=MESH_ID)
        return carry

    def greet_across(step, carry):
        pl.semaphore_signal(barrier, inc=1, device_id=across(lax.rem(there + step, m)), device_id_type=MESH_ID)
        return carry

    lax.fori_loop(1, n, greet, 0)
    lax.fori_loop(1, m, greet_across, 0)
    pl.semaphore_wait(barrier, n - 1 + m - 1)
    own = pltpu.make_async_copy(src_ref, out_ref.at[me], own_sem)
    own.start()
    own_piece = pltpu.make_async_copy(pieces_ref.at[there], pieces_out.at[0], piece_own)
    own_piece.start()

    def send(step, carry):
        gather_copy(step, lax.rem(me + step, n), me).start()
        return carry

    def send_across(step, carry):
        peer = lax.rem(there + step, m)
        piece_copy(step, peer, peer).start()
        return carry

    lax.fori_loop(1, m, send_across, 0)
    lax.fori_loop(1, n, send, 0)

    def finish(step, carry):
        gather_copy(step, lax.rem(me + step, n), me).wait_send()
        source = lax.rem(me + n - step, n)
        gather_copy(step, source, source).wait_recv()
        return carry

    def finish_across(step, carry):
        peer = lax.rem(there + step, m)
        piece_copy(step, peer, peer).wait_send()
        source = lax.rem(there + m - step, m)
        piece_copy(step, source, there).wait_recv()
        return carry

    lax.fori_loop(1, n, finish, 0)
    lax.fori_loop(1, m, finish_across, 0)
    own.wait()
    own_piece.wait()


def gather_and_exchange(x, pieces, axis, ident):
    n = lax.axis_size(axis)
    other = "col" if axis == "row" else "row"
    m = lax.axis_size(other)
    shapes = (
        jax.ShapeDtypeStruct((n,) + x.shape, x.dtype),
        jax.ShapeDtypeStruct(pieces.shape, pieces.dtype),
    )
    moved = 2 * n * x.size * x.dtype.itemsize + 2 * pieces.size * pieces.dtype.itemsize
    return pl.pallas_call(
        functools.partial(_gather_steps_kernel, axis, other, n, m),
        out_shape=shapes,
        in_specs=[pl.BlockSpec(memory_space=pl.ANY), pl.BlockSpec(memory_space=pl.ANY)],
        out_specs=(pl.BlockSpec(memory_space=pl.ANY), pl.BlockSpec(memory_space=pl.ANY)),
        scratch_shapes=[
            pltpu.SemaphoreType.DMA((n,)),
            pltpu.SemaphoreType.DMA((n,)),
            pltpu.SemaphoreType.DMA(()),
            pltpu.SemaphoreType.DMA((m,)),
            pltpu.SemaphoreType.DMA((m,)),
            pltpu.SemaphoreType.DMA(()),
        ],
        compiler_params=pltpu.CompilerParams(collective_id=ident, has_side_effects=True),
        cost_estimate=pl.CostEstimate(flops=0, transcendentals=0, bytes_accessed=moved),
    )(x, pieces)


def _back_kernel(
    n, m, src_ref, w_ref, out_ref, row_buf, col_buf,
    send_sem, recv_sem, own_sem, a_send, a_recv, a_own, b_send, b_recv, b_own,
):
    me = lax.axis_index("row")
    there = lax.axis_index("col")

    def along(k):
        return (k, there)

    def across(k):
        return (me, k)

    def main_copy(step, peer, piece):
        return pltpu.make_async_remote_copy(
            src_ref=src_ref.at[piece], dst_ref=out_ref.at[step], send_sem=send_sem.at[step],
            recv_sem=recv_sem.at[step], device_id=along(peer), device_id_type=MESH_ID,
        )

    def row_copy(step, peer, slot):
        return pltpu.make_async_remote_copy(
            src_ref=w_ref, dst_ref=row_buf.at[slot], send_sem=a_send.at[step],
            recv_sem=a_recv.at[step], device_id=along(peer), device_id_type=MESH_ID,
        )

    def col_copy(step, peer, slot):
        return pltpu.make_async_remote_copy(
            src_ref=row_buf, dst_ref=col_buf.at[slot], send_sem=b_send.at[step],
            recv_sem=b_recv.at[step], device_id=across(peer), device_id_type=MESH_ID,
        )

    barrier = pltpu.get_barrier_semaphore()

    def greet(step, carry):
        pl.semaphore_signal(barrier, inc=1, device_id=along(lax.rem(me + step, n)), device_id_type=MESH_ID)
        return carry

    def greet_across(step, carry):
        pl.semaphore_signal(barrier, inc=1, device_id=across(lax.rem(there + step, m)), device_id_type=MESH_ID)
        return carry

    lax.fori_loop(1, n, greet, 0)
    lax.fori_loop(1, m, greet_across, 0)
    pl.semaphore_wait(barrier, n - 1 + m - 1)
    own = pltpu.make_async_copy(src_ref.at[me], out_ref.at[0], own_sem)
    own.start()
    own_row = pltpu.make_async_copy(w_ref, row_buf.at[me], a_own)
    own_row.start()

    def send_row(step, carry):
        row_copy(step, lax.rem(me + step, n), me).start()
        return carry

    def send_main(step, carry):
        peer = lax.rem(me + step, n)
        main_copy(step, peer, peer).start()
        return carry

    lax.fori_loop(1, n, send_row, 0)
    lax.fori_loop(1, n, send_main, 0)

    def finish_row(step, carry):
        row_copy(step, lax.rem(me + step, n), me).wait_send()
        source = lax.rem(me + n - step, n)
        row_copy(step, source, source).wait_recv()
        return carry

    lax.fori_loop(1, n, finish_row, 0)
    own_row.wait()
    own_col = pltpu.make_async_copy(row_buf, col_buf.at[there], b_own)
    own_col.start()

    def send_col(step, carry):
        col_copy(step, lax.rem(there + step, m), there).start()
        return carry

    lax.fori_loop(1, m, send_col, 0)

    def finish_main(step, carry):
        peer = lax.rem(me + step, n)
        main_copy(step, peer, peer).wait_send()
        source = lax.rem(me + n - step, n)
        main_copy(step, source, me).wait_recv()
        return carry

    lax.fori_loop(1, n, finish_main, 0)

    def finish_col(step, carry):
        col_copy(step, lax.rem(there + step, m), there).wait_send()
        source = lax.rem(there + m - step, m)
        col_copy(step, source, source).wait_recv()
        return carry

    lax.fori_loop(1, m, finish_col, 0)
    own_col.wait()
    own.wait()


def back_exchange(pieces, row, ident):
    n = lax.axis_size("row")
    m = lax.axis_size("col")
    shapes = (
        jax.ShapeDtypeStruct(pieces.shape, pieces.dtype),
        jax.ShapeDtypeStruct((n,) + row.shape, row.dtype),
        jax.ShapeDtypeStruct((m, n) + row.shape, row.dtype),
    )
    moved = 2 * pieces.size * pieces.dtype.itemsize + 2 * m * n * row.size * row.dtype.itemsize
    return pl.pallas_call(
        functools.partial(_back_kernel, n, m),
        out_shape=shapes,
        in_specs=[pl.BlockSpec(memory_space=pl.ANY), pl.BlockSpec(memory_space=pl.ANY)],
        out_specs=tuple(pl.BlockSpec(memory_space=pl.ANY) for _ in range(3)),
        scratch_shapes=[
            pltpu.SemaphoreType.DMA((n,)),
            pltpu.SemaphoreType.DMA((n,)),
            pltpu.SemaphoreType.DMA(()),
            pltpu.SemaphoreType.DMA((n,)),
            pltpu.SemaphoreType.DMA((n,)),
            pltpu.SemaphoreType.DMA(()),
            pltpu.SemaphoreType.DMA((m,)),
            pltpu.SemaphoreType.DMA((m,)),
            pltpu.SemaphoreType.DMA(()),
        ],
        compiler_params=pltpu.CompilerParams(collective_id=ident, has_side_effects=True),
        cost_estimate=pl.CostEstimate(flops=0, transcendentals=0, bytes_accessed=moved),
    )(pieces, row)


def exchange(x, axis, broadcast, ident):
    n = lax.axis_size(axis)
    other = "col" if axis == "row" else "row"
    shape = (n,) + (x.shape if broadcast else x.shape[1:])
    return pl.pallas_call(
        functools.partial(_exchange_kernel, axis, other, n, broadcast),
        out_shape=jax.ShapeDtypeStruct(shape, x.dtype),
        in_specs=[pl.BlockSpec(memory_space=pl.ANY)],
        out_specs=pl.BlockSpec(memory_space=pl.ANY),
        scratch_shapes=[
            pltpu.SemaphoreType.DMA((n,)),
            pltpu.SemaphoreType.DMA((n,)),
            pltpu.SemaphoreType.DMA(()),
        ],
        compiler_params=pltpu.CompilerParams(collective_id=ident, has_side_effects=True),
        cost_estimate=pl.CostEstimate(
            flops=0, transcendentals=0, bytes_accessed=2 * n * x.size * x.dtype.itemsize
        ),
    )(x)


def _slot_kernel(backward, slots, src_ids, tgt_ids, count_ref, vals_ref, src_ref, out_ref, acc_ref):
    s = pl.program_id(0)

    @pl.when(s == 0)
    def _():
        acc_ref[...] = jnp.zeros_like(acc_ref)

    @pl.when(s < count_ref[0])
    def _():
        block = vals_ref[0]
        segment = src_ref[0]
        if backward:
            dims = (((0,), (0,)), ((), ()))
        else:
            dims = (((1,), (0,)), ((), ()))
        product = lax.dot_general(block, segment, dims, preferred_element_type=jnp.float32)
        target = tgt_ids[s]
        acc_ref[target] = acc_ref[target] + product

    @pl.when(s == slots - 1)
    def _():
        out_ref[...] = acc_ref[...].astype(out_ref.dtype)


def slot_product(tile_values, tile_rows, tile_cols, live_count, source, out_len, backward):
    slots, block_size = tile_values.shape[0], tile_values.shape[1]
    width = source.shape[1]
    n_src = source.shape[0] // block_size
    n_out = out_len // block_size
    panels = source.reshape(n_src, block_size, width)
    if backward:
        src_ids, tgt_ids = tile_rows, tile_cols
    else:
        src_ids, tgt_ids = tile_cols, tile_rows
    src_ids = jnp.clip(src_ids, 0, n_src - 1).astype(jnp.int32)
    tgt_ids = jnp.clip(tgt_ids, 0, n_out - 1).astype(jnp.int32)
    count = jnp.reshape(live_count, (1,)).astype(jnp.int32)
    grid_spec = pltpu.PrefetchScalarGridSpec(
        num_scalar_prefetch=3,
        grid=(slots,),
        in_specs=[
            pl.BlockSpec((1, block_size, block_size), lambda s, src, tgt, cnt: (s, 0, 0)),
            pl.BlockSpec((1, block_size, width), lambda s, src, tgt, cnt: (src[s], 0, 0)),
        ],
        out_specs=pl.BlockSpec((n_out, block_size, width), lambda s, src, tgt, cnt: (0, 0, 0)),
        scratch_shapes=[pltpu.VMEM((n_out, block_size, width), jnp.float32)],
    )
    out = pl.pallas_call(
        functools.partial(_slot_kernel, backward, slots),
        out_shape=jax.ShapeDtypeStruct((n_out, block_size, width), jnp.bfloat16),
        grid_spec=grid_spec,
        compiler_params=pltpu.CompilerParams(
            dimension_semantics=("arbitrary",), vmem_limit_bytes=48 * 1024 * 1024
        ),
        cost_estimate=pl.CostEstimate(
            flops=2 * slots * block_size * block_size * width,
            transcendentals=0,
            bytes_accessed=2 * (slots * block_size * (block_size + width) + n_out * block_size * width),
        ),
    )(src_ids, tgt_ids, count, tile_values, panels)
    return out.reshape(out_len, width)


def gather_rows(x, axis):
    count = lax.axis_size(axis)
    stacked = jnp.broadcast_to(x[None], (count,) + x.shape)
    received = lax.all_to_all(stacked, axis, split_axis=0, concat_axis=0, tiled=True)
    return received.reshape((count * x.shape[0],) + x.shape[1:])


def scatter_sum(x, axis):
    count = lax.axis_size(axis)
    pieces = x.reshape((count, x.shape[0] // count) + x.shape[1:])
    received = lax.all_to_all(pieces, axis, split_axis=0, concat_axis=0, tiled=True)
    return jnp.sum(received.astype(jnp.float32), axis=0)


def pack_grads(local_weight, local_bias):
    pad = jnp.zeros((local_weight.shape[0], 127), jnp.float32)
    return jnp.concatenate([local_weight, local_bias[:, None], pad], axis=1)


def unpack_grads(by_col_then_row, width):
    cols, rows = by_col_then_row.shape[0], by_col_then_row.shape[1]
    whole = by_col_then_row.transpose(1, 0, 2).reshape(cols * rows, -1)
    return whole[:, :width], whole[:, width]


def transposed_product(left, weight):
    return lax.dot_general(
        left, weight, (((1,), (1,)), ((), ())), preferred_element_type=jnp.float32
    ).astype(jnp.bfloat16)


def source_total(received):
    return jnp.sum(received.astype(jnp.float32), axis=0).astype(jnp.bfloat16)


def per_device(
    features, block_values, block_rows, block_cols, block_count, weight, bias, cotangent
):
    tile_values = block_values[0, 0]
    tile_rows = block_rows[0, 0]
    tile_cols = block_cols[0, 0]
    live_count = block_count[0, 0]
    own_nodes = features.shape[0]
    width = features.shape[1]
    row_len = lax.axis_size("col") * own_nodes
    gathered = exchange(features, "row", True, 4).reshape(-1, width)
    col_len = gathered.shape[0]
    partial_value = slot_product(
        tile_values, tile_rows, tile_cols, live_count, gathered, row_len, False
    )
    pieces = partial_value.reshape(lax.axis_size("col"), own_nodes, width)
    received = exchange_steps(pieces, "col", 0, 1, 2)
    aggregate = jnp.sum(received.astype(jnp.float32), axis=0).astype(jnp.bfloat16)
    preact = jnp.dot(aggregate, weight, preferred_element_type=jnp.float32) + bias
    hidden = jax.nn.silu(preact).astype(jnp.bfloat16)
    sigma = jax.nn.sigmoid(preact)
    grad_pre = cotangent.astype(jnp.float32) * sigma * (1.0 + preact * (1.0 - sigma))
    grad_low = grad_pre.astype(jnp.bfloat16)
    local_weight = lax.dot_general(
        aggregate, grad_low, (((0,), (0,)), ((), ())), preferred_element_type=jnp.float32
    )
    local_bias = jnp.sum(grad_pre, axis=0)
    grad_agg = transposed_product(grad_low, weight)
    packed = pack_grads(local_weight, local_bias)
    rows_count = lax.axis_size("row")
    row_pieces = packed.reshape((rows_count, packed.shape[0] // rows_count) + packed.shape[1:])
    grad_stack, by_row_pieces = gather_and_exchange(grad_agg, row_pieces, "col", 0)
    grad_panel = grad_stack.reshape(-1, width)
    by_row = jnp.sum(by_row_pieces, axis=0)
    reduced = scatter_sum(by_row, "col")
    back = slot_product(tile_values, tile_rows, tile_cols, live_count, grad_panel, col_len, True)
    back_low = back.astype(jnp.bfloat16).reshape(col_len // own_nodes, own_nodes, width)
    received, _, gathered_rows = back_exchange(back_low, reduced, 1)
    every = gathered_rows.reshape(gathered_rows.shape[0], gathered_rows.shape[1], -1)
    feature_grad = jnp.sum(received.astype(jnp.float32), axis=0).astype(jnp.bfloat16)
    weight_grad, bias_grad = unpack_grads(every, width)
    return (hidden, weight_grad, bias_grad, feature_grad)


def solution(mesh):
    in_specs = (
        P(("col", "row"), None),
        P("row", "col", None, None, None),
        P("row", "col", None),
        P("row", "col", None),
        P("row", "col"),
        P(),
        P(),
        P(("row", "col"), None),
    )
    out_specs = (P(("row", "col"), None), P(), P(), P(("col", "row"), None))
    return jax.shard_map(
        per_device, mesh=mesh, in_specs=in_specs, out_specs=out_specs, check_vma=False
    )
```

```python
import functools

import jax
import jax.numpy as jnp
from jax import lax
from jax.experimental import pallas as pl
from jax.experimental.pallas import tpu as pltpu
from jax.sharding import PartitionSpec as P

MESH_ID = pl.DeviceIdType.MESH


def _exchange_kernel(axis, other, n, broadcast, src_ref, out_ref, send_sem, recv_sem, own_sem):
    me = lax.axis_index(axis)
    there = lax.axis_index(other)

    def device(k):
        return (k, there) if axis == "row" else (there, k)

    def piece(k):
        return src_ref if broadcast else src_ref.at[k]

    barrier = pltpu.get_barrier_semaphore()

    def greet(step, carry):
        peer = lax.rem(me + step, n)
        pl.semaphore_signal(barrier, inc=1, device_id=device(peer), device_id_type=MESH_ID)
        return carry

    lax.fori_loop(1, n, greet, 0)
    pl.semaphore_wait(barrier, n - 1)

    own = pltpu.make_async_copy(piece(me), out_ref.at[me], own_sem)
    own.start()

    def send(step, carry):
        peer = lax.rem(me + step, n)
        pltpu.make_async_remote_copy(
            src_ref=piece(peer), dst_ref=out_ref.at[me], send_sem=send_sem.at[step],
            recv_sem=recv_sem.at[step], device_id=device(peer), device_id_type=MESH_ID,
        ).start()
        return carry

    lax.fori_loop(1, n, send, 0)

    def finish(step, carry):
        peer = lax.rem(me + step, n)
        source = lax.rem(me + n - step, n)
        pltpu.make_async_remote_copy(
            src_ref=piece(peer), dst_ref=out_ref.at[me], send_sem=send_sem.at[step],
            recv_sem=recv_sem.at[step], device_id=device(peer), device_id_type=MESH_ID,
        ).wait_send()
        pltpu.make_async_remote_copy(
            src_ref=piece(source), dst_ref=out_ref.at[source], send_sem=send_sem.at[step],
            recv_sem=recv_sem.at[step], device_id=device(source), device_id_type=MESH_ID,
        ).wait_recv()
        return carry

    lax.fori_loop(1, n, finish, 0)
    own.wait()


def _steps_kernel(axis, other, n, first, stride, count, src_ref, out_ref, send_sem, recv_sem, own_sem):
    me = lax.axis_index(axis)
    there = lax.axis_index(other)
    begin = 1 if first == 0 else 0

    def device(k):
        return (k, there) if axis == "row" else (there, k)

    def copy(slot, peer, piece):
        return pltpu.make_async_remote_copy(
            src_ref=src_ref.at[piece], dst_ref=out_ref.at[slot], send_sem=send_sem.at[slot],
            recv_sem=recv_sem.at[slot], device_id=device(peer), device_id_type=MESH_ID,
        )

    barrier = pltpu.get_barrier_semaphore()

    def greet(slot, carry):
        step = first + stride * slot
        for peer in (lax.rem(me + step, n), lax.rem(me + n - step, n)):
            pl.semaphore_signal(barrier, inc=1, device_id=device(peer), device_id_type=MESH_ID)
        return carry

    lax.fori_loop(begin, count, greet, 0)
    pl.semaphore_wait(barrier, 2 * (count - begin))
    if first == 0:
        own = pltpu.make_async_copy(src_ref.at[me], out_ref.at[0], own_sem)
        own.start()

    def send(slot, carry):
        peer = lax.rem(me + first + stride * slot, n)
        copy(slot, peer, peer).start()
        return carry

    lax.fori_loop(begin, count, send, 0)

    def finish(slot, carry):
        step = first + stride * slot
        peer = lax.rem(me + step, n)
        copy(slot, peer, peer).wait_send()
        source = lax.rem(me + n - step, n)
        copy(slot, source, me).wait_recv()
        return carry

    lax.fori_loop(begin, count, finish, 0)
    if first == 0:
        own.wait()


def exchange_steps(pieces, axis, first, stride, ident):
    n = lax.axis_size(axis)
    count = (n - first + stride - 1) // stride
    other = "col" if axis == "row" else "row"
    shape = (count,) + pieces.shape[1:]
    return pl.pallas_call(
        functools.partial(_steps_kernel, axis, other, n, first, stride, count),
        out_shape=jax.ShapeDtypeStruct(shape, pieces.dtype),
        in_specs=[pl.BlockSpec(memory_space=pl.ANY)],
        out_specs=pl.BlockSpec(memory_space=pl.ANY),
        scratch_shapes=[
            pltpu.SemaphoreType.DMA((count,)),
            pltpu.SemaphoreType.DMA((count,)),
            pltpu.SemaphoreType.DMA(()),
        ],
        compiler_params=pltpu.CompilerParams(collective_id=ident, has_side_effects=True),
        cost_estimate=pl.CostEstimate(
            flops=0, transcendentals=0, bytes_accessed=2 * count * pieces[0].size * pieces.dtype.itemsize
        ),
    )(pieces)


def _gather_steps_kernel(
    axis, other, n, m, src_ref, pieces_ref, out_ref, pieces_out,
    send_sem, recv_sem, own_sem, piece_send, piece_recv, piece_own,
):
    me = lax.axis_index(axis)
    there = lax.axis_index(other)

    def device(k):
        return (k, there) if axis == "row" else (there, k)

    def across(k):
        return (me, k) if axis == "row" else (k, me)

    def gather_copy(step, peer, slot):
        return pltpu.make_async_remote_copy(
            src_ref=src_ref, dst_ref=out_ref.at[slot], send_sem=send_sem.at[step],
            recv_sem=recv_sem.at[step], device_id=device(peer), device_id_type=MESH_ID,
        )

    def piece_copy(step, peer, piece):
        return pltpu.make_async_remote_copy(
            src_ref=pieces_ref.at[piece], dst_ref=pieces_out.at[step], send_sem=piece_send.at[step],
            recv_sem=piece_recv.at[step], device_id=across(peer), device_id_type=MESH_ID,
        )

    barrier = pltpu.get_barrier_semaphore()

    def greet(step, carry):
        pl.semaphore_signal(barrier, inc=1, device_id=device(lax.rem(me + step, n)), device_id_type=MESH_ID)
        return carry

    def greet_across(step, carry):
        pl.semaphore_signal(barrier, inc=1, device_id=across(lax.rem(there + step, m)), device_id_type=MESH_ID)
        return carry

    lax.fori_loop(1, n, greet, 0)
    lax.fori_loop(1, m, greet_across, 0)
    pl.semaphore_wait(barrier, n - 1 + m - 1)
    own = pltpu.make_async_copy(src_ref, out_ref.at[me], own_sem)
    own.start()
    own_piece = pltpu.make_async_copy(pieces_ref.at[there], pieces_out.at[0], piece_own)
    own_piece.start()

    def send(step, carry):
        gather_copy(step, lax.rem(me + step, n), me).start()
        return carry

    def send_across(step, carry):
        peer = lax.rem(there + step, m)
        piece_copy(step, peer, peer).start()
        return carry

    lax.fori_loop(1, m, send_across, 0)
    lax.fori_loop(1, n, send, 0)

    def finish(step, carry):
        gather_copy(step, lax.rem(me + step, n), me).wait_send()
        source = lax.rem(me + n - step, n)
        gather_copy(step, source, source).wait_recv()
        return carry

    def finish_across(step, carry):
        peer = lax.rem(there + step, m)
        piece_copy(step, peer, peer).wait_send()
        source = lax.rem(there + m - step, m)
        piece_copy(step, source, there).wait_recv()
        return carry

    lax.fori_loop(1, n, finish, 0)
    lax.fori_loop(1, m, finish_across, 0)
    own.wait()
    own_piece.wait()


def gather_and_exchange(x, pieces, axis, ident):
    n = lax.axis_size(axis)
    other = "col" if axis == "row" else "row"
    m = lax.axis_size(other)
    shapes = (
        jax.ShapeDtypeStruct((n,) + x.shape, x.dtype),
        jax.ShapeDtypeStruct(pieces.shape, pieces.dtype),
    )
    moved = 2 * n * x.size * x.dtype.itemsize + 2 * pieces.size * pieces.dtype.itemsize
    return pl.pallas_call(
        functools.partial(_gather_steps_kernel, axis, other, n, m),
        out_shape=shapes,
        in_specs=[pl.BlockSpec(memory_space=pl.ANY), pl.BlockSpec(memory_space=pl.ANY)],
        out_specs=(pl.BlockSpec(memory_space=pl.ANY), pl.BlockSpec(memory_space=pl.ANY)),
        scratch_shapes=[
            pltpu.SemaphoreType.DMA((n,)),
            pltpu.SemaphoreType.DMA((n,)),
            pltpu.SemaphoreType.DMA(()),
            pltpu.SemaphoreType.DMA((m,)),
            pltpu.SemaphoreType.DMA((m,)),
            pltpu.SemaphoreType.DMA(()),
        ],
        compiler_params=pltpu.CompilerParams(collective_id=ident, has_side_effects=True),
        cost_estimate=pl.CostEstimate(flops=0, transcendentals=0, bytes_accessed=moved),
    )(x, pieces)


def _back_kernel(
    n, m, src_ref, part_ref, out_ref, row_buf, col_buf,
    send_sem, recv_sem, own_sem, a_send, a_recv, a_own, b_send, b_recv, b_own,
    c_send, c_recv, c_own, part_buf, w_ref,
):
    me = lax.axis_index("row")
    there = lax.axis_index("col")

    def along(k):
        return (k, there)

    def across(k):
        return (me, k)

    def main_copy(step, peer, piece):
        return pltpu.make_async_remote_copy(
            src_ref=src_ref.at[piece], dst_ref=out_ref.at[step], send_sem=send_sem.at[step],
            recv_sem=recv_sem.at[step], device_id=along(peer), device_id_type=MESH_ID,
        )

    def row_copy(step, peer, slot):
        return pltpu.make_async_remote_copy(
            src_ref=w_ref, dst_ref=row_buf.at[slot], send_sem=a_send.at[step],
            recv_sem=a_recv.at[step], device_id=along(peer), device_id_type=MESH_ID,
        )

    def col_copy(step, peer, slot):
        return pltpu.make_async_remote_copy(
            src_ref=row_buf, dst_ref=col_buf.at[slot], send_sem=b_send.at[step],
            recv_sem=b_recv.at[step], device_id=across(peer), device_id_type=MESH_ID,
        )

    def part_copy(step, peer):
        return pltpu.make_async_remote_copy(
            src_ref=part_ref.at[peer], dst_ref=part_buf.at[step], send_sem=c_send.at[step],
            recv_sem=c_recv.at[step], device_id=across(peer), device_id_type=MESH_ID,
        )

    barrier = pltpu.get_barrier_semaphore()

    def greet(step, carry):
        pl.semaphore_signal(barrier, inc=1, device_id=along(lax.rem(me + step, n)), device_id_type=MESH_ID)
        return carry

    def greet_across(step, carry):
        pl.semaphore_signal(barrier, inc=1, device_id=across(lax.rem(there + step, m)), device_id_type=MESH_ID)
        return carry

    lax.fori_loop(1, n, greet, 0)
    lax.fori_loop(1, m, greet_across, 0)
    pl.semaphore_wait(barrier, n - 1 + m - 1)
    own = pltpu.make_async_copy(src_ref.at[me], out_ref.at[0], own_sem)
    own.start()
    own_part = pltpu.make_async_copy(part_ref.at[there], part_buf.at[0], c_own)
    own_part.start()

    def send_part(step, carry):
        part_copy(step, lax.rem(there + step, m)).start()
        return carry

    def send_main(step, carry):
        peer = lax.rem(me + step, n)
        main_copy(step, peer, peer).start()
        return carry

    lax.fori_loop(1, m, send_part, 0)
    lax.fori_loop(1, n, send_main, 0)

    def finish_part(step, carry):
        part_copy(step, lax.rem(there + step, m)).wait_send()
        part_copy(step, lax.rem(there + m - step, m)).wait_recv()
        return carry

    lax.fori_loop(1, m, finish_part, 0)
    own_part.wait()
    w_ref[...] = jnp.sum(part_buf[...], axis=0)
    own_row = pltpu.make_async_copy(w_ref, row_buf.at[me], a_own)
    own_row.start()

    def send_row(step, carry):
        row_copy(step, lax.rem(me + step, n), me).start()
        return carry

    lax.fori_loop(1, n, send_row, 0)

    def finish_row(step, carry):
        row_copy(step, lax.rem(me + step, n), me).wait_send()
        source = lax.rem(me + n - step, n)
        row_copy(step, source, source).wait_recv()
        return carry

    lax.fori_loop(1, n, finish_row, 0)
    own_row.wait()
    own_col = pltpu.make_async_copy(row_buf, col_buf.at[there], b_own)
    own_col.start()

    def send_col(step, carry):
        col_copy(step, lax.rem(there + step, m), there).start()
        return carry

    lax.fori_loop(1, m, send_col, 0)

    def finish_main(step, carry):
        peer = lax.rem(me + step, n)
        main_copy(step, peer, peer).wait_send()
        source = lax.rem(me + n - step, n)
        main_copy(step, source, me).wait_recv()
        return carry

    lax.fori_loop(1, n, finish_main, 0)

    def finish_col(step, carry):
        col_copy(step, lax.rem(there + step, m), there).wait_send()
        source = lax.rem(there + m - step, m)
        col_copy(step, source, source).wait_recv()
        return carry

    lax.fori_loop(1, m, finish_col, 0)
    own_col.wait()
    own.wait()


def back_exchange(pieces, parts, ident):
    n = lax.axis_size("row")
    m = lax.axis_size("col")
    row = parts[0]
    shapes = (
        jax.ShapeDtypeStruct(pieces.shape, pieces.dtype),
        jax.ShapeDtypeStruct((n,) + row.shape, row.dtype),
        jax.ShapeDtypeStruct((m, n) + row.shape, row.dtype),
    )
    moved = 2 * pieces.size * pieces.dtype.itemsize + 2 * m * n * row.size * row.dtype.itemsize
    return pl.pallas_call(
        functools.partial(_back_kernel, n, m),
        out_shape=shapes,
        in_specs=[pl.BlockSpec(memory_space=pl.ANY), pl.BlockSpec(memory_space=pl.ANY)],
        out_specs=tuple(pl.BlockSpec(memory_space=pl.ANY) for _ in range(3)),
        scratch_shapes=[
            pltpu.SemaphoreType.DMA((n,)),
            pltpu.SemaphoreType.DMA((n,)),
            pltpu.SemaphoreType.DMA(()),
            pltpu.SemaphoreType.DMA((n,)),
            pltpu.SemaphoreType.DMA((n,)),
            pltpu.SemaphoreType.DMA(()),
            pltpu.SemaphoreType.DMA((m,)),
            pltpu.SemaphoreType.DMA((m,)),
            pltpu.SemaphoreType.DMA(()),
            pltpu.SemaphoreType.DMA((m,)),
            pltpu.SemaphoreType.DMA((m,)),
            pltpu.SemaphoreType.DMA(()),
            pltpu.VMEM(parts.shape, parts.dtype),
            pltpu.VMEM(row.shape, row.dtype),
        ],
        compiler_params=pltpu.CompilerParams(collective_id=ident, has_side_effects=True),
        cost_estimate=pl.CostEstimate(flops=0, transcendentals=0, bytes_accessed=moved),
    )(pieces, parts)


def exchange(x, axis, broadcast, ident):
    n = lax.axis_size(axis)
    other = "col" if axis == "row" else "row"
    shape = (n,) + (x.shape if broadcast else x.shape[1:])
    return pl.pallas_call(
        functools.partial(_exchange_kernel, axis, other, n, broadcast),
        out_shape=jax.ShapeDtypeStruct(shape, x.dtype),
        in_specs=[pl.BlockSpec(memory_space=pl.ANY)],
        out_specs=pl.BlockSpec(memory_space=pl.ANY),
        scratch_shapes=[
            pltpu.SemaphoreType.DMA((n,)),
            pltpu.SemaphoreType.DMA((n,)),
            pltpu.SemaphoreType.DMA(()),
        ],
        compiler_params=pltpu.CompilerParams(collective_id=ident, has_side_effects=True),
        cost_estimate=pl.CostEstimate(
            flops=0, transcendentals=0, bytes_accessed=2 * n * x.size * x.dtype.itemsize
        ),
    )(x)


def _slot_kernel(backward, slots, src_ids, tgt_ids, count_ref, vals_ref, src_ref, out_ref, acc_ref):
    s = pl.program_id(0)

    @pl.when(s == 0)
    def _():
        acc_ref[...] = jnp.zeros_like(acc_ref)

    @pl.when(s < count_ref[0])
    def _():
        block = vals_ref[0]
        segment = src_ref[0]
        if backward:
            dims = (((0,), (0,)), ((), ()))
        else:
            dims = (((1,), (0,)), ((), ()))
        product = lax.dot_general(block, segment, dims, preferred_element_type=jnp.float32)
        target = tgt_ids[s]
        acc_ref[target] = acc_ref[target] + product

    @pl.when(s == slots - 1)
    def _():
        out_ref[...] = acc_ref[...].astype(out_ref.dtype)


def slot_product(tile_values, tile_rows, tile_cols, live_count, source, out_len, backward):
    slots, block_size = tile_values.shape[0], tile_values.shape[1]
    width = source.shape[1]
    n_src = source.shape[0] // block_size
    n_out = out_len // block_size
    panels = source.reshape(n_src, block_size, width)
    if backward:
        src_ids, tgt_ids = tile_rows, tile_cols
    else:
        src_ids, tgt_ids = tile_cols, tile_rows
    src_ids = jnp.clip(src_ids, 0, n_src - 1).astype(jnp.int32)
    tgt_ids = jnp.clip(tgt_ids, 0, n_out - 1).astype(jnp.int32)
    count = jnp.reshape(live_count, (1,)).astype(jnp.int32)
    grid_spec = pltpu.PrefetchScalarGridSpec(
        num_scalar_prefetch=3,
        grid=(slots,),
        in_specs=[
            pl.BlockSpec((1, block_size, block_size), lambda s, src, tgt, cnt: (s, 0, 0)),
            pl.BlockSpec((1, block_size, width), lambda s, src, tgt, cnt: (src[s], 0, 0)),
        ],
        out_specs=pl.BlockSpec((n_out, block_size, width), lambda s, src, tgt, cnt: (0, 0, 0)),
        scratch_shapes=[pltpu.VMEM((n_out, block_size, width), jnp.float32)],
    )
    out = pl.pallas_call(
        functools.partial(_slot_kernel, backward, slots),
        out_shape=jax.ShapeDtypeStruct((n_out, block_size, width), jnp.bfloat16),
        grid_spec=grid_spec,
        compiler_params=pltpu.CompilerParams(
            dimension_semantics=("arbitrary",), vmem_limit_bytes=48 * 1024 * 1024
        ),
        cost_estimate=pl.CostEstimate(
            flops=2 * slots * block_size * block_size * width,
            transcendentals=0,
            bytes_accessed=2 * (slots * block_size * (block_size + width) + n_out * block_size * width),
        ),
    )(src_ids, tgt_ids, count, tile_values, panels)
    return out.reshape(out_len, width)


def gather_rows(x, axis):
    count = lax.axis_size(axis)
    stacked = jnp.broadcast_to(x[None], (count,) + x.shape)
    received = lax.all_to_all(stacked, axis, split_axis=0, concat_axis=0, tiled=True)
    return received.reshape((count * x.shape[0],) + x.shape[1:])


def scatter_sum(x, axis):
    count = lax.axis_size(axis)
    pieces = x.reshape((count, x.shape[0] // count) + x.shape[1:])
    received = lax.all_to_all(pieces, axis, split_axis=0, concat_axis=0, tiled=True)
    return jnp.sum(received.astype(jnp.float32), axis=0)


def pack_grads(local_weight, local_bias):
    pad = jnp.zeros((local_weight.shape[0], 127), jnp.float32)
    return jnp.concatenate([local_weight, local_bias[:, None], pad], axis=1)


def unpack_grads(by_col_then_row, width):
    cols, rows = by_col_then_row.shape[0], by_col_then_row.shape[1]
    whole = by_col_then_row.transpose(1, 0, 2).reshape(cols * rows, -1)
    return whole[:, :width], whole[:, width]


def transposed_product(left, weight):
    return lax.dot_general(
        left, weight, (((1,), (1,)), ((), ())), preferred_element_type=jnp.float32
    ).astype(jnp.bfloat16)


def source_total(received):
    return jnp.sum(received.astype(jnp.float32), axis=0).astype(jnp.bfloat16)


def per_device(
    features, block_values, block_rows, block_cols, block_count, weight, bias, cotangent
):
    tile_values = block_values[0, 0]
    tile_rows = block_rows[0, 0]
    tile_cols = block_cols[0, 0]
    live_count = block_count[0, 0]
    own_nodes = features.shape[0]
    width = features.shape[1]
    row_len = lax.axis_size("col") * own_nodes
    gathered = exchange(features, "row", True, 4).reshape(-1, width)
    col_len = gathered.shape[0]
    partial_value = slot_product(
        tile_values, tile_rows, tile_cols, live_count, gathered, row_len, False
    )
    pieces = partial_value.reshape(lax.axis_size("col"), own_nodes, width)
    received = exchange_steps(pieces, "col", 0, 1, 2)
    aggregate = jnp.sum(received.astype(jnp.float32), axis=0).astype(jnp.bfloat16)
    preact = jnp.dot(aggregate, weight, preferred_element_type=jnp.float32) + bias
    hidden = jax.nn.silu(preact).astype(jnp.bfloat16)
    sigma = jax.nn.sigmoid(preact)
    grad_pre = cotangent.astype(jnp.float32) * sigma * (1.0 + preact * (1.0 - sigma))
    grad_low = grad_pre.astype(jnp.bfloat16)
    local_weight = lax.dot_general(
        aggregate, grad_low, (((0,), (0,)), ((), ())), preferred_element_type=jnp.float32
    )
    local_bias = jnp.sum(grad_pre, axis=0)
    grad_agg = transposed_product(grad_low, weight)
    packed = pack_grads(local_weight, local_bias)
    rows_count = lax.axis_size("row")
    row_pieces = packed.reshape((rows_count, packed.shape[0] // rows_count) + packed.shape[1:])
    grad_stack, by_row_pieces = gather_and_exchange(grad_agg, row_pieces, "col", 0)
    grad_panel = grad_stack.reshape(-1, width)
    by_row = jnp.sum(by_row_pieces, axis=0)
    back = slot_product(tile_values, tile_rows, tile_cols, live_count, grad_panel, col_len, True)
    back_low = back.astype(jnp.bfloat16).reshape(col_len // own_nodes, own_nodes, width)
    parts = by_row.reshape((by_row.shape[0], 1) + by_row.shape[1:])
    received, _, gathered_rows = back_exchange(back_low, parts, 1)
    every = gathered_rows.reshape(gathered_rows.shape[0], gathered_rows.shape[1], -1)
    feature_grad = jnp.sum(received.astype(jnp.float32), axis=0).astype(jnp.bfloat16)
    weight_grad, bias_grad = unpack_grads(every, width)
    return (hidden, weight_grad, bias_grad, feature_grad)


def solution(mesh):
    in_specs = (
        P(("col", "row"), None),
        P("row", "col", None, None, None),
        P("row", "col", None),
        P("row", "col", None),
        P("row", "col"),
        P(),
        P(),
        P(("row", "col"), None),
    )
    out_specs = (P(("row", "col"), None), P(), P(), P(("col", "row"), None))
    return jax.shard_map(
        per_device, mesh=mesh, in_specs=in_specs, out_specs=out_specs, check_vma=False
    )
```

```python
import functools

import jax
import jax.numpy as jnp
from jax import lax
from jax.experimental import pallas as pl
from jax.experimental.pallas import tpu as pltpu
from jax.sharding import PartitionSpec as P

MESH_ID = pl.DeviceIdType.MESH


def _exchange_kernel(axis, other, n, broadcast, src_ref, out_ref, send_sem, recv_sem, own_sem):
    me = lax.axis_index(axis)
    there = lax.axis_index(other)

    def device(k):
        return (k, there) if axis == "row" else (there, k)

    def piece(k):
        return src_ref if broadcast else src_ref.at[k]

    barrier = pltpu.get_barrier_semaphore()

    def greet(step, carry):
        peer = lax.rem(me + step, n)
        pl.semaphore_signal(barrier, inc=1, device_id=device(peer), device_id_type=MESH_ID)
        return carry

    lax.fori_loop(1, n, greet, 0)
    pl.semaphore_wait(barrier, n - 1)

    own = pltpu.make_async_copy(piece(me), out_ref.at[me], own_sem)
    own.start()

    def send(step, carry):
        peer = lax.rem(me + step, n)
        pltpu.make_async_remote_copy(
            src_ref=piece(peer), dst_ref=out_ref.at[me], send_sem=send_sem.at[step],
            recv_sem=recv_sem.at[step], device_id=device(peer), device_id_type=MESH_ID,
        ).start()
        return carry

    lax.fori_loop(1, n, send, 0)

    def finish(step, carry):
        peer = lax.rem(me + step, n)
        source = lax.rem(me + n - step, n)
        pltpu.make_async_remote_copy(
            src_ref=piece(peer), dst_ref=out_ref.at[me], send_sem=send_sem.at[step],
            recv_sem=recv_sem.at[step], device_id=device(peer), device_id_type=MESH_ID,
        ).wait_send()
        pltpu.make_async_remote_copy(
            src_ref=piece(source), dst_ref=out_ref.at[source], send_sem=send_sem.at[step],
            recv_sem=recv_sem.at[step], device_id=device(source), device_id_type=MESH_ID,
        ).wait_recv()
        return carry

    lax.fori_loop(1, n, finish, 0)
    own.wait()


def _steps_kernel(axis, other, n, first, stride, count, src_ref, out_ref, send_sem, recv_sem, own_sem):
    me = lax.axis_index(axis)
    there = lax.axis_index(other)
    begin = 1 if first == 0 else 0

    def device(k):
        return (k, there) if axis == "row" else (there, k)

    def copy(slot, peer, piece):
        return pltpu.make_async_remote_copy(
            src_ref=src_ref.at[piece], dst_ref=out_ref.at[slot], send_sem=send_sem.at[slot],
            recv_sem=recv_sem.at[slot], device_id=device(peer), device_id_type=MESH_ID,
        )

    barrier = pltpu.get_barrier_semaphore()

    def greet(slot, carry):
        step = first + stride * slot
        for peer in (lax.rem(me + step, n), lax.rem(me + n - step, n)):
            pl.semaphore_signal(barrier, inc=1, device_id=device(peer), device_id_type=MESH_ID)
        return carry

    lax.fori_loop(begin, count, greet, 0)
    pl.semaphore_wait(barrier, 2 * (count - begin))
    if first == 0:
        own = pltpu.make_async_copy(src_ref.at[me], out_ref.at[0], own_sem)
        own.start()

    def send(slot, carry):
        peer = lax.rem(me + first + stride * slot, n)
        copy(slot, peer, peer).start()
        return carry

    lax.fori_loop(begin, count, send, 0)

    def finish(slot, carry):
        step = first + stride * slot
        peer = lax.rem(me + step, n)
        copy(slot, peer, peer).wait_send()
        source = lax.rem(me + n - step, n)
        copy(slot, source, me).wait_recv()
        return carry

    lax.fori_loop(begin, count, finish, 0)
    if first == 0:
        own.wait()


def exchange_steps(pieces, axis, first, stride, ident):
    n = lax.axis_size(axis)
    count = (n - first + stride - 1) // stride
    other = "col" if axis == "row" else "row"
    shape = (count,) + pieces.shape[1:]
    return pl.pallas_call(
        functools.partial(_steps_kernel, axis, other, n, first, stride, count),
        out_shape=jax.ShapeDtypeStruct(shape, pieces.dtype),
        in_specs=[pl.BlockSpec(memory_space=pl.ANY)],
        out_specs=pl.BlockSpec(memory_space=pl.ANY),
        scratch_shapes=[
            pltpu.SemaphoreType.DMA((count,)),
            pltpu.SemaphoreType.DMA((count,)),
            pltpu.SemaphoreType.DMA(()),
        ],
        compiler_params=pltpu.CompilerParams(collective_id=ident, has_side_effects=True),
        cost_estimate=pl.CostEstimate(
            flops=0, transcendentals=0, bytes_accessed=2 * count * pieces[0].size * pieces.dtype.itemsize
        ),
    )(pieces)


def _gather_steps_kernel(
    axis, other, n, m, src_ref, pieces_ref, out_ref, pieces_out,
    send_sem, recv_sem, own_sem, piece_send, piece_recv, piece_own,
):
    me = lax.axis_index(axis)
    there = lax.axis_index(other)

    def device(k):
        return (k, there) if axis == "row" else (there, k)

    def across(k):
        return (me, k) if axis == "row" else (k, me)

    def gather_copy(step, peer, slot):
        return pltpu.make_async_remote_copy(
            src_ref=src_ref, dst_ref=out_ref.at[slot], send_sem=send_sem.at[step],
            recv_sem=recv_sem.at[step], device_id=device(peer), device_id_type=MESH_ID,
        )

    def piece_copy(step, peer, piece):
        return pltpu.make_async_remote_copy(
            src_ref=pieces_ref.at[piece], dst_ref=pieces_out.at[step], send_sem=piece_send.at[step],
            recv_sem=piece_recv.at[step], device_id=across(peer), device_id_type=MESH_ID,
        )

    barrier = pltpu.get_barrier_semaphore()

    def greet(step, carry):
        pl.semaphore_signal(barrier, inc=1, device_id=device(lax.rem(me + step, n)), device_id_type=MESH_ID)
        return carry

    def greet_across(step, carry):
        pl.semaphore_signal(barrier, inc=1, device_id=across(lax.rem(there + step, m)), device_id_type=MESH_ID)
        return carry

    lax.fori_loop(1, n, greet, 0)
    lax.fori_loop(1, m, greet_across, 0)
    pl.semaphore_wait(barrier, n - 1 + m - 1)
    own = pltpu.make_async_copy(src_ref, out_ref.at[me], own_sem)
    own.start()
    own_piece = pltpu.make_async_copy(pieces_ref.at[there], pieces_out.at[0], piece_own)
    own_piece.start()

    def send(step, carry):
        gather_copy(step, lax.rem(me + step, n), me).start()
        return carry

    def send_across(step, carry):
        peer = lax.rem(there + step, m)
        piece_copy(step, peer, peer).start()
        return carry

    lax.fori_loop(1, m, send_across, 0)
    lax.fori_loop(1, n, send, 0)

    def finish(step, carry):
        gather_copy(step, lax.rem(me + step, n), me).wait_send()
        source = lax.rem(me + n - step, n)
        gather_copy(step, source, source).wait_recv()
        return carry

    def finish_across(step, carry):
        peer = lax.rem(there + step, m)
        piece_copy(step, peer, peer).wait_send()
        source = lax.rem(there + m - step, m)
        piece_copy(step, source, there).wait_recv()
        return carry

    lax.fori_loop(1, n, finish, 0)
    lax.fori_loop(1, m, finish_across, 0)
    own.wait()
    own_piece.wait()


def gather_and_exchange(x, pieces, axis, ident):
    n = lax.axis_size(axis)
    other = "col" if axis == "row" else "row"
    m = lax.axis_size(other)
    shapes = (
        jax.ShapeDtypeStruct((n,) + x.shape, x.dtype),
        jax.ShapeDtypeStruct(pieces.shape, pieces.dtype),
    )
    moved = 2 * n * x.size * x.dtype.itemsize + 2 * pieces.size * pieces.dtype.itemsize
    return pl.pallas_call(
        functools.partial(_gather_steps_kernel, axis, other, n, m),
        out_shape=shapes,
        in_specs=[pl.BlockSpec(memory_space=pl.ANY), pl.BlockSpec(memory_space=pl.ANY)],
        out_specs=(pl.BlockSpec(memory_space=pl.ANY), pl.BlockSpec(memory_space=pl.ANY)),
        scratch_shapes=[
            pltpu.SemaphoreType.DMA((n,)),
            pltpu.SemaphoreType.DMA((n,)),
            pltpu.SemaphoreType.DMA(()),
            pltpu.SemaphoreType.DMA((m,)),
            pltpu.SemaphoreType.DMA((m,)),
            pltpu.SemaphoreType.DMA(()),
        ],
        compiler_params=pltpu.CompilerParams(collective_id=ident, has_side_effects=True),
        cost_estimate=pl.CostEstimate(flops=0, transcendentals=0, bytes_accessed=moved),
    )(x, pieces)


def _back_kernel(
    n, m, src_ref, part_ref, out_ref, row_buf, col_buf,
    send_sem, recv_sem, own_sem, a_send, a_recv, a_own, b_send, b_recv, b_own,
    c_send, c_recv, c_own, part_buf, w_ref,
):
    me = lax.axis_index("row")
    there = lax.axis_index("col")

    def along(k):
        return (k, there)

    def across(k):
        return (me, k)

    def main_copy(step, peer, piece):
        return pltpu.make_async_remote_copy(
            src_ref=src_ref.at[piece], dst_ref=out_ref.at[step], send_sem=send_sem.at[step],
            recv_sem=recv_sem.at[step], device_id=along(peer), device_id_type=MESH_ID,
        )

    def row_copy(step, peer, slot):
        return pltpu.make_async_remote_copy(
            src_ref=w_ref, dst_ref=row_buf.at[slot], send_sem=a_send.at[step],
            recv_sem=a_recv.at[step], device_id=along(peer), device_id_type=MESH_ID,
        )

    def col_copy(step, peer, slot):
        return pltpu.make_async_remote_copy(
            src_ref=row_buf, dst_ref=col_buf.at[slot], send_sem=b_send.at[step],
            recv_sem=b_recv.at[step], device_id=across(peer), device_id_type=MESH_ID,
        )

    def part_copy(step, peer):
        return pltpu.make_async_remote_copy(
            src_ref=part_ref.at[peer], dst_ref=part_buf.at[step], send_sem=c_send.at[step],
            recv_sem=c_recv.at[step], device_id=across(peer), device_id_type=MESH_ID,
        )

    barrier = pltpu.get_barrier_semaphore()

    def greet(step, carry):
        pl.semaphore_signal(barrier, inc=1, device_id=along(lax.rem(me + step, n)), device_id_type=MESH_ID)
        return carry

    def greet_across(step, carry):
        pl.semaphore_signal(barrier, inc=1, device_id=across(lax.rem(there + step, m)), device_id_type=MESH_ID)
        return carry

    lax.fori_loop(1, n, greet, 0)
    lax.fori_loop(1, m, greet_across, 0)
    pl.semaphore_wait(barrier, n - 1 + m - 1)
    own = pltpu.make_async_copy(src_ref.at[me], out_ref.at[0], own_sem)
    own.start()
    own_part = pltpu.make_async_copy(part_ref.at[there], part_buf.at[0], c_own)
    own_part.start()

    def send_part(step, carry):
        part_copy(step, lax.rem(there + step, m)).start()
        return carry

    def send_main(step, carry):
        peer = lax.rem(me + step, n)
        main_copy(step, peer, peer).start()
        return carry

    lax.fori_loop(1, m, send_part, 0)

    def finish_part(step, carry):
        part_copy(step, lax.rem(there + step, m)).wait_send()
        part_copy(step, lax.rem(there + m - step, m)).wait_recv()
        return carry

    lax.fori_loop(1, m, finish_part, 0)
    own_part.wait()
    w_ref[...] = jnp.sum(part_buf[...], axis=0)
    own_row = pltpu.make_async_copy(w_ref, row_buf.at[me], a_own)
    own_row.start()

    def send_row(step, carry):
        row_copy(step, lax.rem(me + step, n), me).start()
        return carry

    lax.fori_loop(1, n, send_row, 0)
    lax.fori_loop(1, n, send_main, 0)

    def finish_row(step, carry):
        row_copy(step, lax.rem(me + step, n), me).wait_send()
        source = lax.rem(me + n - step, n)
        row_copy(step, source, source).wait_recv()
        return carry

    lax.fori_loop(1, n, finish_row, 0)
    own_row.wait()
    own_col = pltpu.make_async_copy(row_buf, col_buf.at[there], b_own)
    own_col.start()

    def send_col(step, carry):
        col_copy(step, lax.rem(there + step, m), there).start()
        return carry

    lax.fori_loop(1, m, send_col, 0)

    def finish_main(step, carry):
        peer = lax.rem(me + step, n)
        main_copy(step, peer, peer).wait_send()
        source = lax.rem(me + n - step, n)
        main_copy(step, source, me).wait_recv()
        return carry

    lax.fori_loop(1, n, finish_main, 0)

    def finish_col(step, carry):
        col_copy(step, lax.rem(there + step, m), there).wait_send()
        source = lax.rem(there + m - step, m)
        col_copy(step, source, source).wait_recv()
        return carry

    lax.fori_loop(1, m, finish_col, 0)
    own_col.wait()
    own.wait()


def back_exchange(pieces, parts, ident):
    n = lax.axis_size("row")
    m = lax.axis_size("col")
    row = parts[0]
    shapes = (
        jax.ShapeDtypeStruct(pieces.shape, pieces.dtype),
        jax.ShapeDtypeStruct((n,) + row.shape, row.dtype),
        jax.ShapeDtypeStruct((m, n) + row.shape, row.dtype),
    )
    moved = 2 * pieces.size * pieces.dtype.itemsize + 2 * m * n * row.size * row.dtype.itemsize
    return pl.pallas_call(
        functools.partial(_back_kernel, n, m),
        out_shape=shapes,
        in_specs=[pl.BlockSpec(memory_space=pl.ANY), pl.BlockSpec(memory_space=pl.ANY)],
        out_specs=tuple(pl.BlockSpec(memory_space=pl.ANY) for _ in range(3)),
        scratch_shapes=[
            pltpu.SemaphoreType.DMA((n,)),
            pltpu.SemaphoreType.DMA((n,)),
            pltpu.SemaphoreType.DMA(()),
            pltpu.SemaphoreType.DMA((n,)),
            pltpu.SemaphoreType.DMA((n,)),
            pltpu.SemaphoreType.DMA(()),
            pltpu.SemaphoreType.DMA((m,)),
            pltpu.SemaphoreType.DMA((m,)),
            pltpu.SemaphoreType.DMA(()),
            pltpu.SemaphoreType.DMA((m,)),
            pltpu.SemaphoreType.DMA((m,)),
            pltpu.SemaphoreType.DMA(()),
            pltpu.VMEM(parts.shape, parts.dtype),
            pltpu.VMEM(row.shape, row.dtype),
        ],
        compiler_params=pltpu.CompilerParams(collective_id=ident, has_side_effects=True),
        cost_estimate=pl.CostEstimate(flops=0, transcendentals=0, bytes_accessed=moved),
    )(pieces, parts)


def exchange(x, axis, broadcast, ident):
    n = lax.axis_size(axis)
    other = "col" if axis == "row" else "row"
    shape = (n,) + (x.shape if broadcast else x.shape[1:])
    return pl.pallas_call(
        functools.partial(_exchange_kernel, axis, other, n, broadcast),
        out_shape=jax.ShapeDtypeStruct(shape, x.dtype),
        in_specs=[pl.BlockSpec(memory_space=pl.ANY)],
        out_specs=pl.BlockSpec(memory_space=pl.ANY),
        scratch_shapes=[
            pltpu.SemaphoreType.DMA((n,)),
            pltpu.SemaphoreType.DMA((n,)),
            pltpu.SemaphoreType.DMA(()),
        ],
        compiler_params=pltpu.CompilerParams(collective_id=ident, has_side_effects=True),
        cost_estimate=pl.CostEstimate(
            flops=0, transcendentals=0, bytes_accessed=2 * n * x.size * x.dtype.itemsize
        ),
    )(x)


def _slot_kernel(backward, slots, src_ids, tgt_ids, count_ref, vals_ref, src_ref, out_ref, acc_ref):
    s = pl.program_id(0)

    @pl.when(s == 0)
    def _():
        acc_ref[...] = jnp.zeros_like(acc_ref)

    @pl.when(s < count_ref[0])
    def _():
        block = vals_ref[0]
        segment = src_ref[0]
        if backward:
            dims = (((0,), (0,)), ((), ()))
        else:
            dims = (((1,), (0,)), ((), ()))
        product = lax.dot_general(block, segment, dims, preferred_element_type=jnp.float32)
        target = tgt_ids[s]
        acc_ref[target] = acc_ref[target] + product

    @pl.when(s == slots - 1)
    def _():
        out_ref[...] = acc_ref[...].astype(out_ref.dtype)


def slot_product(tile_values, tile_rows, tile_cols, live_count, source, out_len, backward):
    slots, block_size = tile_values.shape[0], tile_values.shape[1]
    width = source.shape[1]
    n_src = source.shape[0] // block_size
    n_out = out_len // block_size
    panels = source.reshape(n_src, block_size, width)
    if backward:
        src_ids, tgt_ids = tile_rows, tile_cols
    else:
        src_ids, tgt_ids = tile_cols, tile_rows
    src_ids = jnp.clip(src_ids, 0, n_src - 1).astype(jnp.int32)
    tgt_ids = jnp.clip(tgt_ids, 0, n_out - 1).astype(jnp.int32)
    count = jnp.reshape(live_count, (1,)).astype(jnp.int32)
    grid_spec = pltpu.PrefetchScalarGridSpec(
        num_scalar_prefetch=3,
        grid=(slots,),
        in_specs=[
            pl.BlockSpec((1, block_size, block_size), lambda s, src, tgt, cnt: (s, 0, 0)),
            pl.BlockSpec((1, block_size, width), lambda s, src, tgt, cnt: (src[s], 0, 0)),
        ],
        out_specs=pl.BlockSpec((n_out, block_size, width), lambda s, src, tgt, cnt: (0, 0, 0)),
        scratch_shapes=[pltpu.VMEM((n_out, block_size, width), jnp.float32)],
    )
    out = pl.pallas_call(
        functools.partial(_slot_kernel, backward, slots),
        out_shape=jax.ShapeDtypeStruct((n_out, block_size, width), jnp.bfloat16),
        grid_spec=grid_spec,
        compiler_params=pltpu.CompilerParams(
            dimension_semantics=("arbitrary",), vmem_limit_bytes=48 * 1024 * 1024
        ),
        cost_estimate=pl.CostEstimate(
            flops=2 * slots * block_size * block_size * width,
            transcendentals=0,
            bytes_accessed=2 * (slots * block_size * (block_size + width) + n_out * block_size * width),
        ),
    )(src_ids, tgt_ids, count, tile_values, panels)
    return out.reshape(out_len, width)


def gather_rows(x, axis):
    count = lax.axis_size(axis)
    stacked = jnp.broadcast_to(x[None], (count,) + x.shape)
    received = lax.all_to_all(stacked, axis, split_axis=0, concat_axis=0, tiled=True)
    return received.reshape((count * x.shape[0],) + x.shape[1:])


def scatter_sum(x, axis):
    count = lax.axis_size(axis)
    pieces = x.reshape((count, x.shape[0] // count) + x.shape[1:])
    received = lax.all_to_all(pieces, axis, split_axis=0, concat_axis=0, tiled=True)
    return jnp.sum(received.astype(jnp.float32), axis=0)


def pack_grads(local_weight, local_bias):
    pad = jnp.zeros((local_weight.shape[0], 127), jnp.float32)
    return jnp.concatenate([local_weight, local_bias[:, None], pad], axis=1)


def unpack_grads(by_col_then_row, width):
    cols, rows = by_col_then_row.shape[0], by_col_then_row.shape[1]
    whole = by_col_then_row.transpose(1, 0, 2).reshape(cols * rows, -1)
    return whole[:, :width], whole[:, width]


def transposed_product(left, weight):
    return lax.dot_general(
        left, weight, (((1,), (1,)), ((), ())), preferred_element_type=jnp.float32
    ).astype(jnp.bfloat16)


def source_total(received):
    return jnp.sum(received.astype(jnp.float32), axis=0).astype(jnp.bfloat16)


def per_device(
    features, block_values, block_rows, block_cols, block_count, weight, bias, cotangent
):
    tile_values = block_values[0, 0]
    tile_rows = block_rows[0, 0]
    tile_cols = block_cols[0, 0]
    live_count = block_count[0, 0]
    own_nodes = features.shape[0]
    width = features.shape[1]
    row_len = lax.axis_size("col") * own_nodes
    gathered = exchange(features, "row", True, 4).reshape(-1, width)
    col_len = gathered.shape[0]
    partial_value = slot_product(
        tile_values, tile_rows, tile_cols, live_count, gathered, row_len, False
    )
    pieces = partial_value.reshape(lax.axis_size("col"), own_nodes, width)
    received = exchange_steps(pieces, "col", 0, 1, 2)
    aggregate = jnp.sum(received.astype(jnp.float32), axis=0).astype(jnp.bfloat16)
    preact = jnp.dot(aggregate, weight, preferred_element_type=jnp.float32) + bias
    hidden = jax.nn.silu(preact).astype(jnp.bfloat16)
    sigma = jax.nn.sigmoid(preact)
    grad_pre = cotangent.astype(jnp.float32) * sigma * (1.0 + preact * (1.0 - sigma))
    grad_low = grad_pre.astype(jnp.bfloat16)
    local_weight = lax.dot_general(
        aggregate, grad_low, (((0,), (0,)), ((), ())), preferred_element_type=jnp.float32
    )
    local_bias = jnp.sum(grad_pre, axis=0)
    grad_agg = transposed_product(grad_low, weight)
    packed = pack_grads(local_weight, local_bias)
    rows_count = lax.axis_size("row")
    row_pieces = packed.reshape((rows_count, packed.shape[0] // rows_count) + packed.shape[1:])
    grad_stack, by_row_pieces = gather_and_exchange(grad_agg, row_pieces, "col", 0)
    grad_panel = grad_stack.reshape(-1, width)
    by_row = jnp.sum(by_row_pieces, axis=0)
    back = slot_product(tile_values, tile_rows, tile_cols, live_count, grad_panel, col_len, True)
    back_low = back.astype(jnp.bfloat16).reshape(col_len // own_nodes, own_nodes, width)
    parts = by_row.reshape((by_row.shape[0], 1) + by_row.shape[1:])
    received, _, gathered_rows = back_exchange(back_low, parts, 1)
    every = gathered_rows.reshape(gathered_rows.shape[0], gathered_rows.shape[1], -1)
    feature_grad = jnp.sum(received.astype(jnp.float32), axis=0).astype(jnp.bfloat16)
    weight_grad, bias_grad = unpack_grads(every, width)
    return (hidden, weight_grad, bias_grad, feature_grad)


def solution(mesh):
    in_specs = (
        P(("col", "row"), None),
        P("row", "col", None, None, None),
        P("row", "col", None),
        P("row", "col", None),
        P("row", "col"),
        P(),
        P(),
        P(("row", "col"), None),
    )
    out_specs = (P(("row", "col"), None), P(), P(), P(("col", "row"), None))
    return jax.shard_map(
        per_device, mesh=mesh, in_specs=in_specs, out_specs=out_specs, check_vma=False
    )
```

```python
import functools

import jax
import jax.numpy as jnp
from jax import lax
from jax.experimental import pallas as pl
from jax.experimental.pallas import tpu as pltpu
from jax.sharding import PartitionSpec as P

MESH_ID = pl.DeviceIdType.MESH


def _exchange_kernel(axis, other, n, broadcast, src_ref, out_ref, send_sem, recv_sem, own_sem):
    me = lax.axis_index(axis)
    there = lax.axis_index(other)

    def device(k):
        return (k, there) if axis == "row" else (there, k)

    def piece(k):
        return src_ref if broadcast else src_ref.at[k]

    barrier = pltpu.get_barrier_semaphore()

    def greet(step, carry):
        peer = lax.rem(me + step, n)
        pl.semaphore_signal(barrier, inc=1, device_id=device(peer), device_id_type=MESH_ID)
        return carry

    lax.fori_loop(1, n, greet, 0)
    pl.semaphore_wait(barrier, n - 1)

    own = pltpu.make_async_copy(piece(me), out_ref.at[me], own_sem)
    own.start()

    def send(step, carry):
        peer = lax.rem(me + step, n)
        pltpu.make_async_remote_copy(
            src_ref=piece(peer), dst_ref=out_ref.at[me], send_sem=send_sem.at[step],
            recv_sem=recv_sem.at[step], device_id=device(peer), device_id_type=MESH_ID,
        ).start()
        return carry

    lax.fori_loop(1, n, send, 0)

    def finish(step, carry):
        peer = lax.rem(me + step, n)
        source = lax.rem(me + n - step, n)
        pltpu.make_async_remote_copy(
            src_ref=piece(peer), dst_ref=out_ref.at[me], send_sem=send_sem.at[step],
            recv_sem=recv_sem.at[step], device_id=device(peer), device_id_type=MESH_ID,
        ).wait_send()
        pltpu.make_async_remote_copy(
            src_ref=piece(source), dst_ref=out_ref.at[source], send_sem=send_sem.at[step],
            recv_sem=recv_sem.at[step], device_id=device(source), device_id_type=MESH_ID,
        ).wait_recv()
        return carry

    lax.fori_loop(1, n, finish, 0)
    own.wait()


def _steps_kernel(axis, other, n, first, stride, count, src_ref, out_ref, send_sem, recv_sem, own_sem):
    me = lax.axis_index(axis)
    there = lax.axis_index(other)
    begin = 1 if first == 0 else 0

    def device(k):
        return (k, there) if axis == "row" else (there, k)

    def copy(slot, peer, piece):
        return pltpu.make_async_remote_copy(
            src_ref=src_ref.at[piece], dst_ref=out_ref.at[slot], send_sem=send_sem.at[slot],
            recv_sem=recv_sem.at[slot], device_id=device(peer), device_id_type=MESH_ID,
        )

    barrier = pltpu.get_barrier_semaphore()

    def greet(slot, carry):
        step = first + stride * slot
        for peer in (lax.rem(me + step, n), lax.rem(me + n - step, n)):
            pl.semaphore_signal(barrier, inc=1, device_id=device(peer), device_id_type=MESH_ID)
        return carry

    lax.fori_loop(begin, count, greet, 0)
    pl.semaphore_wait(barrier, 2 * (count - begin))
    if first == 0:
        own = pltpu.make_async_copy(src_ref.at[me], out_ref.at[0], own_sem)
        own.start()

    def send(slot, carry):
        peer = lax.rem(me + first + stride * slot, n)
        copy(slot, peer, peer).start()
        return carry

    lax.fori_loop(begin, count, send, 0)

    def finish(slot, carry):
        step = first + stride * slot
        peer = lax.rem(me + step, n)
        copy(slot, peer, peer).wait_send()
        source = lax.rem(me + n - step, n)
        copy(slot, source, me).wait_recv()
        return carry

    lax.fori_loop(begin, count, finish, 0)
    if first == 0:
        own.wait()


def exchange_steps(pieces, axis, first, stride, ident):
    n = lax.axis_size(axis)
    count = (n - first + stride - 1) // stride
    other = "col" if axis == "row" else "row"
    shape = (count,) + pieces.shape[1:]
    return pl.pallas_call(
        functools.partial(_steps_kernel, axis, other, n, first, stride, count),
        out_shape=jax.ShapeDtypeStruct(shape, pieces.dtype),
        in_specs=[pl.BlockSpec(memory_space=pl.ANY)],
        out_specs=pl.BlockSpec(memory_space=pl.ANY),
        scratch_shapes=[
            pltpu.SemaphoreType.DMA((count,)),
            pltpu.SemaphoreType.DMA((count,)),
            pltpu.SemaphoreType.DMA(()),
        ],
        compiler_params=pltpu.CompilerParams(collective_id=ident, has_side_effects=True),
        cost_estimate=pl.CostEstimate(
            flops=0, transcendentals=0, bytes_accessed=2 * count * pieces[0].size * pieces.dtype.itemsize
        ),
    )(pieces)


def _gather_steps_kernel(
    axis, other, n, m, src_ref, pieces_ref, out_ref, pieces_out,
    send_sem, recv_sem, own_sem, piece_send, piece_recv, piece_own,
):
    me = lax.axis_index(axis)
    there = lax.axis_index(other)

    def device(k):
        return (k, there) if axis == "row" else (there, k)

    def across(k):
        return (me, k) if axis == "row" else (k, me)

    def gather_copy(step, peer, slot):
        return pltpu.make_async_remote_copy(
            src_ref=src_ref, dst_ref=out_ref.at[slot], send_sem=send_sem.at[step],
            recv_sem=recv_sem.at[step], device_id=device(peer), device_id_type=MESH_ID,
        )

    def piece_copy(step, peer, piece):
        return pltpu.make_async_remote_copy(
            src_ref=pieces_ref.at[piece], dst_ref=pieces_out.at[step], send_sem=piece_send.at[step],
            recv_sem=piece_recv.at[step], device_id=across(peer), device_id_type=MESH_ID,
        )

    barrier = pltpu.get_barrier_semaphore()

    def greet(step, carry):
        pl.semaphore_signal(barrier, inc=1, device_id=device(lax.rem(me + step, n)), device_id_type=MESH_ID)
        return carry

    def greet_across(step, carry):
        pl.semaphore_signal(barrier, inc=1, device_id=across(lax.rem(there + step, m)), device_id_type=MESH_ID)
        return carry

    lax.fori_loop(1, n, greet, 0)
    lax.fori_loop(1, m, greet_across, 0)
    pl.semaphore_wait(barrier, n - 1 + m - 1)
    own = pltpu.make_async_copy(src_ref, out_ref.at[me], own_sem)
    own.start()
    own_piece = pltpu.make_async_copy(pieces_ref.at[there], pieces_out.at[0], piece_own)
    own_piece.start()

    def send(step, carry):
        gather_copy(step, lax.rem(me + step, n), me).start()
        return carry

    def send_across(step, carry):
        peer = lax.rem(there + step, m)
        piece_copy(step, peer, peer).start()
        return carry

    lax.fori_loop(1, m, send_across, 0)
    lax.fori_loop(1, n, send, 0)

    def finish(step, carry):
        gather_copy(step, lax.rem(me + step, n), me).wait_send()
        source = lax.rem(me + n - step, n)
        gather_copy(step, source, source).wait_recv()
        return carry

    def finish_across(step, carry):
        peer = lax.rem(there + step, m)
        piece_copy(step, peer, peer).wait_send()
        source = lax.rem(there + m - step, m)
        piece_copy(step, source, there).wait_recv()
        return carry

    lax.fori_loop(1, n, finish, 0)
    lax.fori_loop(1, m, finish_across, 0)
    own.wait()
    own_piece.wait()


def gather_and_exchange(x, pieces, axis, ident):
    n = lax.axis_size(axis)
    other = "col" if axis == "row" else "row"
    m = lax.axis_size(other)
    shapes = (
        jax.ShapeDtypeStruct((n,) + x.shape, x.dtype),
        jax.ShapeDtypeStruct(pieces.shape, pieces.dtype),
    )
    moved = 2 * n * x.size * x.dtype.itemsize + 2 * pieces.size * pieces.dtype.itemsize
    return pl.pallas_call(
        functools.partial(_gather_steps_kernel, axis, other, n, m),
        out_shape=shapes,
        in_specs=[pl.BlockSpec(memory_space=pl.ANY), pl.BlockSpec(memory_space=pl.ANY)],
        out_specs=(pl.BlockSpec(memory_space=pl.ANY), pl.BlockSpec(memory_space=pl.ANY)),
        scratch_shapes=[
            pltpu.SemaphoreType.DMA((n,)),
            pltpu.SemaphoreType.DMA((n,)),
            pltpu.SemaphoreType.DMA(()),
            pltpu.SemaphoreType.DMA((m,)),
            pltpu.SemaphoreType.DMA((m,)),
            pltpu.SemaphoreType.DMA(()),
        ],
        compiler_params=pltpu.CompilerParams(collective_id=ident, has_side_effects=True),
        cost_estimate=pl.CostEstimate(flops=0, transcendentals=0, bytes_accessed=moved),
    )(x, pieces)


def _back_kernel(
    n, m, src_ref, part_ref, out_ref, row_buf, col_buf,
    send_sem, recv_sem, own_sem, a_send, a_recv, a_own, b_send, b_recv, b_own,
    c_send, c_recv, c_own, part_buf, w_ref,
):
    me = lax.axis_index("row")
    there = lax.axis_index("col")

    def along(k):
        return (k, there)

    def across(k):
        return (me, k)

    def main_copy(step, peer, piece):
        return pltpu.make_async_remote_copy(
            src_ref=src_ref.at[piece], dst_ref=out_ref.at[step], send_sem=send_sem.at[step],
            recv_sem=recv_sem.at[step], device_id=along(peer), device_id_type=MESH_ID,
        )

    def row_copy(step, peer, slot):
        return pltpu.make_async_remote_copy(
            src_ref=w_ref, dst_ref=row_buf.at[slot], send_sem=a_send.at[step],
            recv_sem=a_recv.at[step], device_id=along(peer), device_id_type=MESH_ID,
        )

    def col_copy(step, peer, slot):
        return pltpu.make_async_remote_copy(
            src_ref=row_buf, dst_ref=col_buf.at[slot], send_sem=b_send.at[step],
            recv_sem=b_recv.at[step], device_id=across(peer), device_id_type=MESH_ID,
        )

    def part_copy(step, peer):
        return pltpu.make_async_remote_copy(
            src_ref=part_ref.at[peer], dst_ref=part_buf.at[step], send_sem=c_send.at[step],
            recv_sem=c_recv.at[step], device_id=across(peer), device_id_type=MESH_ID,
        )

    barrier = pltpu.get_barrier_semaphore()

    def greet(step, carry):
        pl.semaphore_signal(barrier, inc=1, device_id=along(lax.rem(me + step, n)), device_id_type=MESH_ID)
        return carry

    def greet_across(step, carry):
        pl.semaphore_signal(barrier, inc=1, device_id=across(lax.rem(there + step, m)), device_id_type=MESH_ID)
        return carry

    lax.fori_loop(1, n, greet, 0)
    lax.fori_loop(1, m, greet_across, 0)
    pl.semaphore_wait(barrier, n - 1 + m - 1)
    own = pltpu.make_async_copy(src_ref.at[me], out_ref.at[0], own_sem)
    own.start()
    own_part = pltpu.make_async_copy(part_ref.at[there], part_buf.at[0], c_own)
    own_part.start()

    def send_part(step, carry):
        part_copy(step, lax.rem(there + step, m)).start()
        return carry

    def send_main(step, carry):
        peer = lax.rem(me + step, n)
        main_copy(step, peer, peer).start()
        return carry

    lax.fori_loop(1, m, send_part, 0)
    lax.fori_loop(0, n // 2, lambda i, c: send_main(1 + 2 * i, c), 0)

    def finish_part(step, carry):
        part_copy(step, lax.rem(there + step, m)).wait_send()
        part_copy(step, lax.rem(there + m - step, m)).wait_recv()
        return carry

    lax.fori_loop(1, m, finish_part, 0)
    own_part.wait()
    w_ref[...] = jnp.sum(part_buf[...], axis=0)
    own_row = pltpu.make_async_copy(w_ref, row_buf.at[me], a_own)
    own_row.start()

    def send_row(step, carry):
        row_copy(step, lax.rem(me + step, n), me).start()
        return carry

    lax.fori_loop(1, n, send_row, 0)
    lax.fori_loop(1, n // 2, lambda i, c: send_main(2 * i, c), 0)

    def finish_row(step, carry):
        row_copy(step, lax.rem(me + step, n), me).wait_send()
        source = lax.rem(me + n - step, n)
        row_copy(step, source, source).wait_recv()
        return carry

    lax.fori_loop(1, n, finish_row, 0)
    own_row.wait()
    own_col = pltpu.make_async_copy(row_buf, col_buf.at[there], b_own)
    own_col.start()

    def send_col(step, carry):
        col_copy(step, lax.rem(there + step, m), there).start()
        return carry

    lax.fori_loop(1, m, send_col, 0)

    def finish_main(step, carry):
        peer = lax.rem(me + step, n)
        main_copy(step, peer, peer).wait_send()
        source = lax.rem(me + n - step, n)
        main_copy(step, source, me).wait_recv()
        return carry

    lax.fori_loop(1, n, finish_main, 0)

    def finish_col(step, carry):
        col_copy(step, lax.rem(there + step, m), there).wait_send()
        source = lax.rem(there + m - step, m)
        col_copy(step, source, source).wait_recv()
        return carry

    lax.fori_loop(1, m, finish_col, 0)
    own_col.wait()
    own.wait()


def back_exchange(pieces, parts, ident):
    n = lax.axis_size("row")
    m = lax.axis_size("col")
    row = parts[0]
    shapes = (
        jax.ShapeDtypeStruct(pieces.shape, pieces.dtype),
        jax.ShapeDtypeStruct((n,) + row.shape, row.dtype),
        jax.ShapeDtypeStruct((m, n) + row.shape, row.dtype),
    )
    moved = 2 * pieces.size * pieces.dtype.itemsize + 2 * m * n * row.size * row.dtype.itemsize
    return pl.pallas_call(
        functools.partial(_back_kernel, n, m),
        out_shape=shapes,
        in_specs=[pl.BlockSpec(memory_space=pl.ANY), pl.BlockSpec(memory_space=pl.ANY)],
        out_specs=tuple(pl.BlockSpec(memory_space=pl.ANY) for _ in range(3)),
        scratch_shapes=[
            pltpu.SemaphoreType.DMA((n,)),
            pltpu.SemaphoreType.DMA((n,)),
            pltpu.SemaphoreType.DMA(()),
            pltpu.SemaphoreType.DMA((n,)),
            pltpu.SemaphoreType.DMA((n,)),
            pltpu.SemaphoreType.DMA(()),
            pltpu.SemaphoreType.DMA((m,)),
            pltpu.SemaphoreType.DMA((m,)),
            pltpu.SemaphoreType.DMA(()),
            pltpu.SemaphoreType.DMA((m,)),
            pltpu.SemaphoreType.DMA((m,)),
            pltpu.SemaphoreType.DMA(()),
            pltpu.VMEM(parts.shape, parts.dtype),
            pltpu.VMEM(row.shape, row.dtype),
        ],
        compiler_params=pltpu.CompilerParams(collective_id=ident, has_side_effects=True),
        cost_estimate=pl.CostEstimate(flops=0, transcendentals=0, bytes_accessed=moved),
    )(pieces, parts)


def exchange(x, axis, broadcast, ident):
    n = lax.axis_size(axis)
    other = "col" if axis == "row" else "row"
    shape = (n,) + (x.shape if broadcast else x.shape[1:])
    return pl.pallas_call(
        functools.partial(_exchange_kernel, axis, other, n, broadcast),
        out_shape=jax.ShapeDtypeStruct(shape, x.dtype),
        in_specs=[pl.BlockSpec(memory_space=pl.ANY)],
        out_specs=pl.BlockSpec(memory_space=pl.ANY),
        scratch_shapes=[
            pltpu.SemaphoreType.DMA((n,)),
            pltpu.SemaphoreType.DMA((n,)),
            pltpu.SemaphoreType.DMA(()),
        ],
        compiler_params=pltpu.CompilerParams(collective_id=ident, has_side_effects=True),
        cost_estimate=pl.CostEstimate(
            flops=0, transcendentals=0, bytes_accessed=2 * n * x.size * x.dtype.itemsize
        ),
    )(x)


def _slot_kernel(backward, slots, src_ids, tgt_ids, count_ref, vals_ref, src_ref, out_ref, acc_ref):
    s = pl.program_id(0)

    @pl.when(s == 0)
    def _():
        acc_ref[...] = jnp.zeros_like(acc_ref)

    @pl.when(s < count_ref[0])
    def _():
        block = vals_ref[0]
        segment = src_ref[0]
        if backward:
            dims = (((0,), (0,)), ((), ()))
        else:
            dims = (((1,), (0,)), ((), ()))
        product = lax.dot_general(block, segment, dims, preferred_element_type=jnp.float32)
        target = tgt_ids[s]
        acc_ref[target] = acc_ref[target] + product

    @pl.when(s == slots - 1)
    def _():
        out_ref[...] = acc_ref[...].astype(out_ref.dtype)


def slot_product(tile_values, tile_rows, tile_cols, live_count, source, out_len, backward):
    slots, block_size = tile_values.shape[0], tile_values.shape[1]
    width = source.shape[1]
    n_src = source.shape[0] // block_size
    n_out = out_len // block_size
    panels = source.reshape(n_src, block_size, width)
    if backward:
        src_ids, tgt_ids = tile_rows, tile_cols
    else:
        src_ids, tgt_ids = tile_cols, tile_rows
    src_ids = jnp.clip(src_ids, 0, n_src - 1).astype(jnp.int32)
    tgt_ids = jnp.clip(tgt_ids, 0, n_out - 1).astype(jnp.int32)
    count = jnp.reshape(live_count, (1,)).astype(jnp.int32)
    grid_spec = pltpu.PrefetchScalarGridSpec(
        num_scalar_prefetch=3,
        grid=(slots,),
        in_specs=[
            pl.BlockSpec((1, block_size, block_size), lambda s, src, tgt, cnt: (s, 0, 0)),
            pl.BlockSpec((1, block_size, width), lambda s, src, tgt, cnt: (src[s], 0, 0)),
        ],
        out_specs=pl.BlockSpec((n_out, block_size, width), lambda s, src, tgt, cnt: (0, 0, 0)),
        scratch_shapes=[pltpu.VMEM((n_out, block_size, width), jnp.float32)],
    )
    out = pl.pallas_call(
        functools.partial(_slot_kernel, backward, slots),
        out_shape=jax.ShapeDtypeStruct((n_out, block_size, width), jnp.bfloat16),
        grid_spec=grid_spec,
        compiler_params=pltpu.CompilerParams(
            dimension_semantics=("arbitrary",), vmem_limit_bytes=48 * 1024 * 1024
        ),
        cost_estimate=pl.CostEstimate(
            flops=2 * slots * block_size * block_size * width,
            transcendentals=0,
            bytes_accessed=2 * (slots * block_size * (block_size + width) + n_out * block_size * width),
        ),
    )(src_ids, tgt_ids, count, tile_values, panels)
    return out.reshape(out_len, width)


def gather_rows(x, axis):
    count = lax.axis_size(axis)
    stacked = jnp.broadcast_to(x[None], (count,) + x.shape)
    received = lax.all_to_all(stacked, axis, split_axis=0, concat_axis=0, tiled=True)
    return received.reshape((count * x.shape[0],) + x.shape[1:])


def scatter_sum(x, axis):
    count = lax.axis_size(axis)
    pieces = x.reshape((count, x.shape[0] // count) + x.shape[1:])
    received = lax.all_to_all(pieces, axis, split_axis=0, concat_axis=0, tiled=True)
    return jnp.sum(received.astype(jnp.float32), axis=0)


def pack_grads(local_weight, local_bias):
    pad = jnp.zeros((local_weight.shape[0], 127), jnp.float32)
    return jnp.concatenate([local_weight, local_bias[:, None], pad], axis=1)


def unpack_grads(by_col_then_row, width):
    cols, rows = by_col_then_row.shape[0], by_col_then_row.shape[1]
    whole = by_col_then_row.transpose(1, 0, 2).reshape(cols * rows, -1)
    return whole[:, :width], whole[:, width]


def transposed_product(left, weight):
    return lax.dot_general(
        left, weight, (((1,), (1,)), ((), ())), preferred_element_type=jnp.float32
    ).astype(jnp.bfloat16)


def source_total(received):
    return jnp.sum(received.astype(jnp.float32), axis=0).astype(jnp.bfloat16)


def per_device(
    features, block_values, block_rows, block_cols, block_count, weight, bias, cotangent
):
    tile_values = block_values[0, 0]
    tile_rows = block_rows[0, 0]
    tile_cols = block_cols[0, 0]
    live_count = block_count[0, 0]
    own_nodes = features.shape[0]
    width = features.shape[1]
    row_len = lax.axis_size("col") * own_nodes
    gathered = exchange(features, "row", True, 4).reshape(-1, width)
    col_len = gathered.shape[0]
    partial_value = slot_product(
        tile_values, tile_rows, tile_cols, live_count, gathered, row_len, False
    )
    pieces = partial_value.reshape(lax.axis_size("col"), own_nodes, width)
    received = exchange_steps(pieces, "col", 0, 1, 2)
    aggregate = jnp.sum(received.astype(jnp.float32), axis=0).astype(jnp.bfloat16)
    preact = jnp.dot(aggregate, weight, preferred_element_type=jnp.float32) + bias
    hidden = jax.nn.silu(preact).astype(jnp.bfloat16)
    sigma = jax.nn.sigmoid(preact)
    grad_pre = cotangent.astype(jnp.float32) * sigma * (1.0 + preact * (1.0 - sigma))
    grad_low = grad_pre.astype(jnp.bfloat16)
    local_weight = lax.dot_general(
        aggregate, grad_low, (((0,), (0,)), ((), ())), preferred_element_type=jnp.float32
    )
    local_bias = jnp.sum(grad_pre, axis=0)
    grad_agg = transposed_product(grad_low, weight)
    packed = pack_grads(local_weight, local_bias)
    rows_count = lax.axis_size("row")
    row_pieces = packed.reshape((rows_count, packed.shape[0] // rows_count) + packed.shape[1:])
    grad_stack, by_row_pieces = gather_and_exchange(grad_agg, row_pieces, "col", 0)
    grad_panel = grad_stack.reshape(-1, width)
    by_row = jnp.sum(by_row_pieces, axis=0)
    back = slot_product(tile_values, tile_rows, tile_cols, live_count, grad_panel, col_len, True)
    back_low = back.astype(jnp.bfloat16).reshape(col_len // own_nodes, own_nodes, width)
    parts = by_row.reshape((by_row.shape[0], 1) + by_row.shape[1:])
    received, _, gathered_rows = back_exchange(back_low, parts, 1)
    every = gathered_rows.reshape(gathered_rows.shape[0], gathered_rows.shape[1], -1)
    feature_grad = jnp.sum(received.astype(jnp.float32), axis=0).astype(jnp.bfloat16)
    weight_grad, bias_grad = unpack_grads(every, width)
    return (hidden, weight_grad, bias_grad, feature_grad)


def solution(mesh):
    in_specs = (
        P(("col", "row"), None),
        P("row", "col", None, None, None),
        P("row", "col", None),
        P("row", "col", None),
        P("row", "col"),
        P(),
        P(),
        P(("row", "col"), None),
    )
    out_specs = (P(("row", "col"), None), P(), P(), P(("col", "row"), None))
    return jax.shard_map(
        per_device, mesh=mesh, in_specs=in_specs, out_specs=out_specs, check_vma=False
    )
```

```python
import functools

import jax
import jax.numpy as jnp
from jax import lax
from jax.experimental import pallas as pl
from jax.experimental.pallas import tpu as pltpu
from jax.sharding import PartitionSpec as P

MESH_ID = pl.DeviceIdType.MESH


def _exchange_kernel(axis, other, n, broadcast, src_ref, out_ref, send_sem, recv_sem, own_sem):
    me = lax.axis_index(axis)
    there = lax.axis_index(other)

    def device(k):
        return (k, there) if axis == "row" else (there, k)

    def piece(k):
        return src_ref if broadcast else src_ref.at[k]

    barrier = pltpu.get_barrier_semaphore()

    def greet(step, carry):
        peer = lax.rem(me + step, n)
        pl.semaphore_signal(barrier, inc=1, device_id=device(peer), device_id_type=MESH_ID)
        return carry

    lax.fori_loop(1, n, greet, 0)
    pl.semaphore_wait(barrier, n - 1)

    own = pltpu.make_async_copy(piece(me), out_ref.at[me], own_sem)
    own.start()

    def send(step, carry):
        peer = lax.rem(me + step, n)
        pltpu.make_async_remote_copy(
            src_ref=piece(peer), dst_ref=out_ref.at[me], send_sem=send_sem.at[step],
            recv_sem=recv_sem.at[step], device_id=device(peer), device_id_type=MESH_ID,
        ).start()
        return carry

    lax.fori_loop(1, n, send, 0)

    def finish(step, carry):
        peer = lax.rem(me + step, n)
        source = lax.rem(me + n - step, n)
        pltpu.make_async_remote_copy(
            src_ref=piece(peer), dst_ref=out_ref.at[me], send_sem=send_sem.at[step],
            recv_sem=recv_sem.at[step], device_id=device(peer), device_id_type=MESH_ID,
        ).wait_send()
        pltpu.make_async_remote_copy(
            src_ref=piece(source), dst_ref=out_ref.at[source], send_sem=send_sem.at[step],
            recv_sem=recv_sem.at[step], device_id=device(source), device_id_type=MESH_ID,
        ).wait_recv()
        return carry

    lax.fori_loop(1, n, finish, 0)
    own.wait()


def _steps_kernel(axis, other, n, first, stride, count, src_ref, out_ref, send_sem, recv_sem, own_sem):
    me = lax.axis_index(axis)
    there = lax.axis_index(other)
    begin = 1 if first == 0 else 0

    def device(k):
        return (k, there) if axis == "row" else (there, k)

    def copy(slot, peer, piece):
        return pltpu.make_async_remote_copy(
            src_ref=src_ref.at[piece], dst_ref=out_ref.at[slot], send_sem=send_sem.at[slot],
            recv_sem=recv_sem.at[slot], device_id=device(peer), device_id_type=MESH_ID,
        )

    barrier = pltpu.get_barrier_semaphore()

    def greet(slot, carry):
        step = first + stride * slot
        for peer in (lax.rem(me + step, n), lax.rem(me + n - step, n)):
            pl.semaphore_signal(barrier, inc=1, device_id=device(peer), device_id_type=MESH_ID)
        return carry

    lax.fori_loop(begin, count, greet, 0)
    pl.semaphore_wait(barrier, 2 * (count - begin))
    if first == 0:
        own = pltpu.make_async_copy(src_ref.at[me], out_ref.at[0], own_sem)
        own.start()

    def send(slot, carry):
        peer = lax.rem(me + first + stride * slot, n)
        copy(slot, peer, peer).start()
        return carry

    lax.fori_loop(begin, count, send, 0)

    def finish(slot, carry):
        step = first + stride * slot
        peer = lax.rem(me + step, n)
        copy(slot, peer, peer).wait_send()
        source = lax.rem(me + n - step, n)
        copy(slot, source, me).wait_recv()
        return carry

    lax.fori_loop(begin, count, finish, 0)
    if first == 0:
        own.wait()


def exchange_steps(pieces, axis, first, stride, ident):
    n = lax.axis_size(axis)
    count = (n - first + stride - 1) // stride
    other = "col" if axis == "row" else "row"
    shape = (count,) + pieces.shape[1:]
    return pl.pallas_call(
        functools.partial(_steps_kernel, axis, other, n, first, stride, count),
        out_shape=jax.ShapeDtypeStruct(shape, pieces.dtype),
        in_specs=[pl.BlockSpec(memory_space=pl.ANY)],
        out_specs=pl.BlockSpec(memory_space=pl.ANY),
        scratch_shapes=[
            pltpu.SemaphoreType.DMA((count,)),
            pltpu.SemaphoreType.DMA((count,)),
            pltpu.SemaphoreType.DMA(()),
        ],
        compiler_params=pltpu.CompilerParams(collective_id=ident, has_side_effects=True),
        cost_estimate=pl.CostEstimate(
            flops=0, transcendentals=0, bytes_accessed=2 * count * pieces[0].size * pieces.dtype.itemsize
        ),
    )(pieces)


def _gather_steps_kernel(
    axis, other, n, m, src_ref, pieces_ref, out_ref, pieces_out,
    send_sem, recv_sem, own_sem, piece_send, piece_recv, piece_own,
):
    me = lax.axis_index(axis)
    there = lax.axis_index(other)

    def device(k):
        return (k, there) if axis == "row" else (there, k)

    def across(k):
        return (me, k) if axis == "row" else (k, me)

    def gather_copy(step, peer, slot):
        return pltpu.make_async_remote_copy(
            src_ref=src_ref, dst_ref=out_ref.at[slot], send_sem=send_sem.at[step],
            recv_sem=recv_sem.at[step], device_id=device(peer), device_id_type=MESH_ID,
        )

    def piece_copy(step, peer, piece):
        return pltpu.make_async_remote_copy(
            src_ref=pieces_ref.at[piece], dst_ref=pieces_out.at[step], send_sem=piece_send.at[step],
            recv_sem=piece_recv.at[step], device_id=across(peer), device_id_type=MESH_ID,
        )

    barrier = pltpu.get_barrier_semaphore()

    def greet(step, carry):
        pl.semaphore_signal(barrier, inc=1, device_id=device(lax.rem(me + step, n)), device_id_type=MESH_ID)
        return carry

    def greet_across(step, carry):
        pl.semaphore_signal(barrier, inc=1, device_id=across(lax.rem(there + step, m)), device_id_type=MESH_ID)
        return carry

    lax.fori_loop(1, n, greet, 0)
    lax.fori_loop(1, m, greet_across, 0)
    pl.semaphore_wait(barrier, n - 1 + m - 1)
    own = pltpu.make_async_copy(src_ref, out_ref.at[me], own_sem)
    own.start()
    own_piece = pltpu.make_async_copy(pieces_ref.at[there], pieces_out.at[0], piece_own)
    own_piece.start()

    def send(step, carry):
        gather_copy(step, lax.rem(me + step, n), me).start()
        return carry

    def send_across(step, carry):
        peer = lax.rem(there + step, m)
        piece_copy(step, peer, peer).start()
        return carry

    lax.fori_loop(1, m, send_across, 0)
    lax.fori_loop(1, n, send, 0)

    def finish(step, carry):
        gather_copy(step, lax.rem(me + step, n), me).wait_send()
        source = lax.rem(me + n - step, n)
        gather_copy(step, source, source).wait_recv()
        return carry

    def finish_across(step, carry):
        peer = lax.rem(there + step, m)
        piece_copy(step, peer, peer).wait_send()
        source = lax.rem(there + m - step, m)
        piece_copy(step, source, there).wait_recv()
        return carry

    lax.fori_loop(1, n, finish, 0)
    lax.fori_loop(1, m, finish_across, 0)
    own.wait()
    own_piece.wait()


def gather_and_exchange(x, pieces, axis, ident):
    n = lax.axis_size(axis)
    other = "col" if axis == "row" else "row"
    m = lax.axis_size(other)
    shapes = (
        jax.ShapeDtypeStruct((n,) + x.shape, x.dtype),
        jax.ShapeDtypeStruct(pieces.shape, pieces.dtype),
    )
    moved = 2 * n * x.size * x.dtype.itemsize + 2 * pieces.size * pieces.dtype.itemsize
    return pl.pallas_call(
        functools.partial(_gather_steps_kernel, axis, other, n, m),
        out_shape=shapes,
        in_specs=[pl.BlockSpec(memory_space=pl.ANY), pl.BlockSpec(memory_space=pl.ANY)],
        out_specs=(pl.BlockSpec(memory_space=pl.ANY), pl.BlockSpec(memory_space=pl.ANY)),
        scratch_shapes=[
            pltpu.SemaphoreType.DMA((n,)),
            pltpu.SemaphoreType.DMA((n,)),
            pltpu.SemaphoreType.DMA(()),
            pltpu.SemaphoreType.DMA((m,)),
            pltpu.SemaphoreType.DMA((m,)),
            pltpu.SemaphoreType.DMA(()),
        ],
        compiler_params=pltpu.CompilerParams(collective_id=ident, has_side_effects=True),
        cost_estimate=pl.CostEstimate(flops=0, transcendentals=0, bytes_accessed=moved),
    )(x, pieces)


def _back_kernel(
    n, m, src_ref, part_ref, out_ref, row_buf, col_buf,
    send_sem, recv_sem, own_sem, a_send, a_recv, a_own, b_send, b_recv, b_own,
    c_send, c_recv, c_own, part_buf, w_ref,
):
    me = lax.axis_index("row")
    there = lax.axis_index("col")

    def along(k):
        return (k, there)

    def across(k):
        return (me, k)

    def main_copy(step, peer, piece):
        return pltpu.make_async_remote_copy(
            src_ref=src_ref.at[piece], dst_ref=out_ref.at[step], send_sem=send_sem.at[step],
            recv_sem=recv_sem.at[step], device_id=along(peer), device_id_type=MESH_ID,
        )

    def row_copy(step, peer, slot):
        return pltpu.make_async_remote_copy(
            src_ref=w_ref, dst_ref=row_buf.at[slot], send_sem=a_send.at[step],
            recv_sem=a_recv.at[step], device_id=along(peer), device_id_type=MESH_ID,
        )

    def col_copy(step, peer, slot):
        return pltpu.make_async_remote_copy(
            src_ref=row_buf, dst_ref=col_buf.at[slot], send_sem=b_send.at[step],
            recv_sem=b_recv.at[step], device_id=across(peer), device_id_type=MESH_ID,
        )

    def part_copy(step, peer):
        return pltpu.make_async_remote_copy(
            src_ref=part_ref.at[peer], dst_ref=part_buf.at[step], send_sem=c_send.at[step],
            recv_sem=c_recv.at[step], device_id=across(peer), device_id_type=MESH_ID,
        )

    barrier = pltpu.get_barrier_semaphore()

    def greet(step, carry):
        pl.semaphore_signal(barrier, inc=1, device_id=along(lax.rem(me + step, n)), device_id_type=MESH_ID)
        return carry

    def greet_across(step, carry):
        pl.semaphore_signal(barrier, inc=1, device_id=across(lax.rem(there + step, m)), device_id_type=MESH_ID)
        return carry

    lax.fori_loop(1, n, greet, 0)
    lax.fori_loop(1, m, greet_across, 0)
    pl.semaphore_wait(barrier, n - 1 + m - 1)
    own = pltpu.make_async_copy(src_ref.at[me], out_ref.at[0], own_sem)
    own.start()
    own_part = pltpu.make_async_copy(part_ref.at[there], part_buf.at[0], c_own)
    own_part.start()

    def send_part(step, carry):
        part_copy(step, lax.rem(there + step, m)).start()
        return carry

    def send_main(step, carry):
        peer = lax.rem(me + step, n)
        main_copy(step, peer, peer).start()
        return carry

    lax.fori_loop(1, m, send_part, 0)
    lax.fori_loop(0, n // 4, lambda i, c: send_main(2 + 4 * i, c), 0)

    def finish_part(step, carry):
        part_copy(step, lax.rem(there + step, m)).wait_send()
        part_copy(step, lax.rem(there + m - step, m)).wait_recv()
        return carry

    lax.fori_loop(1, m, finish_part, 0)
    own_part.wait()
    w_ref[...] = jnp.sum(part_buf[...], axis=0)
    own_row = pltpu.make_async_copy(w_ref, row_buf.at[me], a_own)
    own_row.start()

    def send_row(step, carry):
        row_copy(step, lax.rem(me + step, n), me).start()
        return carry

    lax.fori_loop(1, n, send_row, 0)
    lax.fori_loop(0, n // 2, lambda i, c: send_main(1 + 2 * i, c), 0)
    lax.fori_loop(1, n // 4, lambda i, c: send_main(4 * i, c), 0)

    def finish_row(step, carry):
        row_copy(step, lax.rem(me + step, n), me).wait_send()
        source = lax.rem(me + n - step, n)
        row_copy(step, source, source).wait_recv()
        return carry

    lax.fori_loop(1, n, finish_row, 0)
    own_row.wait()
    own_col = pltpu.make_async_copy(row_buf, col_buf.at[there], b_own)
    own_col.start()

    def send_col(step, carry):
        col_copy(step, lax.rem(there + step, m), there).start()
        return carry

    lax.fori_loop(1, m, send_col, 0)

    def finish_main(step, carry):
        peer = lax.rem(me + step, n)
        main_copy(step, peer, peer).wait_send()
        source = lax.rem(me + n - step, n)
        main_copy(step, source, me).wait_recv()
        return carry

    lax.fori_loop(1, n, finish_main, 0)

    def finish_col(step, carry):
        col_copy(step, lax.rem(there + step, m), there).wait_send()
        source = lax.rem(there + m - step, m)
        col_copy(step, source, source).wait_recv()
        return carry

    lax.fori_loop(1, m, finish_col, 0)
    own_col.wait()
    own.wait()


def back_exchange(pieces, parts, ident):
    n = lax.axis_size("row")
    m = lax.axis_size("col")
    row = parts[0]
    shapes = (
        jax.ShapeDtypeStruct(pieces.shape, pieces.dtype),
        jax.ShapeDtypeStruct((n,) + row.shape, row.dtype),
        jax.ShapeDtypeStruct((m, n) + row.shape, row.dtype),
    )
    moved = 2 * pieces.size * pieces.dtype.itemsize + 2 * m * n * row.size * row.dtype.itemsize
    return pl.pallas_call(
        functools.partial(_back_kernel, n, m),
        out_shape=shapes,
        in_specs=[pl.BlockSpec(memory_space=pl.ANY), pl.BlockSpec(memory_space=pl.ANY)],
        out_specs=tuple(pl.BlockSpec(memory_space=pl.ANY) for _ in range(3)),
        scratch_shapes=[
            pltpu.SemaphoreType.DMA((n,)),
            pltpu.SemaphoreType.DMA((n,)),
            pltpu.SemaphoreType.DMA(()),
            pltpu.SemaphoreType.DMA((n,)),
            pltpu.SemaphoreType.DMA((n,)),
            pltpu.SemaphoreType.DMA(()),
            pltpu.SemaphoreType.DMA((m,)),
            pltpu.SemaphoreType.DMA((m,)),
            pltpu.SemaphoreType.DMA(()),
            pltpu.SemaphoreType.DMA((m,)),
            pltpu.SemaphoreType.DMA((m,)),
            pltpu.SemaphoreType.DMA(()),
            pltpu.VMEM(parts.shape, parts.dtype),
            pltpu.VMEM(row.shape, row.dtype),
        ],
        compiler_params=pltpu.CompilerParams(collective_id=ident, has_side_effects=True),
        cost_estimate=pl.CostEstimate(flops=0, transcendentals=0, bytes_accessed=moved),
    )(pieces, parts)


def exchange(x, axis, broadcast, ident):
    n = lax.axis_size(axis)
    other = "col" if axis == "row" else "row"
    shape = (n,) + (x.shape if broadcast else x.shape[1:])
    return pl.pallas_call(
        functools.partial(_exchange_kernel, axis, other, n, broadcast),
        out_shape=jax.ShapeDtypeStruct(shape, x.dtype),
        in_specs=[pl.BlockSpec(memory_space=pl.ANY)],
        out_specs=pl.BlockSpec(memory_space=pl.ANY),
        scratch_shapes=[
            pltpu.SemaphoreType.DMA((n,)),
            pltpu.SemaphoreType.DMA((n,)),
            pltpu.SemaphoreType.DMA(()),
        ],
        compiler_params=pltpu.CompilerParams(collective_id=ident, has_side_effects=True),
        cost_estimate=pl.CostEstimate(
            flops=0, transcendentals=0, bytes_accessed=2 * n * x.size * x.dtype.itemsize
        ),
    )(x)


def _slot_kernel(backward, slots, src_ids, tgt_ids, count_ref, vals_ref, src_ref, out_ref, acc_ref):
    s = pl.program_id(0)

    @pl.when(s == 0)
    def _():
        acc_ref[...] = jnp.zeros_like(acc_ref)

    @pl.when(s < count_ref[0])
    def _():
        block = vals_ref[0]
        segment = src_ref[0]
        if backward:
            dims = (((0,), (0,)), ((), ()))
        else:
            dims = (((1,), (0,)), ((), ()))
        product = lax.dot_general(block, segment, dims, preferred_element_type=jnp.float32)
        target = tgt_ids[s]
        acc_ref[target] = acc_ref[target] + product

    @pl.when(s == slots - 1)
    def _():
        out_ref[...] = acc_ref[...].astype(out_ref.dtype)


def slot_product(tile_values, tile_rows, tile_cols, live_count, source, out_len, backward):
    slots, block_size = tile_values.shape[0], tile_values.shape[1]
    width = source.shape[1]
    n_src = source.shape[0] // block_size
    n_out = out_len // block_size
    panels = source.reshape(n_src, block_size, width)
    if backward:
        src_ids, tgt_ids = tile_rows, tile_cols
    else:
        src_ids, tgt_ids = tile_cols, tile_rows
    src_ids = jnp.clip(src_ids, 0, n_src - 1).astype(jnp.int32)
    tgt_ids = jnp.clip(tgt_ids, 0, n_out - 1).astype(jnp.int32)
    count = jnp.reshape(live_count, (1,)).astype(jnp.int32)
    grid_spec = pltpu.PrefetchScalarGridSpec(
        num_scalar_prefetch=3,
        grid=(slots,),
        in_specs=[
            pl.BlockSpec((1, block_size, block_size), lambda s, src, tgt, cnt: (s, 0, 0)),
            pl.BlockSpec((1, block_size, width), lambda s, src, tgt, cnt: (src[s], 0, 0)),
        ],
        out_specs=pl.BlockSpec((n_out, block_size, width), lambda s, src, tgt, cnt: (0, 0, 0)),
        scratch_shapes=[pltpu.VMEM((n_out, block_size, width), jnp.float32)],
    )
    out = pl.pallas_call(
        functools.partial(_slot_kernel, backward, slots),
        out_shape=jax.ShapeDtypeStruct((n_out, block_size, width), jnp.bfloat16),
        grid_spec=grid_spec,
        compiler_params=pltpu.CompilerParams(
            dimension_semantics=("arbitrary",), vmem_limit_bytes=48 * 1024 * 1024
        ),
        cost_estimate=pl.CostEstimate(
            flops=2 * slots * block_size * block_size * width,
            transcendentals=0,
            bytes_accessed=2 * (slots * block_size * (block_size + width) + n_out * block_size * width),
        ),
    )(src_ids, tgt_ids, count, tile_values, panels)
    return out.reshape(out_len, width)


def gather_rows(x, axis):
    count = lax.axis_size(axis)
    stacked = jnp.broadcast_to(x[None], (count,) + x.shape)
    received = lax.all_to_all(stacked, axis, split_axis=0, concat_axis=0, tiled=True)
    return received.reshape((count * x.shape[0],) + x.shape[1:])


def scatter_sum(x, axis):
    count = lax.axis_size(axis)
    pieces = x.reshape((count, x.shape[0] // count) + x.shape[1:])
    received = lax.all_to_all(pieces, axis, split_axis=0, concat_axis=0, tiled=True)
    return jnp.sum(received.astype(jnp.float32), axis=0)


def pack_grads(local_weight, local_bias):
    pad = jnp.zeros((local_weight.shape[0], 127), jnp.float32)
    return jnp.concatenate([local_weight, local_bias[:, None], pad], axis=1)


def unpack_grads(by_col_then_row, width):
    cols, rows = by_col_then_row.shape[0], by_col_then_row.shape[1]
    whole = by_col_then_row.transpose(1, 0, 2).reshape(cols * rows, -1)
    return whole[:, :width], whole[:, width]


def transposed_product(left, weight):
    return lax.dot_general(
        left, weight, (((1,), (1,)), ((), ())), preferred_element_type=jnp.float32
    ).astype(jnp.bfloat16)


def source_total(received):
    return jnp.sum(received.astype(jnp.float32), axis=0).astype(jnp.bfloat16)


def per_device(
    features, block_values, block_rows, block_cols, block_count, weight, bias, cotangent
):
    tile_values = block_values[0, 0]
    tile_rows = block_rows[0, 0]
    tile_cols = block_cols[0, 0]
    live_count = block_count[0, 0]
    own_nodes = features.shape[0]
    width = features.shape[1]
    row_len = lax.axis_size("col") * own_nodes
    gathered = exchange(features, "row", True, 4).reshape(-1, width)
    col_len = gathered.shape[0]
    partial_value = slot_product(
        tile_values, tile_rows, tile_cols, live_count, gathered, row_len, False
    )
    pieces = partial_value.reshape(lax.axis_size("col"), own_nodes, width)
    received = exchange_steps(pieces, "col", 0, 1, 2)
    aggregate = jnp.sum(received.astype(jnp.float32), axis=0).astype(jnp.bfloat16)
    preact = jnp.dot(aggregate, weight, preferred_element_type=jnp.float32) + bias
    hidden = jax.nn.silu(preact).astype(jnp.bfloat16)
    sigma = jax.nn.sigmoid(preact)
    grad_pre = cotangent.astype(jnp.float32) * sigma * (1.0 + preact * (1.0 - sigma))
    grad_low = grad_pre.astype(jnp.bfloat16)
    local_weight = lax.dot_general(
        aggregate, grad_low, (((0,), (0,)), ((), ())), preferred_element_type=jnp.float32
    )
    local_bias = jnp.sum(grad_pre, axis=0)
    grad_agg = transposed_product(grad_low, weight)
    packed = pack_grads(local_weight, local_bias)
    rows_count = lax.axis_size("row")
    row_pieces = packed.reshape((rows_count, packed.shape[0] // rows_count) + packed.shape[1:])
    grad_stack, by_row_pieces = gather_and_exchange(grad_agg, row_pieces, "col", 0)
    grad_panel = grad_stack.reshape(-1, width)
    by_row = jnp.sum(by_row_pieces, axis=0)
    back = slot_product(tile_values, tile_rows, tile_cols, live_count, grad_panel, col_len, True)
    back_low = back.astype(jnp.bfloat16).reshape(col_len // own_nodes, own_nodes, width)
    parts = by_row.reshape((by_row.shape[0], 1) + by_row.shape[1:])
    received, _, gathered_rows = back_exchange(back_low, parts, 1)
    every = gathered_rows.reshape(gathered_rows.shape[0], gathered_rows.shape[1], -1)
    feature_grad = jnp.sum(received.astype(jnp.float32), axis=0).astype(jnp.bfloat16)
    weight_grad, bias_grad = unpack_grads(every, width)
    return (hidden, weight_grad, bias_grad, feature_grad)


def solution(mesh):
    in_specs = (
        P(("col", "row"), None),
        P("row", "col", None, None, None),
        P("row", "col", None),
        P("row", "col", None),
        P("row", "col"),
        P(),
        P(),
        P(("row", "col"), None),
    )
    out_specs = (P(("row", "col"), None), P(), P(), P(("col", "row"), None))
    return jax.shard_map(
        per_device, mesh=mesh, in_specs=in_specs, out_specs=out_specs, check_vma=False
    )
```

```python
import functools

import jax
import jax.numpy as jnp
from jax import lax
from jax.experimental import pallas as pl
from jax.experimental.pallas import tpu as pltpu
from jax.sharding import PartitionSpec as P

MESH_ID = pl.DeviceIdType.MESH


def _exchange_kernel(axis, other, n, broadcast, src_ref, out_ref, send_sem, recv_sem, own_sem):
    me = lax.axis_index(axis)
    there = lax.axis_index(other)

    def device(k):
        return (k, there) if axis == "row" else (there, k)

    def piece(k):
        return src_ref if broadcast else src_ref.at[k]

    barrier = pltpu.get_barrier_semaphore()

    def greet(step, carry):
        peer = lax.rem(me + step, n)
        pl.semaphore_signal(barrier, inc=1, device_id=device(peer), device_id_type=MESH_ID)
        return carry

    lax.fori_loop(1, n, greet, 0)
    pl.semaphore_wait(barrier, n - 1)

    own = pltpu.make_async_copy(piece(me), out_ref.at[me], own_sem)
    own.start()

    def send(step, carry):
        peer = lax.rem(me + step, n)
        pltpu.make_async_remote_copy(
            src_ref=piece(peer), dst_ref=out_ref.at[me], send_sem=send_sem.at[step],
            recv_sem=recv_sem.at[step], device_id=device(peer), device_id_type=MESH_ID,
        ).start()
        return carry

    lax.fori_loop(1, n, send, 0)

    def finish(step, carry):
        peer = lax.rem(me + step, n)
        source = lax.rem(me + n - step, n)
        pltpu.make_async_remote_copy(
            src_ref=piece(peer), dst_ref=out_ref.at[me], send_sem=send_sem.at[step],
            recv_sem=recv_sem.at[step], device_id=device(peer), device_id_type=MESH_ID,
        ).wait_send()
        pltpu.make_async_remote_copy(
            src_ref=piece(source), dst_ref=out_ref.at[source], send_sem=send_sem.at[step],
            recv_sem=recv_sem.at[step], device_id=device(source), device_id_type=MESH_ID,
        ).wait_recv()
        return carry

    lax.fori_loop(1, n, finish, 0)
    own.wait()


def _steps_kernel(axis, other, n, first, stride, count, src_ref, out_ref, send_sem, recv_sem, own_sem):
    me = lax.axis_index(axis)
    there = lax.axis_index(other)
    begin = 1 if first == 0 else 0

    def device(k):
        return (k, there) if axis == "row" else (there, k)

    def copy(slot, peer, piece):
        return pltpu.make_async_remote_copy(
            src_ref=src_ref.at[piece], dst_ref=out_ref.at[slot], send_sem=send_sem.at[slot],
            recv_sem=recv_sem.at[slot], device_id=device(peer), device_id_type=MESH_ID,
        )

    barrier = pltpu.get_barrier_semaphore()

    def greet(slot, carry):
        step = first + stride * slot
        for peer in (lax.rem(me + step, n), lax.rem(me + n - step, n)):
            pl.semaphore_signal(barrier, inc=1, device_id=device(peer), device_id_type=MESH_ID)
        return carry

    lax.fori_loop(begin, count, greet, 0)
    pl.semaphore_wait(barrier, 2 * (count - begin))
    if first == 0:
        own = pltpu.make_async_copy(src_ref.at[me], out_ref.at[0], own_sem)
        own.start()

    def send(slot, carry):
        peer = lax.rem(me + first + stride * slot, n)
        copy(slot, peer, peer).start()
        return carry

    lax.fori_loop(begin, count, send, 0)

    def finish(slot, carry):
        step = first + stride * slot
        peer = lax.rem(me + step, n)
        copy(slot, peer, peer).wait_send()
        source = lax.rem(me + n - step, n)
        copy(slot, source, me).wait_recv()
        return carry

    lax.fori_loop(begin, count, finish, 0)
    if first == 0:
        own.wait()


def exchange_steps(pieces, axis, first, stride, ident):
    n = lax.axis_size(axis)
    count = (n - first + stride - 1) // stride
    other = "col" if axis == "row" else "row"
    shape = (count,) + pieces.shape[1:]
    return pl.pallas_call(
        functools.partial(_steps_kernel, axis, other, n, first, stride, count),
        out_shape=jax.ShapeDtypeStruct(shape, pieces.dtype),
        in_specs=[pl.BlockSpec(memory_space=pl.ANY)],
        out_specs=pl.BlockSpec(memory_space=pl.ANY),
        scratch_shapes=[
            pltpu.SemaphoreType.DMA((count,)),
            pltpu.SemaphoreType.DMA((count,)),
            pltpu.SemaphoreType.DMA(()),
        ],
        compiler_params=pltpu.CompilerParams(collective_id=ident, has_side_effects=True),
        cost_estimate=pl.CostEstimate(
            flops=0, transcendentals=0, bytes_accessed=2 * count * pieces[0].size * pieces.dtype.itemsize
        ),
    )(pieces)


def _gather_steps_kernel(
    axis, other, n, m, src_ref, pieces_ref, out_ref, pieces_out,
    send_sem, recv_sem, own_sem, piece_send, piece_recv, piece_own,
):
    me = lax.axis_index(axis)
    there = lax.axis_index(other)

    def device(k):
        return (k, there) if axis == "row" else (there, k)

    def across(k):
        return (me, k) if axis == "row" else (k, me)

    def gather_copy(step, peer, slot):
        return pltpu.make_async_remote_copy(
            src_ref=src_ref, dst_ref=out_ref.at[slot], send_sem=send_sem.at[step],
            recv_sem=recv_sem.at[step], device_id=device(peer), device_id_type=MESH_ID,
        )

    def piece_copy(step, peer, piece):
        return pltpu.make_async_remote_copy(
            src_ref=pieces_ref.at[piece], dst_ref=pieces_out.at[step], send_sem=piece_send.at[step],
            recv_sem=piece_recv.at[step], device_id=across(peer), device_id_type=MESH_ID,
        )

    barrier = pltpu.get_barrier_semaphore()

    def greet(step, carry):
        pl.semaphore_signal(barrier, inc=1, device_id=device(lax.rem(me + step, n)), device_id_type=MESH_ID)
        return carry

    def greet_across(step, carry):
        pl.semaphore_signal(barrier, inc=1, device_id=across(lax.rem(there + step, m)), device_id_type=MESH_ID)
        return carry

    lax.fori_loop(1, n, greet, 0)
    lax.fori_loop(1, m, greet_across, 0)
    pl.semaphore_wait(barrier, n - 1 + m - 1)
    own = pltpu.make_async_copy(src_ref, out_ref.at[me], own_sem)
    own.start()
    own_piece = pltpu.make_async_copy(pieces_ref.at[there], pieces_out.at[0], piece_own)
    own_piece.start()

    def send(step, carry):
        gather_copy(step, lax.rem(me + step, n), me).start()
        return carry

    def send_across(step, carry):
        peer = lax.rem(there + step, m)
        piece_copy(step, peer, peer).start()
        return carry

    lax.fori_loop(1, m, send_across, 0)
    lax.fori_loop(1, n, send, 0)

    def finish(step, carry):
        gather_copy(step, lax.rem(me + step, n), me).wait_send()
        source = lax.rem(me + n - step, n)
        gather_copy(step, source, source).wait_recv()
        return carry

    def finish_across(step, carry):
        peer = lax.rem(there + step, m)
        piece_copy(step, peer, peer).wait_send()
        source = lax.rem(there + m - step, m)
        piece_copy(step, source, there).wait_recv()
        return carry

    lax.fori_loop(1, n, finish, 0)
    lax.fori_loop(1, m, finish_across, 0)
    own.wait()
    own_piece.wait()


def gather_and_exchange(x, pieces, axis, ident):
    n = lax.axis_size(axis)
    other = "col" if axis == "row" else "row"
    m = lax.axis_size(other)
    shapes = (
        jax.ShapeDtypeStruct((n,) + x.shape, x.dtype),
        jax.ShapeDtypeStruct(pieces.shape, pieces.dtype),
    )
    moved = 2 * n * x.size * x.dtype.itemsize + 2 * pieces.size * pieces.dtype.itemsize
    return pl.pallas_call(
        functools.partial(_gather_steps_kernel, axis, other, n, m),
        out_shape=shapes,
        in_specs=[pl.BlockSpec(memory_space=pl.ANY), pl.BlockSpec(memory_space=pl.ANY)],
        out_specs=(pl.BlockSpec(memory_space=pl.ANY), pl.BlockSpec(memory_space=pl.ANY)),
        scratch_shapes=[
            pltpu.SemaphoreType.DMA((n,)),
            pltpu.SemaphoreType.DMA((n,)),
            pltpu.SemaphoreType.DMA(()),
            pltpu.SemaphoreType.DMA((m,)),
            pltpu.SemaphoreType.DMA((m,)),
            pltpu.SemaphoreType.DMA(()),
        ],
        compiler_params=pltpu.CompilerParams(collective_id=ident, has_side_effects=True),
        cost_estimate=pl.CostEstimate(flops=0, transcendentals=0, bytes_accessed=moved),
    )(x, pieces)


def _back_kernel(
    n, m, src_ref, part_ref, out_ref, row_buf, col_buf,
    send_sem, recv_sem, own_sem, a_send, a_recv, a_own, b_send, b_recv, b_own,
    c_send, c_recv, c_own, part_buf, w_ref,
):
    me = lax.axis_index("row")
    there = lax.axis_index("col")

    def along(k):
        return (k, there)

    def across(k):
        return (me, k)

    def main_copy(step, peer, piece):
        return pltpu.make_async_remote_copy(
            src_ref=src_ref.at[piece], dst_ref=out_ref.at[step], send_sem=send_sem.at[step],
            recv_sem=recv_sem.at[step], device_id=along(peer), device_id_type=MESH_ID,
        )

    def row_copy(step, peer, slot):
        return pltpu.make_async_remote_copy(
            src_ref=w_ref, dst_ref=row_buf.at[slot], send_sem=a_send.at[step],
            recv_sem=a_recv.at[step], device_id=along(peer), device_id_type=MESH_ID,
        )

    def col_copy(step, peer, slot):
        return pltpu.make_async_remote_copy(
            src_ref=row_buf, dst_ref=col_buf.at[slot], send_sem=b_send.at[step],
            recv_sem=b_recv.at[step], device_id=across(peer), device_id_type=MESH_ID,
        )

    def part_copy(step, peer):
        return pltpu.make_async_remote_copy(
            src_ref=part_ref.at[peer], dst_ref=part_buf.at[step], send_sem=c_send.at[step],
            recv_sem=c_recv.at[step], device_id=across(peer), device_id_type=MESH_ID,
        )

    barrier = pltpu.get_barrier_semaphore()

    def greet(step, carry):
        pl.semaphore_signal(barrier, inc=1, device_id=along(lax.rem(me + step, n)), device_id_type=MESH_ID)
        return carry

    def greet_across(step, carry):
        pl.semaphore_signal(barrier, inc=1, device_id=across(lax.rem(there + step, m)), device_id_type=MESH_ID)
        return carry

    lax.fori_loop(1, n, greet, 0)
    lax.fori_loop(1, m, greet_across, 0)
    pl.semaphore_wait(barrier, n - 1 + m - 1)
    own = pltpu.make_async_copy(src_ref.at[me], out_ref.at[0], own_sem)
    own.start()
    own_part = pltpu.make_async_copy(part_ref.at[there], part_buf.at[0], c_own)
    own_part.start()

    def send_part(step, carry):
        part_copy(step, lax.rem(there + step, m)).start()
        return carry

    def send_main(step, carry):
        peer = lax.rem(me + step, n)
        main_copy(step, peer, peer).start()
        return carry

    lax.fori_loop(1, m, send_part, 0)
    lax.fori_loop(0, n // 2, lambda i, c: send_main(1 + 2 * i, c), 0)
    lax.fori_loop(0, n // 4, lambda i, c: send_main(2 + 4 * i, c), 0)

    def finish_part(step, carry):
        part_copy(step, lax.rem(there + step, m)).wait_send()
        part_copy(step, lax.rem(there + m - step, m)).wait_recv()
        return carry

    lax.fori_loop(1, m, finish_part, 0)
    own_part.wait()
    w_ref[...] = jnp.sum(part_buf[...], axis=0)
    own_row = pltpu.make_async_copy(w_ref, row_buf.at[me], a_own)
    own_row.start()

    def send_row(step, carry):
        row_copy(step, lax.rem(me + step, n), me).start()
        return carry

    lax.fori_loop(1, n, send_row, 0)
    lax.fori_loop(1, n // 4, lambda i, c: send_main(4 * i, c), 0)

    def finish_row(step, carry):
        row_copy(step, lax.rem(me + step, n), me).wait_send()
        source = lax.rem(me + n - step, n)
        row_copy(step, source, source).wait_recv()
        return carry

    lax.fori_loop(1, n, finish_row, 0)
    own_row.wait()
    own_col = pltpu.make_async_copy(row_buf, col_buf.at[there], b_own)
    own_col.start()

    def send_col(step, carry):
        col_copy(step, lax.rem(there + step, m), there).start()
        return carry

    lax.fori_loop(1, m, send_col, 0)

    def finish_main(step, carry):
        peer = lax.rem(me + step, n)
        main_copy(step, peer, peer).wait_send()
        source = lax.rem(me + n - step, n)
        main_copy(step, source, me).wait_recv()
        return carry

    lax.fori_loop(1, n, finish_main, 0)

    def finish_col(step, carry):
        col_copy(step, lax.rem(there + step, m), there).wait_send()
        source = lax.rem(there + m - step, m)
        col_copy(step, source, source).wait_recv()
        return carry

    lax.fori_loop(1, m, finish_col, 0)
    own_col.wait()
    own.wait()


def back_exchange(pieces, parts, ident):
    n = lax.axis_size("row")
    m = lax.axis_size("col")
    row = parts[0]
    shapes = (
        jax.ShapeDtypeStruct(pieces.shape, pieces.dtype),
        jax.ShapeDtypeStruct((n,) + row.shape, row.dtype),
        jax.ShapeDtypeStruct((m, n) + row.shape, row.dtype),
    )
    moved = 2 * pieces.size * pieces.dtype.itemsize + 2 * m * n * row.size * row.dtype.itemsize
    return pl.pallas_call(
        functools.partial(_back_kernel, n, m),
        out_shape=shapes,
        in_specs=[pl.BlockSpec(memory_space=pl.ANY), pl.BlockSpec(memory_space=pl.ANY)],
        out_specs=tuple(pl.BlockSpec(memory_space=pl.ANY) for _ in range(3)),
        scratch_shapes=[
            pltpu.SemaphoreType.DMA((n,)),
            pltpu.SemaphoreType.DMA((n,)),
            pltpu.SemaphoreType.DMA(()),
            pltpu.SemaphoreType.DMA((n,)),
            pltpu.SemaphoreType.DMA((n,)),
            pltpu.SemaphoreType.DMA(()),
            pltpu.SemaphoreType.DMA((m,)),
            pltpu.SemaphoreType.DMA((m,)),
            pltpu.SemaphoreType.DMA(()),
            pltpu.SemaphoreType.DMA((m,)),
            pltpu.SemaphoreType.DMA((m,)),
            pltpu.SemaphoreType.DMA(()),
            pltpu.VMEM(parts.shape, parts.dtype),
            pltpu.VMEM(row.shape, row.dtype),
        ],
        compiler_params=pltpu.CompilerParams(collective_id=ident, has_side_effects=True),
        cost_estimate=pl.CostEstimate(flops=0, transcendentals=0, bytes_accessed=moved),
    )(pieces, parts)


def exchange(x, axis, broadcast, ident):
    n = lax.axis_size(axis)
    other = "col" if axis == "row" else "row"
    shape = (n,) + (x.shape if broadcast else x.shape[1:])
    return pl.pallas_call(
        functools.partial(_exchange_kernel, axis, other, n, broadcast),
        out_shape=jax.ShapeDtypeStruct(shape, x.dtype),
        in_specs=[pl.BlockSpec(memory_space=pl.ANY)],
        out_specs=pl.BlockSpec(memory_space=pl.ANY),
        scratch_shapes=[
            pltpu.SemaphoreType.DMA((n,)),
            pltpu.SemaphoreType.DMA((n,)),
            pltpu.SemaphoreType.DMA(()),
        ],
        compiler_params=pltpu.CompilerParams(collective_id=ident, has_side_effects=True),
        cost_estimate=pl.CostEstimate(
            flops=0, transcendentals=0, bytes_accessed=2 * n * x.size * x.dtype.itemsize
        ),
    )(x)


def _slot_kernel(backward, slots, src_ids, tgt_ids, count_ref, vals_ref, src_ref, out_ref, acc_ref):
    s = pl.program_id(0)

    @pl.when(s == 0)
    def _():
        acc_ref[...] = jnp.zeros_like(acc_ref)

    @pl.when(s < count_ref[0])
    def _():
        block = vals_ref[0]
        segment = src_ref[0]
        if backward:
            dims = (((0,), (0,)), ((), ()))
        else:
            dims = (((1,), (0,)), ((), ()))
        product = lax.dot_general(block, segment, dims, preferred_element_type=jnp.float32)
        target = tgt_ids[s]
        acc_ref[target] = acc_ref[target] + product

    @pl.when(s == slots - 1)
    def _():
        out_ref[...] = acc_ref[...].astype(out_ref.dtype)


def slot_product(tile_values, tile_rows, tile_cols, live_count, source, out_len, backward):
    slots, block_size = tile_values.shape[0], tile_values.shape[1]
    width = source.shape[1]
    n_src = source.shape[0] // block_size
    n_out = out_len // block_size
    panels = source.reshape(n_src, block_size, width)
    if backward:
        src_ids, tgt_ids = tile_rows, tile_cols
    else:
        src_ids, tgt_ids = tile_cols, tile_rows
    src_ids = jnp.clip(src_ids, 0, n_src - 1).astype(jnp.int32)
    tgt_ids = jnp.clip(tgt_ids, 0, n_out - 1).astype(jnp.int32)
    count = jnp.reshape(live_count, (1,)).astype(jnp.int32)
    grid_spec = pltpu.PrefetchScalarGridSpec(
        num_scalar_prefetch=3,
        grid=(slots,),
        in_specs=[
            pl.BlockSpec((1, block_size, block_size), lambda s, src, tgt, cnt: (s, 0, 0)),
            pl.BlockSpec((1, block_size, width), lambda s, src, tgt, cnt: (src[s], 0, 0)),
        ],
        out_specs=pl.BlockSpec((n_out, block_size, width), lambda s, src, tgt, cnt: (0, 0, 0)),
        scratch_shapes=[pltpu.VMEM((n_out, block_size, width), jnp.float32)],
    )
    out = pl.pallas_call(
        functools.partial(_slot_kernel, backward, slots),
        out_shape=jax.ShapeDtypeStruct((n_out, block_size, width), jnp.bfloat16),
        grid_spec=grid_spec,
        compiler_params=pltpu.CompilerParams(
            dimension_semantics=("arbitrary",), vmem_limit_bytes=48 * 1024 * 1024
        ),
        cost_estimate=pl.CostEstimate(
            flops=2 * slots * block_size * block_size * width,
            transcendentals=0,
            bytes_accessed=2 * (slots * block_size * (block_size + width) + n_out * block_size * width),
        ),
    )(src_ids, tgt_ids, count, tile_values, panels)
    return out.reshape(out_len, width)


def gather_rows(x, axis):
    count = lax.axis_size(axis)
    stacked = jnp.broadcast_to(x[None], (count,) + x.shape)
    received = lax.all_to_all(stacked, axis, split_axis=0, concat_axis=0, tiled=True)
    return received.reshape((count * x.shape[0],) + x.shape[1:])


def scatter_sum(x, axis):
    count = lax.axis_size(axis)
    pieces = x.reshape((count, x.shape[0] // count) + x.shape[1:])
    received = lax.all_to_all(pieces, axis, split_axis=0, concat_axis=0, tiled=True)
    return jnp.sum(received.astype(jnp.float32), axis=0)


def pack_grads(local_weight, local_bias):
    pad = jnp.zeros((local_weight.shape[0], 127), jnp.float32)
    return jnp.concatenate([local_weight, local_bias[:, None], pad], axis=1)


def unpack_grads(by_col_then_row, width):
    cols, rows = by_col_then_row.shape[0], by_col_then_row.shape[1]
    whole = by_col_then_row.transpose(1, 0, 2).reshape(cols * rows, -1)
    return whole[:, :width], whole[:, width]


def transposed_product(left, weight):
    return lax.dot_general(
        left, weight, (((1,), (1,)), ((), ())), preferred_element_type=jnp.float32
    ).astype(jnp.bfloat16)


def source_total(received):
    return jnp.sum(received.astype(jnp.float32), axis=0).astype(jnp.bfloat16)


def per_device(
    features, block_values, block_rows, block_cols, block_count, weight, bias, cotangent
):
    tile_values = block_values[0, 0]
    tile_rows = block_rows[0, 0]
    tile_cols = block_cols[0, 0]
    live_count = block_count[0, 0]
    own_nodes = features.shape[0]
    width = features.shape[1]
    row_len = lax.axis_size("col") * own_nodes
    gathered = exchange(features, "row", True, 4).reshape(-1, width)
    col_len = gathered.shape[0]
    partial_value = slot_product(
        tile_values, tile_rows, tile_cols, live_count, gathered, row_len, False
    )
    pieces = partial_value.reshape(lax.axis_size("col"), own_nodes, width)
    received = exchange_steps(pieces, "col", 0, 1, 2)
    aggregate = jnp.sum(received.astype(jnp.float32), axis=0).astype(jnp.bfloat16)
    preact = jnp.dot(aggregate, weight, preferred_element_type=jnp.float32) + bias
    hidden = jax.nn.silu(preact).astype(jnp.bfloat16)
    sigma = jax.nn.sigmoid(preact)
    grad_pre = cotangent.astype(jnp.float32) * sigma * (1.0 + preact * (1.0 - sigma))
    grad_low = grad_pre.astype(jnp.bfloat16)
    local_weight = lax.dot_general(
        aggregate, grad_low, (((0,), (0,)), ((), ())), preferred_element_type=jnp.float32
    )
    local_bias = jnp.sum(grad_pre, axis=0)
    grad_agg = transposed_product(grad_low, weight)
    packed = pack_grads(local_weight, local_bias)
    rows_count = lax.axis_size("row")
    row_pieces = packed.reshape((rows_count, packed.shape[0] // rows_count) + packed.shape[1:])
    grad_stack, by_row_pieces = gather_and_exchange(grad_agg, row_pieces, "col", 0)
    grad_panel = grad_stack.reshape(-1, width)
    by_row = jnp.sum(by_row_pieces, axis=0)
    back = slot_product(tile_values, tile_rows, tile_cols, live_count, grad_panel, col_len, True)
    back_low = back.astype(jnp.bfloat16).reshape(col_len // own_nodes, own_nodes, width)
    parts = by_row.reshape((by_row.shape[0], 1) + by_row.shape[1:])
    received, _, gathered_rows = back_exchange(back_low, parts, 1)
    every = gathered_rows.reshape(gathered_rows.shape[0], gathered_rows.shape[1], -1)
    feature_grad = jnp.sum(received.astype(jnp.float32), axis=0).astype(jnp.bfloat16)
    weight_grad, bias_grad = unpack_grads(every, width)
    return (hidden, weight_grad, bias_grad, feature_grad)


def solution(mesh):
    in_specs = (
        P(("col", "row"), None),
        P("row", "col", None, None, None),
        P("row", "col", None),
        P("row", "col", None),
        P("row", "col"),
        P(),
        P(),
        P(("row", "col"), None),
    )
    out_specs = (P(("row", "col"), None), P(), P(), P(("col", "row"), None))
    return jax.shard_map(
        per_device, mesh=mesh, in_specs=in_specs, out_specs=out_specs, check_vma=False
    )
```
